32 devices in a mesh: gen: 4 (over y, x), fit: 8 (over z, core).
Axes of the slice: x: 2, y: 2, z: 4, core: 2. Of those that a mesh axis runs over, the one named last changes fastest.
Arguments:
- raw_columns: bfloat16 [8, 2000, 2000], P(None, 'gen', 'fit'), as said below
- pivot_pairs: int32 [8], replicated, may hold values from 0 to 3999999, as said below
- collocation: bfloat16 [2000, 4096], P('gen', 'fit'), may hold values from -0.125 to 0.125
- metric_factor: float32 [4096, 4096], P('fit', 'gen'), as said below
Outputs:
- panel: float32 [8, 4096], P('gen', 'fit')
The draws below stay inside these ranges and needn't reach their ends.
Inputs may be any that keep to these rules, and one draw needn't show every extreme that they name: `pivot_pairs`: 8 distinct orbital-pair indices p * 2000 + q. The entries at the pivots, raw_columns[P, pivot_pairs[Q] // 2000, pivot_pairs[Q] % 2000], form a symmetric positive definite matrix. `metric_factor`: lower triangular with a positive diagonal.
All inputs are finite; a program needn't handle non-finite values.
Results may differ from the reference program's by a relative error of at most 0.0029.
Values may be sent and summed in bfloat16 or wider, within the bound.
No kernel may reach another device: no remote copies, remote signals or barrier semaphores. Data moves between devices by JAX's collectives and lax.ppermute only.
A program may use at most 64 MiB of HBM per device.

```python
import math
import jax
import jax.numpy as jnp
from jax import lax

NORB = 2000
NPT_DEV = 512
NVEC = 8
NPTS = 4096


def pivot_choice(key):
    stride = NORB * NORB // NVEC
    position = jnp.arange(NVEC, dtype=jnp.int32)
    offsets = jax.random.randint(jax.random.fold_in(key, 11), (NVEC,), 0, stride, dtype=jnp.int32)
    offsets = jnp.where(position == 0, 0, offsets)
    offsets = jnp.where(position == NVEC - 1, stride - 1, offsets)
    chosen = position * stride + offsets
    shuffle = jax.random.permutation(jax.random.fold_in(key, 12), NVEC)
    return chosen[shuffle].astype(jnp.int32)


def draw_pivot_pairs(key, part):
    return pivot_choice(key)


def draw_raw_columns(key, part):
    pivot_list = pivot_choice(key)
    value_key = jax.random.fold_in(key, 21)
    values = jax.random.normal(value_key, (NVEC, NORB, NORB), jnp.float32)
    values = values * math.sqrt(NVEC)
    coupling = jax.random.uniform(jax.random.fold_in(key, 23), (NVEC, NVEC), jnp.float32, -1.0, 1.0)
    coupling = 0.5 * (coupling + coupling.T)
    heights = NVEC * jax.random.uniform(jax.random.fold_in(key, 24), (NVEC,), jnp.float32, 1.0, 2.0)
    identity = jnp.eye(NVEC, dtype=jnp.float32)
    pivot_values = coupling * (1.0 - identity) + identity * heights[None, :]
    values = values.at[:, pivot_list // NORB, pivot_list % NORB].set(pivot_values)
    return values.astype(jnp.bfloat16)


def draw_metric_factor(key, part):
    entry_key = jax.random.fold_in(key, 31)
    entries = jax.random.uniform(entry_key, (NPTS, NPTS), jnp.float32, -5.0, 5.0)
    entries = entries / math.sqrt(NPTS)
    heights = jax.random.uniform(jax.random.fold_in(key, 32), (NPTS,), jnp.float32, 1.5, 3.0)
    row_index = jnp.arange(NPTS)[:, None]
    col_index = jnp.arange(NPTS)[None, :]
    return jnp.where(row_index > col_index, entries, jnp.where(row_index == col_index, heights[:, None], 0.0))


def steps_of(key, shape, split, least, high):
    loudness, own = 1.0, jax.random.fold_in(key, 6)
    for axis_at, shards_of in split:
        steps = jnp.exp(jax.random.uniform(jax.random.fold_in(own, axis_at), (shards_of,), jnp.float32, least / len(split), high / len(split)))
        loudness = loudness * jnp.repeat(steps, shape[axis_at] // shards_of).reshape([-1 if axis == axis_at else 1 for axis in range(len(shape))])
    return loudness


def scatter_about(key, shape, width, reach, pieces=(), held_as=jnp.bfloat16):
    array = jax.random.normal(key, shape, jnp.float32) * width
    if len(pieces) > 0:
        array = steps_of(key, shape, pieces, -0.22, 0.18) * array
    return jnp.clip(array, min=-reach, max=reach).astype(held_as)


def setup_inputs(seed: int = 0) -> dict:
    splits = jax.random.split(jax.random.key(seed), 5)
    return {
        "raw_columns": draw_raw_columns(jax.random.fold_in(splits[4], 71), 0),
        "pivot_pairs": draw_pivot_pairs(jax.random.fold_in(splits[4], 71), 0),
        "collocation": scatter_about(splits[2], (NORB, NPTS), NORB ** -0.5, 0.125, ((0, 4), (1, 8))),
        "metric_factor": draw_metric_factor(jax.random.fold_in(splits[4], 71), 0),
    }


def reference(raw_columns, pivot_pairs, collocation, metric_factor):
    columns = raw_columns.astype(jnp.float32).reshape(NVEC, NORB * NORB)
    pivot_block = jnp.take(columns, pivot_pairs, axis=1)
    factor = jnp.linalg.cholesky(pivot_block)
    vectors = jax.scipy.linalg.solve_triangular(factor, columns, lower=True)
    vectors = lax.optimization_barrier(vectors.astype(jnp.bfloat16))
    vectors = vectors.astype(jnp.float32).reshape(NVEC, NORB, NORB)
    orbitals = collocation.astype(jnp.float32).reshape(NORB, NPTS // NPT_DEV, NPT_DEV).transpose(1, 0, 2)

    def one_block(points):
        mixed_terms = jnp.einsum('apq,pn->aqn', vectors, points)
        return jnp.sum(mixed_terms * points[None], axis=1)
    projected = lax.map(one_block, orbitals).transpose(1, 0, 2).reshape(NVEC, NPTS)
    solved = jax.scipy.linalg.solve_triangular(metric_factor, projected.T, lower=True)
    return solved.T
```

```python
import functools

import jax
import jax.numpy as jnp
from jax import lax
from jax.experimental import pallas as pl
from jax.experimental.pallas import tpu as pltpu
from jax.sharding import PartitionSpec as P

NORB = 2000
F32 = jnp.float32
BF16 = jnp.bfloat16
BOTH = ("gen", "fit")
HIGHEST = lax.Precision.HIGHEST


def mover(gen_count):
    fit_count = 2 * gen_count

    def move(value, target):
        pairs = []
        for g in range(gen_count):
            for j in range(gen_count):
                for c in range(2):
                    to = target(g, j, c)
                    if to is not None:
                        pairs.append(
                            (g * fit_count + 2 * j + c, to[0] * fit_count + 2 * to[1] + to[2])
                        )
        return lax.ppermute(value, BOTH, pairs)

    return move


def split_hi_lo(x):
    hi = lax.reduce_precision(x, 8, 7)
    return hi.astype(BF16), (x - hi).astype(BF16)


def pivot_kernel(raw_ref, rows_ref, cols_ref, out_ref):
    i = pl.program_id(0)
    picked = jnp.dot(rows_ref[...], raw_ref[0], preferred_element_type=F32)
    entries = jnp.sum(picked * cols_ref[...], axis=1, keepdims=True)
    out_ref[pl.ds(i, 1), :] = entries.T


def pivot_entries(raw, row_hits, col_hits):
    vec_total, orb, pair = raw.shape
    return pl.pallas_call(
        pivot_kernel,
        grid=(vec_total,),
        in_specs=[
            pl.BlockSpec((1, orb, pair), lambda i: (i, 0, 0)),
            pl.BlockSpec((vec_total, orb), lambda i: (0, 0)),
            pl.BlockSpec((vec_total, pair), lambda i: (0, 0)),
        ],
        out_specs=pl.BlockSpec((vec_total, vec_total), lambda i: (0, 0)),
        out_shape=jax.ShapeDtypeStruct((vec_total, vec_total), F32),
        name="pivot_entries",
    )(raw, row_hits, col_hits)


def factor_inverse_kernel(block_ref, out_ref):
    a = block_ref[...]
    n = a.shape[0]
    row = lax.broadcasted_iota(jnp.int32, (n, n), 0)
    col = lax.broadcasted_iota(jnp.int32, (n, n), 1)
    w = (row == col).astype(F32)
    for i in range(n):
        pivot = a[i : i + 1, i : i + 1]
        scale = jnp.where(row[:, :1] > i, a[:, i : i + 1] / pivot, 0.0)
        w = w - scale * w[i : i + 1, :]
        a = a - scale * a[i : i + 1, :]
    diag = jnp.sum(jnp.where(row == col, a, 0.0), axis=1, keepdims=True)
    out_ref[...] = w / jnp.sqrt(diag)


def factor_inverse(block):
    return pl.pallas_call(
        factor_inverse_kernel,
        out_shape=jax.ShapeDtypeStruct(block.shape, F32),
        name="factor_inverse",
    )(block)


def project_kernel(where_ref, own_ref, sib_ref, cq_ref, cp_ref, out_ref):
    i = pl.program_id(0)
    core = where_ref[1]
    mixed = jnp.dot(own_ref[0], cq_ref[0, core], preferred_element_type=F32)
    mixed += jnp.dot(sib_ref[0], cq_ref[0, 1 - core], preferred_element_type=F32)
    out_ref[pl.ds(i, 1), :] = jnp.sum(mixed * cp_ref[...].astype(F32), axis=0, keepdims=True)


def project(where, own, sib, cq, cp):
    vec_total, orb, pair = own.shape
    points = cp.shape[1]
    return pl.pallas_call(
        project_kernel,
        grid_spec=pltpu.PrefetchScalarGridSpec(
            num_scalar_prefetch=1,
            grid=(vec_total,),
            in_specs=[
                pl.BlockSpec((1, orb, pair), lambda i, s: (i, 0, 0)),
                pl.BlockSpec((1, orb, pair), lambda i, s: (i, 0, 0)),
                pl.BlockSpec((1, 2, pair, points), lambda i, s: (s[0], 0, 0, 0)),
                pl.BlockSpec((orb, points), lambda i, s: (0, 0)),
            ],
            out_specs=pl.BlockSpec((vec_total, points), lambda i, s: (0, 0)),
        ),
        out_shape=jax.ShapeDtypeStruct((vec_total, points), F32),
        compiler_params=pltpu.CompilerParams(vmem_limit_bytes=32 << 20),
        name="project",
    )(where, own, sib, cq, cp)


def invert_kernel(where_ref, block_ref, out_ref):
    n = block_ref.shape[0]
    tile = 128
    count = n // tile
    holds = where_ref[1] == 1
    row = lax.broadcasted_iota(jnp.int32, (tile, tile), 0)
    col = lax.broadcasted_iota(jnp.int32, (tile, tile), 1)
    eye = (row == col).astype(F32)
    dot = functools.partial(jnp.dot, precision=HIGHEST, preferred_element_type=F32)
    parts, xs = [], []
    for b in range(count):
        part = block_ref[b * tile : (b + 1) * tile, b * tile : (b + 1) * tile]
        part = jnp.where(holds, part, eye)
        diag = jnp.sum(part * eye, axis=1, keepdims=True)
        parts.append(part)
        xs.append(eye / diag)
    size = 1
    while size < tile:
        pick = (row // (2 * size) == col // (2 * size)) & (row // size != col // size) & (row > col)
        for b in range(count):
            off = jnp.where(pick, parts[b], 0.0)
            xs[b] = xs[b] - dot(xs[b], dot(off, xs[b]))
        size *= 2
    out_ref[...] = jnp.zeros_like(out_ref)
    for b in range(count):
        out_ref[b * tile : (b + 1) * tile, b * tile : (b + 1) * tile] = xs[b]
    size = tile
    while size < n:
        for b in range(0, n, 2 * size):
            mid, end = b + size, b + 2 * size
            lower = jnp.where(holds, block_ref[mid:end, b:mid], 0.0)
            inner = dot(lower, out_ref[b:mid, b:mid])
            out_ref[mid:end, b:mid] = -dot(out_ref[mid:end, mid:end], inner)
        size *= 2


def invert_block(where, metric):
    n = metric.shape[0]
    return pl.pallas_call(
        invert_kernel,
        grid_spec=pltpu.PrefetchScalarGridSpec(
            num_scalar_prefetch=1,
            grid=(1,),
            in_specs=[pl.BlockSpec((n, n), lambda i, s: (0, s[0]))],
            out_specs=pl.BlockSpec((n, n), lambda i, s: (0, 0)),
        ),
        out_shape=jax.ShapeDtypeStruct((n, n), F32),
        compiler_params=pltpu.CompilerParams(vmem_limit_bytes=32 << 20),
        name="invert_block",
    )(where, metric)


def apply_kernel(sign, where_ref, hi_ref, lo_ref, xa_ref, xb_ref, bias_ref, out_ref):
    core = where_ref[0]
    total = jnp.zeros(out_ref.shape, F32)
    n = out_ref.shape[0]
    dims = (((1,), (1,)), ((), ()))
    for x_ref, half in ((xa_ref, core), (xb_ref, 1 - core)):
        hi = x_ref[...].astype(BF16)
        lo = (x_ref[...] - hi.astype(F32)).astype(BF16)
        hi_w = hi_ref[half]
        total += lax.dot_general(hi, hi_w, dims, preferred_element_type=F32)
        total += lax.dot_general(lo, hi_w, dims, preferred_element_type=F32)
        total += lax.dot_general(hi, lo_ref[half], dims, preferred_element_type=F32)
    if sign < 0:
        total = -total
    out_ref[...] = bias_ref[...] + total


def apply_weights(where, weights, xa, xb, bias, sign):
    hi, lo = weights
    return pl.pallas_call(
        functools.partial(apply_kernel, sign),
        in_specs=[pl.BlockSpec(memory_space=pltpu.SMEM)] + [pl.BlockSpec(memory_space=pltpu.VMEM)] * 5,
        out_specs=pl.BlockSpec(memory_space=pltpu.VMEM),
        out_shape=jax.ShapeDtypeStruct(xa.shape, F32),
        compiler_params=pltpu.CompilerParams(vmem_limit_bytes=32 << 20),
        name="apply_weights",
    )(where, hi, lo, xa, xb, bias)


def on_device(raw_columns, pivot_pairs, collocation, metric_factor):
    vec_total, orb_block, pair_block = raw_columns.shape
    gen_count = lax.axis_size("gen")
    gen_index = lax.axis_index("gen")
    fit_index = lax.axis_index("fit")
    chip = fit_index // 2
    core = fit_index % 2
    points = metric_factor.shape[0]
    vec_dev = vec_total // gen_count
    move = mover(gen_count)
    others = range(1, gen_count)
    diagonal = gen_index == chip
    swap = lambda g, j, c: (g, j, 1 - c)

    first_side = [collocation] + [
        move(collocation, lambda g, j, c, k=k: (g, j ^ k, c)) for k in others
    ]
    part = points // gen_count
    halves = collocation.reshape(2, orb_block // 2, points)
    pieces = []
    for m in range(gen_count):
        start = lax.rem(m - chip + gen_count, gen_count) * part
        piece = lax.dynamic_slice_in_dim(halves, start, part, 2)
        pieces.append(move(piece, lambda g, j, c, m=m: ((m - j) % gen_count, g, c)))
    pieces = jnp.stack(pieces + pieces)
    pieces = lax.dynamic_slice_in_dim(pieces, gen_index, gen_count, 0)
    second_side = lax.all_gather(pieces, "gen", axis=3, tiled=True)
    sibling = move(raw_columns, swap)

    pair_first = pivot_pairs // NORB
    pair_second = pivot_pairs % NORB
    row_hits = (
        pair_first[:, None] == gen_index * orb_block + jnp.arange(orb_block)[None, :]
    ).astype(BF16)
    col_hits = (
        pair_second[:, None] == fit_index * pair_block + jnp.arange(pair_block)[None, :]
    ).astype(F32)
    entries = pivot_entries(raw_columns, row_hits, col_hits)
    entries = entries + move(entries, swap)
    entries = sum([move(entries, lambda g, j, c, k=k: (g, j ^ k, c)) for k in others], entries)
    entries = sum([move(entries, lambda g, j, c, k=k: (g ^ k, j, c)) for k in others], entries)
    inverse_factor = factor_inverse(entries)

    own_inverse = invert_block(jnp.stack([core, diagonal.astype(jnp.int32)]), metric_factor)
    upper = move(own_inverse, swap)
    corner = jnp.dot(metric_factor[:, :points], upper, precision=HIGHEST)
    corner = -jnp.dot(own_inverse, corner, precision=HIGHEST)
    zeros = jnp.zeros_like(own_inverse)
    inverse_rows = jnp.stack(
        [jnp.where(core == 0, own_inverse, corner), jnp.where(core == 0, zeros, own_inverse)]
    )
    left = move(metric_factor, lambda g, j, c: (g + 1, j, c) if j == g + 1 else None)
    left_sib = move(left, swap)
    top = jnp.where(core == 0, left, left_sib)
    bottom = jnp.where(core == 0, left_sib, left)
    step_rows = jnp.dot(inverse_rows[0], top, precision=HIGHEST) + jnp.dot(
        inverse_rows[1], bottom, precision=HIGHEST
    )
    step_rows = jnp.stack([step_rows[:, :points], step_rows[:, points:]])
    own_rows = jnp.stack([metric_factor[:, :points], metric_factor[:, points:]])
    inverse_rows = split_hi_lo(inverse_rows)
    step_rows = split_hi_lo(step_rows)
    own_rows = split_hi_lo(own_rows)

    total = None
    for k in range(gen_count):
        where = jnp.stack([chip ^ k, core])
        share = project(where, raw_columns, sibling, second_side, first_side[k])
        if k:
            share = move(share, lambda g, j, c, k=k: (g, j ^ k, c))
        total = share if total is None else total + share
    total = sum([move(total, lambda g, j, c, k=k: (g ^ k, j, c)) for k in others], total)
    rest = jnp.dot(inverse_factor, total, precision=HIGHEST)

    at_core = core[None]
    nothing = jnp.zeros_like(rest)
    solved = apply_weights(at_core, inverse_rows, rest, move(rest, swap), nothing, 1)
    kept = solved
    for t in range(gen_count - 1):
        near = move(kept, lambda g, j, c: (t + 1, t + 1, c) if g == j == t else None)
        near_sib = move(kept, lambda g, j, c: (t + 1, t + 1, 1 - c) if g == j == t else None)
        if t + 2 < gen_count:
            far, far_sib = nothing, nothing
            for z in range(t + 2, gen_count):
                far += move(kept, lambda g, j, c: (t, z, c) if g == j == t else None)
                far_sib += move(kept, lambda g, j, c: (t, z, 1 - c) if g == j == t else None)
            brought = apply_weights(at_core, own_rows, far, far_sib, nothing, 1)
            brought = move(brought, lambda g, j, c: (j, j, c) if g == t and j >= t + 2 else None)
        if t > 0:
            base = apply_weights(at_core, inverse_rows, rest, move(rest, swap), nothing, 1)
        else:
            base = solved
        stepped = apply_weights(at_core, step_rows, near, near_sib, base, -1)
        kept = jnp.where(jnp.logical_and(diagonal, gen_index == t + 1), stepped, kept)
        if t + 2 < gen_count:
            rest = rest - brought

    def rows_of(index):
        return lax.dynamic_slice_in_dim(kept, index * vec_dev, vec_dev, 0)

    result = jnp.where(diagonal, rows_of(gen_index), 0.0)
    for k in others:
        result += move(
            rows_of(gen_index ^ k), lambda g, j, c, k=k: (g ^ k, j, c) if g == j else None
        )
    return result


def solution(mesh):
    in_specs = (P(None, "gen", "fit"), P(), P("gen", "fit"), P("fit", "gen"))
    out_specs = P("gen", "fit")
    return jax.shard_map(
        on_device, mesh=mesh, in_specs=in_specs, out_specs=out_specs, check_vma=False
    )
```

```python
import functools

import jax
import jax.numpy as jnp
from jax import lax
from jax.experimental import pallas as pl
from jax.experimental.pallas import tpu as pltpu
from jax.sharding import PartitionSpec as P

NORB = 2000
F32 = jnp.float32
BF16 = jnp.bfloat16
BOTH = ("gen", "fit")
HIGHEST = lax.Precision.HIGHEST


def mover(gen_count):
    fit_count = 2 * gen_count

    def move(value, target):
        pairs = []
        for g in range(gen_count):
            for j in range(gen_count):
                for c in range(2):
                    to = target(g, j, c)
                    if to is not None:
                        pairs.append(
                            (g * fit_count + 2 * j + c, to[0] * fit_count + 2 * to[1] + to[2])
                        )
        return lax.ppermute(value, BOTH, pairs)

    return move


def split_hi_lo(x):
    hi = lax.reduce_precision(x, 8, 7)
    return hi.astype(BF16), (x - hi).astype(BF16)


def pivot_kernel(row_ref, own_ref, sib_ref, own_col_ref, sib_col_ref, out_ref, buffer, sems):
    count, orb = out_ref.shape[1], own_ref.shape[0]
    copies = []
    for i in range(count):
        row = jnp.clip(row_ref[i], 0, orb - 1)
        for n, ref in enumerate((own_ref, sib_ref)):
            copies.append(
                pltpu.make_async_copy(ref.at[row], buffer.at[2 * i + n], sems.at[2 * i + n])
            )
            copies[-1].start()
    lane = lax.broadcasted_iota(jnp.int32, buffer.shape[1:], 1)
    for i in range(count):
        copies[2 * i].wait()
        copies[2 * i + 1].wait()
        local = jnp.logical_and(row_ref[i] >= 0, row_ref[i] < orb)
        kept = jnp.where(lane == own_col_ref[i], buffer[2 * i].astype(F32), 0.0)
        kept += jnp.where(lane == sib_col_ref[i], buffer[2 * i + 1].astype(F32), 0.0)
        kept = jnp.where(local, kept, 0.0)
        out_ref[:, i : i + 1] = jnp.sum(kept, axis=1, keepdims=True)


def pivot_entries(own, sib, rows, own_cols, sib_cols):
    vec_total, pair = own.shape[1:]
    return pl.pallas_call(
        pivot_kernel,
        in_specs=[
            pl.BlockSpec(memory_space=pltpu.SMEM),
            pl.BlockSpec(memory_space=pl.ANY),
            pl.BlockSpec(memory_space=pl.ANY),
            pl.BlockSpec(memory_space=pltpu.SMEM),
            pl.BlockSpec(memory_space=pltpu.SMEM),
        ],
        out_specs=pl.BlockSpec(memory_space=pltpu.VMEM),
        out_shape=jax.ShapeDtypeStruct((vec_total, vec_total), F32),
        scratch_shapes=[
            pltpu.VMEM((2 * vec_total, vec_total, pair), BF16),
            pltpu.SemaphoreType.DMA((2 * vec_total,)),
        ],
        name="pivot_entries",
    )(rows, own, sib, own_cols, sib_cols)


def factor_inverse_kernel(block_ref, out_ref):
    a = block_ref[...]
    n = a.shape[0]
    row = lax.broadcasted_iota(jnp.int32, (n, n), 0)
    col = lax.broadcasted_iota(jnp.int32, (n, n), 1)
    w = (row == col).astype(F32)
    for i in range(n):
        pivot = a[i : i + 1, i : i + 1]
        scale = jnp.where(row[:, :1] > i, a[:, i : i + 1] / pivot, 0.0)
        w = w - scale * w[i : i + 1, :]
        a = a - scale * a[i : i + 1, :]
    diag = jnp.sum(jnp.where(row == col, a, 0.0), axis=1, keepdims=True)
    out_ref[...] = w / jnp.sqrt(diag)


def factor_inverse(block):
    return pl.pallas_call(
        factor_inverse_kernel,
        out_shape=jax.ShapeDtypeStruct(block.shape, F32),
        name="factor_inverse",
    )(block)


def project_kernel(vec_total, chunk, group, where_ref, own_ref, sib_ref, cp_ref, *rest):
    part_refs, (out_ref, cq, cp) = rest[:-3], rest[-3:]
    part = part_refs[0].shape[-1]
    step = pl.program_id(0)
    core = where_ref[0]

    @pl.when(step == 0)
    def _():
        for n, ref in enumerate(part_refs):
            start = 0
            if len(part_refs) > 1:
                start = pl.multiple_of(where_ref[1 + n] * part, part)
            cq[:, :, pl.ds(start, part)] = ref[...]
        cp[...] = cp_ref[...].astype(F32)
        out_ref[...] = jnp.zeros_like(out_ref)

    rows = group * vec_total

    def one_group(i, total):
        start = pl.multiple_of(i * rows, 8)
        mixed = jnp.dot(own_ref[pl.ds(start, rows), :], cq[core], preferred_element_type=F32)
        mixed += jnp.dot(sib_ref[pl.ds(start, rows), :], cq[1 - core], preferred_element_type=F32)
        for p in range(group):
            at = step * chunk + i * group + p
            total += mixed[p * vec_total : (p + 1) * vec_total] * cp[pl.ds(at, 1), :]
        return total

    out_ref[...] = lax.fori_loop(0, chunk // group, one_group, out_ref[...])


def project(where, own, sib, cp, parts):
    orb, points = cp.shape
    pair = own.shape[1]
    vec_total = own.shape[0] // orb
    chunk, group = 125, 25
    part_shape = parts[0].shape
    return pl.pallas_call(
        functools.partial(project_kernel, vec_total, chunk, group),
        grid_spec=pltpu.PrefetchScalarGridSpec(
            num_scalar_prefetch=1,
            grid=(orb // chunk,),
            in_specs=[
                pl.BlockSpec((chunk * vec_total, pair), lambda i, s: (i, 0)),
                pl.BlockSpec((chunk * vec_total, pair), lambda i, s: (i, 0)),
                pl.BlockSpec((orb, points), lambda i, s: (0, 0)),
            ]
            + [pl.BlockSpec(part_shape, lambda i, s: (0, 0, 0))] * len(parts),
            out_specs=pl.BlockSpec((vec_total, points), lambda i, s: (0, 0)),
            scratch_shapes=[
                pltpu.VMEM((2, pair, points), BF16),
                pltpu.VMEM((orb, points), F32),
            ],
        ),
        out_shape=jax.ShapeDtypeStruct((vec_total, points), F32),
        compiler_params=pltpu.CompilerParams(vmem_limit_bytes=32 << 20),
        name="project",
    )(where, own, sib, cp, *parts)


def invert_kernel(where_ref, block_ref, out_ref):
    n = block_ref.shape[0]
    tile = 128
    count = n // tile
    holds = where_ref[1] == 1
    row = lax.broadcasted_iota(jnp.int32, (tile, tile), 0)
    col = lax.broadcasted_iota(jnp.int32, (tile, tile), 1)
    eye = (row == col).astype(F32)
    dot = functools.partial(jnp.dot, precision=HIGHEST, preferred_element_type=F32)
    parts, xs = [], []
    for b in range(count):
        part = block_ref[b * tile : (b + 1) * tile, b * tile : (b + 1) * tile]
        part = jnp.where(holds, part, eye)
        diag = jnp.sum(part * eye, axis=1, keepdims=True)
        parts.append(part)
        xs.append(eye / diag)
    size = 1
    while size < tile:
        pick = (row // (2 * size) == col // (2 * size)) & (row // size != col // size) & (row > col)
        for b in range(count):
            off = jnp.where(pick, parts[b], 0.0)
            xs[b] = xs[b] - dot(xs[b], dot(off, xs[b]))
        size *= 2
    out_ref[...] = jnp.zeros_like(out_ref)
    for b in range(count):
        out_ref[b * tile : (b + 1) * tile, b * tile : (b + 1) * tile] = xs[b]
    size = tile
    while size < n:
        for b in range(0, n, 2 * size):
            mid, end = b + size, b + 2 * size
            lower = jnp.where(holds, block_ref[mid:end, b:mid], 0.0)
            inner = dot(lower, out_ref[b:mid, b:mid])
            out_ref[mid:end, b:mid] = -dot(out_ref[mid:end, mid:end], inner)
        size *= 2


def invert_block(where, metric):
    n = metric.shape[0]
    return pl.pallas_call(
        invert_kernel,
        grid_spec=pltpu.PrefetchScalarGridSpec(
            num_scalar_prefetch=1,
            grid=(1,),
            in_specs=[pl.BlockSpec((n, n), lambda i, s: (0, s[0]))],
            out_specs=pl.BlockSpec((n, n), lambda i, s: (0, 0)),
        ),
        out_shape=jax.ShapeDtypeStruct((n, n), F32),
        compiler_params=pltpu.CompilerParams(vmem_limit_bytes=32 << 20),
        name="invert_block",
    )(where, metric)


def apply_kernel(sign, where_ref, hi_ref, lo_ref, xa_ref, xb_ref, bias_ref, out_ref):
    core = where_ref[0]
    total = jnp.zeros(out_ref.shape, F32)
    n = out_ref.shape[0]
    dims = (((1,), (1,)), ((), ()))
    for x_ref, half in ((xa_ref, core), (xb_ref, 1 - core)):
        hi = x_ref[...].astype(BF16)
        lo = (x_ref[...] - hi.astype(F32)).astype(BF16)
        hi_w = hi_ref[half]
        total += lax.dot_general(hi, hi_w, dims, preferred_element_type=F32)
        total += lax.dot_general(lo, hi_w, dims, preferred_element_type=F32)
        total += lax.dot_general(hi, lo_ref[half], dims, preferred_element_type=F32)
    if sign < 0:
        total = -total
    out_ref[...] = bias_ref[...] + total


def apply_weights(where, weights, xa, xb, bias, sign):
    hi, lo = weights
    return pl.pallas_call(
        functools.partial(apply_kernel, sign),
        in_specs=[pl.BlockSpec(memory_space=pltpu.SMEM)] + [pl.BlockSpec(memory_space=pltpu.VMEM)] * 5,
        out_specs=pl.BlockSpec(memory_space=pltpu.VMEM),
        out_shape=jax.ShapeDtypeStruct(xa.shape, F32),
        compiler_params=pltpu.CompilerParams(vmem_limit_bytes=32 << 20),
        name="apply_weights",
    )(where, hi, lo, xa, xb, bias)


def on_device(raw_columns, pivot_pairs, collocation, metric_factor):
    vec_total, orb_block, pair_block = raw_columns.shape
    gen_count = lax.axis_size("gen")
    gen_index = lax.axis_index("gen")
    fit_index = lax.axis_index("fit")
    chip = fit_index // 2
    core = fit_index % 2
    points = metric_factor.shape[0]
    vec_dev = vec_total // gen_count
    move = mover(gen_count)
    others = range(1, gen_count)
    diagonal = gen_index == chip
    swap = lambda g, j, c: (g, j, 1 - c)

    from_left, from_right = [collocation], [collocation]
    for _ in others:
        from_left.append(move(from_left[-1], lambda g, j, c: (g, j + 1, c) if j + 1 < gen_count else None))
        from_right.append(move(from_right[-1], lambda g, j, c: (g, j - 1, c) if j > 0 else None))

    def first_side(k):
        block = None
        for j in range(gen_count):
            away = j - (j ^ k)
            held = from_left[away] if away > 0 else from_right[-away]
            block = held if block is None else jnp.where(chip == j, held, block)
        return block

    part = points // gen_count
    halves = collocation.reshape(2, orb_block // 2, points)
    spread = []
    for k in range(gen_count):
        piece = lax.dynamic_slice_in_dim(halves, (gen_index ^ k) * part, part, 2)
        spread.append(move(piece, lambda g, j, c, k=k: (g ^ k, j, c)) if k else piece)
    spread = jnp.stack(spread)
    own_parts = []
    for k in range(gen_count):
        piece = lax.dynamic_index_in_dim(spread, gen_index ^ chip ^ k, 0, keepdims=False)
        own_parts.append(move(piece, lambda g, j, c, k=k: (g, j ^ k, c)) if k else piece)
    near_parts, far_parts = [own_parts[0]], [jnp.stack(own_parts[1:])]
    for k in others:
        near_parts.append(move(near_parts[0], lambda g, j, c, k=k: (g ^ k, j, c)))
        far_parts.append(move(far_parts[0], lambda g, j, c, k=k: (g ^ k, j, c)))

    def second_side(k):
        parts = near_parts if k == 0 else [x[k - 1] for x in far_parts]
        if part % 128 == 0:
            return parts
        whole = jnp.zeros(halves.shape, BF16)
        for n, x in enumerate(parts):
            whole = lax.dynamic_update_slice_in_dim(whole, x, (gen_index ^ n) * part, 2)
        return [whole]

    sibling = move(raw_columns, swap)
    own_raw = raw_columns.transpose(1, 0, 2)
    sib_raw = sibling.transpose(1, 0, 2)
    pivot_rows = pivot_pairs // NORB - gen_index * orb_block
    own_cols = pivot_pairs % NORB - fit_index * pair_block
    sib_cols = pivot_pairs % NORB - (fit_index ^ 1) * pair_block
    entries = pivot_entries(own_raw, sib_raw, pivot_rows, own_cols, sib_cols)
    entries = sum([move(entries, lambda g, j, c, k=k: (g, j ^ k, c)) for k in others], entries)
    entries = sum([move(entries, lambda g, j, c, k=k: (g ^ k, j, c)) for k in others], entries)
    inverse_factor = factor_inverse(entries)

    own_inverse = invert_block(jnp.stack([core, diagonal.astype(jnp.int32)]), metric_factor)
    upper = move(own_inverse, swap)
    corner = jnp.dot(metric_factor[:, :points], upper, precision=HIGHEST)
    corner = -jnp.dot(own_inverse, corner, precision=HIGHEST)
    zeros = jnp.zeros_like(own_inverse)
    inverse_rows = jnp.stack(
        [jnp.where(core == 0, own_inverse, corner), jnp.where(core == 0, zeros, own_inverse)]
    )
    left = move(metric_factor, lambda g, j, c: (g + 1, j, c) if j == g + 1 else None)
    left_sib = move(left, swap)
    top = jnp.where(core == 0, left, left_sib)
    bottom = jnp.where(core == 0, left_sib, left)
    step_rows = jnp.dot(inverse_rows[0], top, precision=HIGHEST) + jnp.dot(
        inverse_rows[1], bottom, precision=HIGHEST
    )
    step_rows = jnp.stack([step_rows[:, :points], step_rows[:, points:]])
    own_rows = jnp.stack([metric_factor[:, :points], metric_factor[:, points:]])
    inverse_rows = split_hi_lo(inverse_rows)
    step_rows = split_hi_lo(step_rows)
    own_rows = split_hi_lo(own_rows)

    own_raw = own_raw.reshape(orb_block * vec_total, pair_block)
    sib_raw = sib_raw.reshape(orb_block * vec_total, pair_block)
    where = jnp.stack([core] + [gen_index ^ k for k in range(gen_count)])
    total = None
    for k in range(gen_count):
        block = first_side(k)
        if k == gen_count - 1:
            block, step_rows, inverse_rows, own_rows = lax.optimization_barrier(
                (block, step_rows, inverse_rows, own_rows)
            )
        share = project(where, own_raw, sib_raw, block, second_side(k))
        if k:
            share = move(share, lambda g, j, c, k=k: (g, j ^ k, c))
        total = share if total is None else total + share
    total = sum([move(total, lambda g, j, c, k=k: (g ^ k, j, c)) for k in others], total)
    rest = jnp.dot(inverse_factor, total, precision=HIGHEST)

    at_core = core[None]
    nothing = jnp.zeros_like(rest)
    solved = apply_weights(at_core, inverse_rows, rest, move(rest, swap), nothing, 1)
    kept = solved
    for t in range(gen_count - 1):
        near = move(kept, lambda g, j, c: (t + 1, t + 1, c) if g == j == t else None)
        near_sib = move(kept, lambda g, j, c: (t + 1, t + 1, 1 - c) if g == j == t else None)
        if t + 2 < gen_count:
            far, far_sib = nothing, nothing
            for z in range(t + 2, gen_count):
                far += move(kept, lambda g, j, c: (t, z, c) if g == j == t else None)
                far_sib += move(kept, lambda g, j, c: (t, z, 1 - c) if g == j == t else None)
            brought = apply_weights(at_core, own_rows, far, far_sib, nothing, 1)
            brought = move(brought, lambda g, j, c: (j, j, c) if g == t and j >= t + 2 else None)
        if t > 0:
            base = apply_weights(at_core, inverse_rows, rest, move(rest, swap), nothing, 1)
        else:
            base = solved
        stepped = apply_weights(at_core, step_rows, near, near_sib, base, -1)
        kept = jnp.where(jnp.logical_and(diagonal, gen_index == t + 1), stepped, kept)
        if t + 2 < gen_count:
            rest = rest - brought

    def rows_of(index):
        return lax.dynamic_slice_in_dim(kept, index * vec_dev, vec_dev, 0)

    result = jnp.where(diagonal, rows_of(gen_index), 0.0)
    for k in others:
        result += move(
            rows_of(gen_index ^ k), lambda g, j, c, k=k: (g ^ k, j, c) if g == j else None
        )
    return result


def solution(mesh):
    in_specs = (P(None, "gen", "fit"), P(), P("gen", "fit"), P("fit", "gen"))
    out_specs = P("gen", "fit")
    return jax.shard_map(
        on_device, mesh=mesh, in_specs=in_specs, out_specs=out_specs, check_vma=False
    )
```

```python
import functools

import jax
import jax.numpy as jnp
from jax import lax
from jax.experimental import pallas as pl
from jax.experimental.pallas import tpu as pltpu
from jax.sharding import PartitionSpec as P

NORB = 2000
F32 = jnp.float32
BF16 = jnp.bfloat16
BOTH = ("gen", "fit")
HIGHEST = lax.Precision.HIGHEST


def mover(gen_count):
    fit_count = 2 * gen_count

    def move(value, target):
        pairs = []
        for g in range(gen_count):
            for j in range(gen_count):
                for c in range(2):
                    to = target(g, j, c)
                    if to is not None:
                        pairs.append(
                            (g * fit_count + 2 * j + c, to[0] * fit_count + 2 * to[1] + to[2])
                        )
        return lax.ppermute(value, BOTH, pairs)

    return move


def split_hi_lo(x):
    hi = lax.reduce_precision(x, 8, 7)
    return hi.astype(BF16), (x - hi).astype(BF16)


def pivot_kernel(row_ref, own_ref, sib_ref, own_col_ref, sib_col_ref, out_ref, buffer, sems):
    count, orb = out_ref.shape[1], own_ref.shape[0]
    copies = []
    for i in range(count):
        row = jnp.clip(row_ref[i], 0, orb - 1)
        for n, ref in enumerate((own_ref, sib_ref)):
            copies.append(
                pltpu.make_async_copy(ref.at[row], buffer.at[2 * i + n], sems.at[2 * i + n])
            )
            copies[-1].start()
    lane = lax.broadcasted_iota(jnp.int32, buffer.shape[1:], 1)
    for i in range(count):
        copies[2 * i].wait()
        copies[2 * i + 1].wait()
        local = jnp.logical_and(row_ref[i] >= 0, row_ref[i] < orb)
        kept = jnp.where(lane == own_col_ref[i], buffer[2 * i].astype(F32), 0.0)
        kept += jnp.where(lane == sib_col_ref[i], buffer[2 * i + 1].astype(F32), 0.0)
        kept = jnp.where(local, kept, 0.0)
        out_ref[:, i : i + 1] = jnp.sum(kept, axis=1, keepdims=True)


def pivot_entries(own, sib, rows, own_cols, sib_cols):
    vec_total, pair = own.shape[1:]
    return pl.pallas_call(
        pivot_kernel,
        in_specs=[
            pl.BlockSpec(memory_space=pltpu.SMEM),
            pl.BlockSpec(memory_space=pl.ANY),
            pl.BlockSpec(memory_space=pl.ANY),
            pl.BlockSpec(memory_space=pltpu.SMEM),
            pl.BlockSpec(memory_space=pltpu.SMEM),
        ],
        out_specs=pl.BlockSpec(memory_space=pltpu.VMEM),
        out_shape=jax.ShapeDtypeStruct((vec_total, vec_total), F32),
        scratch_shapes=[
            pltpu.VMEM((2 * vec_total, vec_total, pair), BF16),
            pltpu.SemaphoreType.DMA((2 * vec_total,)),
        ],
        name="pivot_entries",
    )(rows, own, sib, own_cols, sib_cols)


def factor_inverse_kernel(block_ref, out_ref):
    a = block_ref[...]
    n = a.shape[0]
    row = lax.broadcasted_iota(jnp.int32, (n, n), 0)
    col = lax.broadcasted_iota(jnp.int32, (n, n), 1)
    w = (row == col).astype(F32)
    for i in range(n):
        pivot = a[i : i + 1, i : i + 1]
        scale = jnp.where(row[:, :1] > i, a[:, i : i + 1] / pivot, 0.0)
        w = w - scale * w[i : i + 1, :]
        a = a - scale * a[i : i + 1, :]
    diag = jnp.sum(jnp.where(row == col, a, 0.0), axis=1, keepdims=True)
    out_ref[...] = w / jnp.sqrt(diag)


def factor_inverse(block):
    return pl.pallas_call(
        factor_inverse_kernel,
        out_shape=jax.ShapeDtypeStruct(block.shape, F32),
        name="factor_inverse",
    )(block)


def project_kernel(vec_total, chunk, where_ref, own_ref, sib_ref, cp_ref, entries_ref, *rest):
    part_refs, (out_ref, cq, cp, acc) = rest[:-4], rest[-4:]
    part = part_refs[0].shape[-1]
    points = cp.shape[1]
    step = pl.program_id(0)
    core = where_ref[0]

    @pl.when(step == 0)
    def _():
        for n, ref in enumerate(part_refs):
            start = 0
            if len(part_refs) > 1:
                start = pl.multiple_of(where_ref[1 + n] * part, part)
            cq[:, :, pl.ds(start, part)] = ref[0]
        cp[...] = cp_ref[...].astype(F32)
        acc[...] = jnp.zeros_like(acc)
        out_ref[:, points:] = jnp.zeros((vec_total, out_ref.shape[1] - points), F32)
        out_ref[:, points : points + vec_total] = entries_ref[...]

    mixed = jnp.dot(own_ref[...], cq[core], preferred_element_type=F32)
    mixed += jnp.dot(sib_ref[...], cq[1 - core], preferred_element_type=F32)
    total = acc[...]
    for p in range(chunk):
        total += mixed[p * vec_total : (p + 1) * vec_total] * cp[pl.ds(step * chunk + p, 1), :]
    acc[...] = total

    @pl.when(step == pl.num_programs(0) - 1)
    def _():
        out_ref[:, :points] = acc[...]


def project(where, own, sib, cp, entries, parts, slot):
    orb, points = cp.shape
    pair = own.shape[1]
    vec_total = own.shape[0] // orb
    chunk = 125
    part_shape = (1,) + parts[0].shape[1:]
    return pl.pallas_call(
        functools.partial(project_kernel, vec_total, chunk),
        grid_spec=pltpu.PrefetchScalarGridSpec(
            num_scalar_prefetch=1,
            grid=(orb // chunk,),
            in_specs=[
                pl.BlockSpec((chunk * vec_total, pair), lambda i, s: (i, 0)),
                pl.BlockSpec((chunk * vec_total, pair), lambda i, s: (i, 0)),
                pl.BlockSpec((orb, points), lambda i, s: (0, 0)),
                pl.BlockSpec((vec_total, vec_total), lambda i, s: (0, 0)),
            ]
            + [pl.BlockSpec(part_shape, lambda i, s: (slot, 0, 0, 0))] * len(parts),
            out_specs=pl.BlockSpec((vec_total, points + 128), lambda i, s: (0, 0)),
            scratch_shapes=[
                pltpu.VMEM((2, pair, points), BF16),
                pltpu.VMEM((orb, points), F32),
                pltpu.VMEM((vec_total, points), F32),
            ],
        ),
        out_shape=jax.ShapeDtypeStruct((vec_total, points + 128), F32),
        compiler_params=pltpu.CompilerParams(vmem_limit_bytes=20 << 20),
        cost_estimate=pl.CostEstimate(
            flops=4 * orb * vec_total * pair * points, transcendentals=0, bytes_accessed=1 << 20
        ),
        name="project",
    )(where, own, sib, cp, entries, *parts)


def invert_kernel(own_ref, sib_ref, own_out, sib_out):
    n = own_ref.shape[0]
    tile = 128
    row = lax.broadcasted_iota(jnp.int32, (tile, tile), 0)
    col = lax.broadcasted_iota(jnp.int32, (tile, tile), 1)
    eye = (row == col).astype(F32)
    dot = functools.partial(jnp.dot, precision=HIGHEST, preferred_element_type=F32)
    pairs = ((own_ref, own_out), (sib_ref, sib_out))
    places = [(ref, out, b) for ref, out in pairs for b in range(0, n, tile)]
    parts = [ref[b : b + tile, b : b + tile] for ref, _, b in places]
    xs = [eye / jnp.sum(part * eye, axis=1, keepdims=True) for part in parts]
    size = 1
    while size < tile:
        pick = (row // (2 * size) == col // (2 * size)) & (row // size > col // size)
        inner = [dot(jnp.where(pick, part, 0.0), x) for part, x in zip(parts, xs)]
        xs = [x - dot(x, y) for x, y in zip(xs, inner)]
        size *= 2
    own_out[...] = jnp.zeros_like(own_out)
    sib_out[...] = jnp.zeros_like(sib_out)
    for (_, out, b), x in zip(places, xs):
        out[b : b + tile, b : b + tile] = x
    size = tile
    while size < n:
        for ref, out in pairs:
            for b in range(0, n, 2 * size):
                mid, end = b + size, b + 2 * size
                inner = dot(ref[mid:end, b:mid], out[b:mid, b:mid])
                out[mid:end, b:mid] = -dot(out[mid:end, mid:end], inner)
        size *= 2


def invert_blocks(own, sib):
    shape = jax.ShapeDtypeStruct(own.shape, F32)
    return pl.pallas_call(
        invert_kernel,
        out_shape=(shape, shape),
        compiler_params=pltpu.CompilerParams(vmem_limit_bytes=16 << 20),
        cost_estimate=pl.CostEstimate(flops=8 << 30, transcendentals=0, bytes_accessed=1 << 22),
        name="invert_blocks",
    )(own, sib)


def weigh(hi_ref, lo_ref, halves):
    dims = (((1,), (1,)), ((), ()))
    total = None
    for half, x in halves:
        hi = x.astype(BF16)
        lo = (x - hi.astype(F32)).astype(BF16)
        n = x.shape[0]
        both = lax.dot_general(
            jnp.concatenate([hi, lo]), hi_ref[half], dims, preferred_element_type=F32
        )
        part = both[:n] + both[n:]
        part += lax.dot_general(hi, lo_ref[half], dims, preferred_element_type=F32)
        total = part if total is None else total + part
    return total


def apply_kernel(where_ref, hi_ref, lo_ref, xa_ref, xb_ref, out_ref):
    core = where_ref[0]
    out_ref[...] = weigh(hi_ref, lo_ref, [(core, xa_ref[...]), (1 - core, xb_ref[...])])


def apply_weights(where, weights, xa, xb):
    return pl.pallas_call(
        apply_kernel,
        in_specs=[pl.BlockSpec(memory_space=pltpu.SMEM)] + [pl.BlockSpec(memory_space=pltpu.VMEM)] * 4,
        out_specs=pl.BlockSpec(memory_space=pltpu.VMEM),
        out_shape=jax.ShapeDtypeStruct(xa.shape, F32),
        compiler_params=pltpu.CompilerParams(vmem_limit_bytes=12 << 20),
        cost_estimate=pl.CostEstimate(flops=1 << 30, transcendentals=0, bytes_accessed=1 << 21),
        name="apply_weights",
    )(where, *weights, xa, xb)


def turn_kernel(where_ref, *refs):
    own_hi, own_lo, sib_hi, sib_lo, inv_hi, inv_lo, xa, xb, own_rest, sib_rest, out_ref = refs
    core = where_ref[0]
    halves = [(core, xa[...]), (1 - core, xb[...])]
    own = own_rest[...] - weigh(own_hi, own_lo, halves)
    sib = sib_rest[...] - weigh(sib_hi, sib_lo, halves)
    out_ref[...] = weigh(inv_hi, inv_lo, [(core, own), (1 - core, sib)])


def turn(where, left_own, left_sib, inverse, xa, xb, own_rest, sib_rest):
    return pl.pallas_call(
        turn_kernel,
        in_specs=[pl.BlockSpec(memory_space=pltpu.SMEM)] + [pl.BlockSpec(memory_space=pltpu.VMEM)] * 10,
        out_specs=pl.BlockSpec(memory_space=pltpu.VMEM),
        out_shape=jax.ShapeDtypeStruct(xa.shape, F32),
        compiler_params=pltpu.CompilerParams(vmem_limit_bytes=20 << 20),
        cost_estimate=pl.CostEstimate(flops=2 << 30, transcendentals=0, bytes_accessed=1 << 22),
        name="turn",
    )(where, *left_own, *left_sib, *inverse, xa, xb, own_rest, sib_rest)


def combine_kernel(inverse_ref, x_ref, out_ref):
    x = x_ref[...]
    inverse = inverse_ref[...]
    total = inverse[:, :1] * x[:1]
    for i in range(1, x.shape[0]):
        total += inverse[:, i : i + 1] * x[i : i + 1]
    out_ref[...] = total


def combine(inverse, x):
    return pl.pallas_call(
        combine_kernel, out_shape=jax.ShapeDtypeStruct(x.shape, F32), name="combine"
    )(inverse, x)


def on_device(raw_columns, pivot_pairs, collocation, metric_factor):
    vec_total, orb_block, pair_block = raw_columns.shape
    gen_count = lax.axis_size("gen")
    gen_index = lax.axis_index("gen")
    fit_index = lax.axis_index("fit")
    chip = fit_index // 2
    core = fit_index % 2
    points = metric_factor.shape[0]
    vec_dev = vec_total // gen_count
    move = mover(gen_count)
    others = range(1, gen_count)
    diagonal = gen_index == chip
    swap = lambda g, j, c: (g, j, 1 - c)

    part = points // gen_count
    halves = collocation.reshape(2, orb_block // 2, points)
    spread = []
    for k in range(gen_count):
        piece = lax.dynamic_slice_in_dim(halves, (gen_index ^ k) * part, part, 2)
        spread.append(move(piece, lambda g, j, c, k=k: (g ^ k, j, c)) if k else piece)
    spread = jnp.stack(spread)
    own_block = jnp.where(core == 0, metric_factor[:, :points], metric_factor[:, points:])
    own_block = jnp.where(diagonal, own_block, jnp.eye(points, dtype=F32))
    sibling = move(raw_columns, swap)
    sib_block = move(own_block, swap)
    spread, first, sibling, sib_block = lax.optimization_barrier(
        (spread, collocation, sibling, sib_block)
    )
    first_side = [first] + [move(first, lambda g, j, c, k=k: (g, j ^ k, c)) for k in (1, 2)]
    own_parts = []
    for k in range(gen_count):
        piece = lax.dynamic_index_in_dim(spread, gen_index ^ chip ^ k, 0, keepdims=False)
        own_parts.append(move(piece, lambda g, j, c, k=k: (g, j ^ k, c)) if k else piece)
    own_parts, first, first_side[1] = lax.optimization_barrier((own_parts, first, first_side[1]))
    for k in range(3, gen_count):
        first_side.append(move(first, lambda g, j, c, k=k: (g, j ^ k, c)))
    all_parts = [jnp.stack(own_parts)]
    for k in others:
        all_parts.append(move(all_parts[0], lambda g, j, c, k=k: (g ^ k, j, c)))

    def second_side(k):
        if part % 128 == 0:
            return all_parts
        whole = jnp.zeros(halves.shape, BF16)
        for n, x in enumerate(all_parts):
            whole = lax.dynamic_update_slice_in_dim(whole, x[k], (gen_index ^ n) * part, 2)
        return [whole[None]]

    own_raw = raw_columns.transpose(1, 0, 2)
    sib_raw = sibling.transpose(1, 0, 2)
    pivot_rows = pivot_pairs // NORB - gen_index * orb_block
    own_cols = pivot_pairs % NORB - fit_index * pair_block
    sib_cols = pivot_pairs % NORB - (fit_index ^ 1) * pair_block
    entries = pivot_entries(own_raw, sib_raw, pivot_rows, own_cols, sib_cols)

    own_inverse, upper = invert_blocks(own_block, sib_block)
    corner = jnp.dot(metric_factor[:, :points], upper, precision=HIGHEST)
    corner = -jnp.dot(own_inverse, corner, precision=HIGHEST)
    zeros = jnp.zeros_like(own_inverse)
    inverse_rows = split_hi_lo(
        jnp.stack(
            [jnp.where(core == 0, own_inverse, corner), jnp.where(core == 0, zeros, own_inverse)]
        )
    )

    own_hi, own_lo = split_hi_lo(jnp.stack([metric_factor[:, :points], metric_factor[:, points:]]))
    all_parts, first_side[2], entries, inverse_rows, left_hi, left_lo = lax.optimization_barrier(
        (all_parts, first_side[2], entries, inverse_rows, own_hi, own_lo)
    )
    to_diagonal = lambda g, j, c: (g + 1, j, c) if j == g + 1 else None
    left_own = (move(left_hi, to_diagonal), move(left_lo, to_diagonal))
    left_sib = (move(left_own[0], swap), move(left_own[1], swap))

    own_raw = own_raw.reshape(orb_block * vec_total, pair_block)
    sib_raw = sib_raw.reshape(orb_block * vec_total, pair_block)
    where = jnp.stack([core] + [gen_index ^ k for k in range(gen_count)])
    total = None
    for k in range(gen_count):
        block = first_side[k]
        if k == gen_count - 1:
            block, inverse_rows = lax.optimization_barrier((block, inverse_rows))
        share = project(where, own_raw, sib_raw, block, entries, second_side(k), k if part % 128 == 0 else 0)
        if k:
            share = move(share, lambda g, j, c, k=k: (g, j ^ k, c))
        total = share if total is None else total + share
    total = sum([move(total, lambda g, j, c, k=k: (g ^ k, j, c)) for k in others], total)
    rest = total[:, :points]
    pivot_block = total[:, points : points + vec_total]

    at_core = core[None]
    nothing = jnp.zeros_like(rest)
    sib_rest = move(rest, swap)
    solved = apply_weights(at_core, inverse_rows, rest, sib_rest)
    kept = solved
    for t in range(gen_count - 1):
        near = move(solved, lambda g, j, c: (t + 1, t + 1, c) if g == j == t else None)
        near_sib = move(solved, lambda g, j, c: (t + 1, t + 1, 1 - c) if g == j == t else None)
        if t + 2 < gen_count:
            far, far_sib = nothing, nothing
            for z in range(t + 2, gen_count):
                far += move(solved, lambda g, j, c: (t, z, c) if g == j == t else None)
                far_sib += move(solved, lambda g, j, c: (t, z, 1 - c) if g == j == t else None)
            brought = apply_weights(at_core, (own_hi, own_lo), far, far_sib)
            brought = move(brought, lambda g, j, c: (j, j, c) if g == t and j >= t + 2 else None)
        solved = turn(
            at_core, left_own, left_sib, inverse_rows, near, near_sib, rest, sib_rest
        )
        kept = jnp.where(jnp.logical_and(diagonal, gen_index == t + 1), solved, kept)
        if t + 2 < gen_count:
            rest = rest - brought
            sib_rest = move(rest, swap)
    kept = combine(factor_inverse(pivot_block), kept)

    def rows_of(index):
        return lax.dynamic_slice_in_dim(kept, index * vec_dev, vec_dev, 0)

    result = jnp.where(diagonal, rows_of(gen_index), 0.0)
    for k in others:
        result += move(
            rows_of(gen_index ^ k), lambda g, j, c, k=k: (g ^ k, j, c) if g == j else None
        )
    return result


def solution(mesh):
    in_specs = (P(None, "gen", "fit"), P(), P("gen", "fit"), P("fit", "gen"))
    out_specs = P("gen", "fit")
    return jax.shard_map(
        on_device, mesh=mesh, in_specs=in_specs, out_specs=out_specs, check_vma=False
    )
```

```python
import functools

import jax
import jax.numpy as jnp
from jax import lax
from jax.experimental import pallas as pl
from jax.experimental.pallas import tpu as pltpu
from jax.sharding import PartitionSpec as P

NORB = 2000
F32 = jnp.float32
BF16 = jnp.bfloat16
BOTH = ("gen", "fit")
HIGHEST = lax.Precision.HIGHEST


def mover(gen_count):
    fit_count = 2 * gen_count

    def move(value, target):
        pairs = []
        for g in range(gen_count):
            for j in range(gen_count):
                for c in range(2):
                    to = target(g, j, c)
                    if to is not None:
                        pairs.append(
                            (g * fit_count + 2 * j + c, to[0] * fit_count + 2 * to[1] + to[2])
                        )
        return lax.ppermute(value, BOTH, pairs)

    return move


def split_hi_lo(x):
    hi = lax.reduce_precision(x, 8, 7)
    return hi.astype(BF16), (x - hi).astype(BF16)


def pivot_kernel(row_ref, own_ref, sib_ref, own_col_ref, sib_col_ref, out_ref, buffer, sems):
    count, orb = out_ref.shape[1], own_ref.shape[0]
    copies = []
    for i in range(count):
        row = jnp.clip(row_ref[i], 0, orb - 1)
        for n, ref in enumerate((own_ref, sib_ref)):
            copies.append(
                pltpu.make_async_copy(ref.at[row], buffer.at[2 * i + n], sems.at[2 * i + n])
            )
            copies[-1].start()
    lane = lax.broadcasted_iota(jnp.int32, buffer.shape[1:], 1)
    for i in range(count):
        copies[2 * i].wait()
        copies[2 * i + 1].wait()
        local = jnp.logical_and(row_ref[i] >= 0, row_ref[i] < orb)
        kept = jnp.where(lane == own_col_ref[i], buffer[2 * i].astype(F32), 0.0)
        kept += jnp.where(lane == sib_col_ref[i], buffer[2 * i + 1].astype(F32), 0.0)
        kept = jnp.where(local, kept, 0.0)
        out_ref[:, i : i + 1] = jnp.sum(kept, axis=1, keepdims=True)


def pivot_entries(own, sib, rows, own_cols, sib_cols):
    vec_total, pair = own.shape[1:]
    return pl.pallas_call(
        pivot_kernel,
        in_specs=[
            pl.BlockSpec(memory_space=pltpu.SMEM),
            pl.BlockSpec(memory_space=pl.ANY),
            pl.BlockSpec(memory_space=pl.ANY),
            pl.BlockSpec(memory_space=pltpu.SMEM),
            pl.BlockSpec(memory_space=pltpu.SMEM),
        ],
        out_specs=pl.BlockSpec(memory_space=pltpu.VMEM),
        out_shape=jax.ShapeDtypeStruct((vec_total, vec_total), F32),
        scratch_shapes=[
            pltpu.VMEM((2 * vec_total, vec_total, pair), BF16),
            pltpu.SemaphoreType.DMA((2 * vec_total,)),
        ],
        name="pivot_entries",
    )(rows, own, sib, own_cols, sib_cols)


def factor_inverse_kernel(block_ref, out_ref):
    a = block_ref[...]
    n = a.shape[0]
    row = lax.broadcasted_iota(jnp.int32, (n, n), 0)
    col = lax.broadcasted_iota(jnp.int32, (n, n), 1)
    w = (row == col).astype(F32)
    for i in range(n):
        pivot = a[i : i + 1, i : i + 1]
        scale = jnp.where(row[:, :1] > i, a[:, i : i + 1] / pivot, 0.0)
        w = w - scale * w[i : i + 1, :]
        a = a - scale * a[i : i + 1, :]
    diag = jnp.sum(jnp.where(row == col, a, 0.0), axis=1, keepdims=True)
    out_ref[...] = w / jnp.sqrt(diag)


def factor_inverse(block):
    return pl.pallas_call(
        factor_inverse_kernel,
        out_shape=jax.ShapeDtypeStruct(block.shape, F32),
        name="factor_inverse",
    )(block)


def project_kernel(vec_total, chunk, where_ref, own_ref, sib_ref, cp_ref, entries_ref, *rest):
    part_refs, (out_ref, cq, cp, acc) = rest[:-4], rest[-4:]
    part = part_refs[0].shape[-1]
    points = cp.shape[1]
    step = pl.program_id(0)
    core = where_ref[0]

    @pl.when(step == 0)
    def _():
        for n, ref in enumerate(part_refs):
            start = 0
            if len(part_refs) > 1:
                start = pl.multiple_of(where_ref[1 + n] * part, part)
            cq[:, :, pl.ds(start, part)] = ref[0]
        cp[...] = cp_ref[...].astype(F32)
        acc[...] = jnp.zeros_like(acc)
        out_ref[:, points:] = jnp.zeros((vec_total, out_ref.shape[1] - points), F32)
        out_ref[:, points : points + vec_total] = entries_ref[...]

    mixed = jnp.dot(own_ref[...], cq[core], preferred_element_type=F32)
    mixed += jnp.dot(sib_ref[...], cq[1 - core], preferred_element_type=F32)
    total = acc[...]
    for p in range(chunk):
        total += mixed[p * vec_total : (p + 1) * vec_total] * cp[pl.ds(step * chunk + p, 1), :]
    acc[...] = total

    @pl.when(step == pl.num_programs(0) - 1)
    def _():
        out_ref[:, :points] = acc[...]


def project(where, own, sib, cp, entries, parts, slot):
    orb, points = cp.shape
    pair = own.shape[1]
    vec_total = own.shape[0] // orb
    chunk = 125
    part_shape = (1,) + parts[0].shape[1:]
    return pl.pallas_call(
        functools.partial(project_kernel, vec_total, chunk),
        grid_spec=pltpu.PrefetchScalarGridSpec(
            num_scalar_prefetch=1,
            grid=(orb // chunk,),
            in_specs=[
                pl.BlockSpec((chunk * vec_total, pair), lambda i, s: (i, 0)),
                pl.BlockSpec((chunk * vec_total, pair), lambda i, s: (i, 0)),
                pl.BlockSpec((orb, points), lambda i, s: (0, 0)),
                pl.BlockSpec((vec_total, vec_total), lambda i, s: (0, 0)),
            ]
            + [pl.BlockSpec(part_shape, lambda i, s: (slot, 0, 0, 0))] * len(parts),
            out_specs=pl.BlockSpec((vec_total, points + 128), lambda i, s: (0, 0)),
            scratch_shapes=[
                pltpu.VMEM((2, pair, points), BF16),
                pltpu.VMEM((orb, points), F32),
                pltpu.VMEM((vec_total, points), F32),
            ],
        ),
        out_shape=jax.ShapeDtypeStruct((vec_total, points + 128), F32),
        compiler_params=pltpu.CompilerParams(vmem_limit_bytes=20 << 20),
        cost_estimate=pl.CostEstimate(
            flops=4 * orb * vec_total * pair * points, transcendentals=0, bytes_accessed=1 << 20
        ),
        name="project",
    )(where, own, sib, cp, entries, *parts)


def invert_kernel(own_ref, sib_ref, own_out, sib_out):
    n = own_ref.shape[0]
    tile = 128
    row = lax.broadcasted_iota(jnp.int32, (tile, tile), 0)
    col = lax.broadcasted_iota(jnp.int32, (tile, tile), 1)
    eye = (row == col).astype(F32)
    dot = functools.partial(jnp.dot, precision=HIGHEST, preferred_element_type=F32)
    pairs = ((own_ref, own_out), (sib_ref, sib_out))
    places = [(ref, out, b) for ref, out in pairs for b in range(0, n, tile)]
    parts = [ref[b : b + tile, b : b + tile] for ref, _, b in places]
    xs = [eye / jnp.sum(part * eye, axis=1, keepdims=True) for part in parts]
    size = 1
    while size < tile:
        pick = (row // (2 * size) == col // (2 * size)) & (row // size > col // size)
        inner = [dot(jnp.where(pick, part, 0.0), x) for part, x in zip(parts, xs)]
        xs = [x - dot(x, y) for x, y in zip(xs, inner)]
        size *= 2
    own_out[...] = jnp.zeros_like(own_out)
    sib_out[...] = jnp.zeros_like(sib_out)
    for (_, out, b), x in zip(places, xs):
        out[b : b + tile, b : b + tile] = x
    size = tile
    while size < n:
        for ref, out in pairs:
            for b in range(0, n, 2 * size):
                mid, end = b + size, b + 2 * size
                inner = dot(ref[mid:end, b:mid], out[b:mid, b:mid])
                out[mid:end, b:mid] = -dot(out[mid:end, mid:end], inner)
        size *= 2


def invert_blocks(own, sib):
    shape = jax.ShapeDtypeStruct(own.shape, F32)
    return pl.pallas_call(
        invert_kernel,
        out_shape=(shape, shape),
        compiler_params=pltpu.CompilerParams(vmem_limit_bytes=16 << 20),
        cost_estimate=pl.CostEstimate(flops=8 << 30, transcendentals=0, bytes_accessed=1 << 22),
        name="invert_blocks",
    )(own, sib)


def weigh(hi_ref, lo_ref, halves):
    dims = (((1,), (1,)), ((), ()))
    total = None
    for half, x in halves:
        hi = x.astype(BF16)
        lo = (x - hi.astype(F32)).astype(BF16)
        n = x.shape[0]
        both = lax.dot_general(
            jnp.concatenate([hi, lo]), hi_ref[half], dims, preferred_element_type=F32
        )
        part = both[:n] + both[n:]
        if lo_ref is not None:
            part += lax.dot_general(hi, lo_ref[half], dims, preferred_element_type=F32)
        total = part if total is None else total + part
    return total


def apply_kernel(where_ref, hi_ref, lo_ref, xa_ref, xb_ref, out_ref):
    core = where_ref[0]
    out_ref[...] = weigh(hi_ref, lo_ref, [(core, xa_ref[...]), (1 - core, xb_ref[...])])


def apply_weights(where, weights, xa, xb):
    return pl.pallas_call(
        apply_kernel,
        in_specs=[pl.BlockSpec(memory_space=pltpu.SMEM)] + [pl.BlockSpec(memory_space=pltpu.VMEM)] * 4,
        out_specs=pl.BlockSpec(memory_space=pltpu.VMEM),
        out_shape=jax.ShapeDtypeStruct(xa.shape, F32),
        compiler_params=pltpu.CompilerParams(vmem_limit_bytes=12 << 20),
        cost_estimate=pl.CostEstimate(flops=1 << 30, transcendentals=0, bytes_accessed=1 << 21),
        name="apply_weights",
    )(where, *weights, xa, xb)


def turn_kernel(where_ref, *refs):
    own_left, sib_left, inv_hi, inv_lo, xa, xb, own_rest, sib_rest, out_ref = refs
    core = where_ref[0]
    halves = [(core, xa[...]), (1 - core, xb[...])]
    own = own_rest[...] - weigh(own_left, None, halves)
    sib = sib_rest[...] - weigh(sib_left, None, halves)
    out_ref[...] = weigh(inv_hi, inv_lo, [(core, own), (1 - core, sib)])


def turn(where, left_own, left_sib, inverse, xa, xb, own_rest, sib_rest):
    return pl.pallas_call(
        turn_kernel,
        in_specs=[pl.BlockSpec(memory_space=pltpu.SMEM)] + [pl.BlockSpec(memory_space=pltpu.VMEM)] * 8,
        out_specs=pl.BlockSpec(memory_space=pltpu.VMEM),
        out_shape=jax.ShapeDtypeStruct(xa.shape, F32),
        compiler_params=pltpu.CompilerParams(vmem_limit_bytes=16 << 20),
        cost_estimate=pl.CostEstimate(flops=2 << 30, transcendentals=0, bytes_accessed=1 << 22),
        name="turn",
    )(where, left_own, left_sib, *inverse, xa, xb, own_rest, sib_rest)


def combine_kernel(count, turn_ref, inverse_ref, *refs):
    x_refs, out_refs = refs[:count], refs[count:]
    x = jnp.zeros(x_refs[0].shape, F32)
    for t, ref in enumerate(x_refs):
        x = jnp.where(turn_ref[0] == t, ref[...], x)
    inverse = inverse_ref[...]
    total = inverse[:, :1] * x[:1]
    for i in range(1, x.shape[0]):
        total += inverse[:, i : i + 1] * x[i : i + 1]
    rows = out_refs[0].shape[0]
    for n, ref in enumerate(out_refs):
        ref[...] = total[n * rows : (n + 1) * rows]


def combine(which, inverse, turns, rows):
    count = len(turns)
    share = jax.ShapeDtypeStruct((rows, turns[0].shape[1]), F32)
    return pl.pallas_call(
        functools.partial(combine_kernel, count),
        in_specs=[pl.BlockSpec(memory_space=pltpu.SMEM)]
        + [pl.BlockSpec(memory_space=pltpu.VMEM)] * (count + 1),
        out_shape=[share] * count,
        name="combine",
    )(which, inverse, *turns)


def on_device(raw_columns, pivot_pairs, collocation, metric_factor):
    vec_total, orb_block, pair_block = raw_columns.shape
    gen_count = lax.axis_size("gen")
    gen_index = lax.axis_index("gen")
    fit_index = lax.axis_index("fit")
    chip = fit_index // 2
    core = fit_index % 2
    points = metric_factor.shape[0]
    vec_dev = vec_total // gen_count
    move = mover(gen_count)
    others = range(1, gen_count)
    diagonal = gen_index == chip
    swap = lambda g, j, c: (g, j, 1 - c)

    part = points // gen_count
    halves = collocation.reshape(2, orb_block // 2, points)
    spread = []
    for k in range(gen_count):
        piece = lax.dynamic_slice_in_dim(halves, (gen_index ^ k) * part, part, 2)
        spread.append(move(piece, lambda g, j, c, k=k: (g ^ k, j, c)) if k else piece)
    spread = jnp.stack(spread)
    across = lambda k: lambda g, j, c: (g, j ^ k, c)
    sibling = move(raw_columns, swap)
    spread, sibling, metric_late = lax.optimization_barrier((spread, sibling, metric_factor))
    own_block = jnp.where(core == 0, metric_late[:, :points], metric_late[:, points:])
    own_block = jnp.where(diagonal, own_block, jnp.eye(points, dtype=F32))
    sib_block = move(own_block, swap)
    own_parts = []
    for k in range(gen_count):
        piece = lax.dynamic_index_in_dim(spread, gen_index ^ chip ^ k, 0, keepdims=False)
        own_parts.append(move(piece, across(k)) if k else piece)
    own_parts, first, own_block, sib_block = lax.optimization_barrier(
        (own_parts, collocation, own_block, sib_block)
    )
    first_side = [collocation] + [move(first, across(k)) for k in others]
    all_parts = [jnp.stack(own_parts)]
    for k in others:
        all_parts.append(move(all_parts[0], lambda g, j, c, k=k: (g ^ k, j, c)))

    def second_side(k):
        if part % 128 == 0:
            return all_parts
        whole = jnp.zeros(halves.shape, BF16)
        for n, x in enumerate(all_parts):
            whole = lax.dynamic_update_slice_in_dim(whole, x[k], (gen_index ^ n) * part, 2)
        return [whole[None]]

    own_raw = raw_columns.transpose(1, 0, 2)
    sib_raw = sibling.transpose(1, 0, 2)
    pivot_rows = pivot_pairs // NORB - gen_index * orb_block
    own_cols = pivot_pairs % NORB - fit_index * pair_block
    sib_cols = pivot_pairs % NORB - (fit_index ^ 1) * pair_block
    entries = pivot_entries(own_raw, sib_raw, pivot_rows, own_cols, sib_cols)

    own_inverse, upper = invert_blocks(own_block, sib_block)
    corner = jnp.dot(metric_factor[:, :points], upper, precision=HIGHEST)
    corner = -jnp.dot(own_inverse, corner, precision=HIGHEST)
    zeros = jnp.zeros_like(own_inverse)
    inverse_rows = split_hi_lo(
        jnp.stack(
            [jnp.where(core == 0, own_inverse, corner), jnp.where(core == 0, zeros, own_inverse)]
        )
    )

    own_hi, own_lo = split_hi_lo(jnp.stack([metric_factor[:, :points], metric_factor[:, points:]]))
    all_parts, first_side[2], entries, inverse_rows, left_hi = lax.optimization_barrier(
        (all_parts, first_side[2], entries, inverse_rows, own_hi)
    )
    left_own = move(left_hi, lambda g, j, c: (g + 1, j, c) if j == g + 1 else None)

    own_raw = own_raw.reshape(orb_block * vec_total, pair_block)
    sib_raw = sib_raw.reshape(orb_block * vec_total, pair_block)
    where = jnp.stack([core] + [gen_index ^ k for k in range(gen_count)])
    total = None
    for k in range(gen_count):
        block = first_side[k]
        share = project(where, own_raw, sib_raw, block, entries, second_side(k), k if part % 128 == 0 else 0)
        if k:
            share = move(share, lambda g, j, c, k=k: (g, j ^ k, c))
        total = share if total is None else total + share
    total, left_own = lax.optimization_barrier((total, left_own))
    left_sib = move(left_own, swap)
    total = sum([move(total, lambda g, j, c, k=k: (g ^ k, j, c)) for k in others], total)
    rest = total[:, :points]
    pivot_block = total[:, points : points + vec_total]

    at_core = core[None]
    sib_rest = move(rest, swap)
    solved = apply_weights(at_core, inverse_rows, rest, sib_rest)
    turns = [solved]
    waiting = None
    for t in range(gen_count):
        if t + 1 < gen_count:
            near = move(solved, lambda g, j, c: (t + 1, t + 1, c) if g == j == t else None)
            near_sib = move(solved, lambda g, j, c: (t + 1, t + 1, 1 - c) if g == j == t else None)
            near, near_sib, late = lax.optimization_barrier((near, near_sib, solved))
        if waiting is not None:
            if t + 1 < gen_count:
                waiting, near, near_sib = lax.optimization_barrier((waiting, near, near_sib))
            brought = apply_weights(at_core, (own_hi, own_lo), *waiting)
            brought = move(
                brought, lambda g, j, c: (j, j, c) if g == t - 1 and j >= t + 1 else None
            )
        far = None
        if t + 2 < gen_count:
            far = far_sib = None
            for z in range(t + 2, gen_count):
                one = move(late, lambda g, j, c: (t, z, c) if g == j == t else None)
                two = move(late, lambda g, j, c: (t, z, 1 - c) if g == j == t else None)
                far = one if far is None else far + one
                far_sib = two if far_sib is None else far_sib + two
        if waiting is not None:
            rest = rest - brought
            sib_rest = move(rest, swap)
        waiting = None if far is None else (far, far_sib)
        if t + 1 < gen_count:
            solved = turn(at_core, left_own, left_sib, inverse_rows, near, near_sib, rest, sib_rest)
            turns.append(solved)

    inverse_factor = factor_inverse(pivot_block).reshape(gen_count, vec_dev, vec_total)
    order = jnp.stack([gen_index ^ k for k in range(gen_count)])
    inverse_factor = inverse_factor[order].reshape(vec_total, vec_total)
    shares = combine(jnp.where(diagonal, gen_index, -1)[None], inverse_factor, turns, vec_dev)
    result = shares[0]
    for k in others:
        result += move(shares[k], lambda g, j, c, k=k: (g ^ k, j, c) if g == j else None)
    return result


def solution(mesh):
    in_specs = (P(None, "gen", "fit"), P(), P("gen", "fit"), P("fit", "gen"))
    out_specs = P("gen", "fit")
    return jax.shard_map(
        on_device, mesh=mesh, in_specs=in_specs, out_specs=out_specs, check_vma=False
    )
```

```python
import functools

import jax
import jax.numpy as jnp
from jax import lax
from jax.experimental import pallas as pl
from jax.experimental.pallas import tpu as pltpu
from jax.sharding import PartitionSpec as P

NORB = 2000
F32 = jnp.float32
BF16 = jnp.bfloat16
BOTH = ("gen", "fit")
HIGHEST = lax.Precision.HIGHEST


def mover(gen_count):
    fit_count = 2 * gen_count

    def move(value, target):
        pairs = []
        for g in range(gen_count):
            for j in range(gen_count):
                for c in range(2):
                    to = target(g, j, c)
                    if to is not None:
                        pairs.append(
                            (g * fit_count + 2 * j + c, to[0] * fit_count + 2 * to[1] + to[2])
                        )
        return lax.ppermute(value, BOTH, pairs)

    return move


def split_hi_lo(x):
    hi = lax.reduce_precision(x, 8, 7)
    return hi.astype(BF16), (x - hi).astype(BF16)


def pivot_kernel(row_ref, own_ref, sib_ref, own_col_ref, sib_col_ref, out_ref, buffer, sems):
    count, orb = out_ref.shape[1], own_ref.shape[0]
    copies = []
    for i in range(count):
        row = jnp.clip(row_ref[i], 0, orb - 1)
        for n, ref in enumerate((own_ref, sib_ref)):
            copies.append(
                pltpu.make_async_copy(ref.at[row], buffer.at[2 * i + n], sems.at[2 * i + n])
            )
            copies[-1].start()
    lane = lax.broadcasted_iota(jnp.int32, buffer.shape[1:], 1)
    for i in range(count):
        copies[2 * i].wait()
        copies[2 * i + 1].wait()
        local = jnp.logical_and(row_ref[i] >= 0, row_ref[i] < orb)
        kept = jnp.where(lane == own_col_ref[i], buffer[2 * i].astype(F32), 0.0)
        kept += jnp.where(lane == sib_col_ref[i], buffer[2 * i + 1].astype(F32), 0.0)
        kept = jnp.where(local, kept, 0.0)
        out_ref[:, i : i + 1] = jnp.sum(kept, axis=1, keepdims=True)


def pivot_entries(own, sib, rows, own_cols, sib_cols):
    vec_total, pair = own.shape[1:]
    return pl.pallas_call(
        pivot_kernel,
        in_specs=[
            pl.BlockSpec(memory_space=pltpu.SMEM),
            pl.BlockSpec(memory_space=pl.ANY),
            pl.BlockSpec(memory_space=pl.ANY),
            pl.BlockSpec(memory_space=pltpu.SMEM),
            pl.BlockSpec(memory_space=pltpu.SMEM),
        ],
        out_specs=pl.BlockSpec(memory_space=pltpu.VMEM),
        out_shape=jax.ShapeDtypeStruct((vec_total, vec_total), F32),
        scratch_shapes=[
            pltpu.VMEM((2 * vec_total, vec_total, pair), BF16),
            pltpu.SemaphoreType.DMA((2 * vec_total,)),
        ],
        name="pivot_entries",
    )(rows, own, sib, own_cols, sib_cols)


def factor_inverse_kernel(block_ref, out_ref):
    a = block_ref[...]
    n = a.shape[0]
    row = lax.broadcasted_iota(jnp.int32, (n, n), 0)
    col = lax.broadcasted_iota(jnp.int32, (n, n), 1)
    w = (row == col).astype(F32)
    for i in range(n):
        pivot = a[i : i + 1, i : i + 1]
        scale = jnp.where(row[:, :1] > i, a[:, i : i + 1] / pivot, 0.0)
        w = w - scale * w[i : i + 1, :]
        a = a - scale * a[i : i + 1, :]
    diag = jnp.sum(jnp.where(row == col, a, 0.0), axis=1, keepdims=True)
    out_ref[...] = w / jnp.sqrt(diag)


def factor_inverse(block):
    return pl.pallas_call(
        factor_inverse_kernel,
        out_shape=jax.ShapeDtypeStruct(block.shape, F32),
        name="factor_inverse",
    )(block)


def project_kernel(vec_total, chunk, cp_counts, cq_count, where_ref, own_ref, sib_ref, entries_ref, *rest):
    blocks = len(cp_counts)
    cp_refs, rest = rest[: sum(cp_counts)], rest[sum(cp_counts) :]
    cq_refs, rest = rest[: blocks * cq_count], rest[blocks * cq_count :]
    out_refs, (cq, cp, acc) = rest[:blocks], rest[blocks:]
    points = cp.shape[2]
    step = pl.program_id(0)
    core = where_ref[0]

    @pl.when(step == 0)
    def _():
        for b in range(blocks):
            for n in range(cq_count):
                ref = cq_refs[b * cq_count + n]
                part = ref.shape[-1]
                start = 0
                if cq_count > 1:
                    start = pl.multiple_of(where_ref[1 + n] * part, part)
                cq[b, :, :, pl.ds(start, part)] = ref[0]
            start = 0
            for ref in cp_refs[sum(cp_counts[:b]) : sum(cp_counts[: b + 1])]:
                cp[b, :, start : start + ref.shape[1]] = ref[...].astype(F32)
                start += ref.shape[1]
            out_ref = out_refs[b]
            out_ref[:, points:] = jnp.zeros((vec_total, out_ref.shape[1] - points), F32)
            out_ref[:, points : points + vec_total] = entries_ref[...]
        acc[...] = jnp.zeros_like(acc)

    for b in range(blocks):
        mixed = jnp.dot(own_ref[...], cq[b, core], preferred_element_type=F32)
        mixed += jnp.dot(sib_ref[...], cq[b, 1 - core], preferred_element_type=F32)
        total = acc[b]
        for p in range(chunk):
            row = cp[b, pl.ds(step * chunk + p, 1), :]
            total += mixed[p * vec_total : (p + 1) * vec_total] * row
        acc[b] = total

    @pl.when(step == pl.num_programs(0) - 1)
    def _():
        for b in range(blocks):
            out_refs[b][:, :points] = acc[b]


def project(where, own, sib, entries, first, second, slots):
    orb = first[0][0].shape[0]
    points = sum(x.shape[1] for x in first[0])
    pair = own.shape[1]
    vec_total = own.shape[0] // orb
    chunk = 125
    blocks = len(first)
    whole = lambda i, s: (0, 0)
    specs, arrays = [], []
    for parts in first:
        for x in parts:
            specs.append(pl.BlockSpec(x.shape, whole))
            arrays.append(x)
    for parts, slot in zip(second, slots):
        for x in parts:
            specs.append(
                pl.BlockSpec((1,) + x.shape[1:], lambda i, s, slot=slot: (slot, 0, 0, 0))
            )
            arrays.append(x)
    kernel = functools.partial(
        project_kernel, vec_total, chunk, tuple(len(x) for x in first), len(second[0])
    )
    return pl.pallas_call(
        kernel,
        grid_spec=pltpu.PrefetchScalarGridSpec(
            num_scalar_prefetch=1,
            grid=(orb // chunk,),
            in_specs=[
                pl.BlockSpec((chunk * vec_total, pair), lambda i, s: (i, 0)),
                pl.BlockSpec((chunk * vec_total, pair), lambda i, s: (i, 0)),
                pl.BlockSpec((vec_total, vec_total), whole),
            ]
            + specs,
            out_specs=[pl.BlockSpec((vec_total, points + 128), whole)] * blocks,
            scratch_shapes=[
                pltpu.VMEM((blocks, 2, pair, points), BF16),
                pltpu.VMEM((blocks, orb, points), F32),
                pltpu.VMEM((blocks, vec_total, points), F32),
            ],
        ),
        out_shape=[jax.ShapeDtypeStruct((vec_total, points + 128), F32)] * blocks,
        compiler_params=pltpu.CompilerParams(vmem_limit_bytes=32 << 20),
        cost_estimate=pl.CostEstimate(
            flops=4 * orb * vec_total * pair * points * blocks,
            transcendentals=0,
            bytes_accessed=1 << 20,
        ),
        name="project",
    )(where, own, sib, entries, *arrays)


def invert_kernel(where_ref, own_ref, sib_ref, own_out, sib_out):
    n = own_ref.shape[0]
    tile = 128
    row = lax.broadcasted_iota(jnp.int32, (tile, tile), 0)
    col = lax.broadcasted_iota(jnp.int32, (tile, tile), 1)
    eye = (row == col).astype(F32)
    dot = functools.partial(jnp.dot, precision=HIGHEST, preferred_element_type=F32)
    pairs = ((own_ref, own_out), (sib_ref, sib_out))
    places = [(ref, out, b) for ref, out in pairs for b in range(0, n, tile)]
    holds = where_ref[1] == 1
    parts = [jnp.where(holds, ref[b : b + tile, b : b + tile], eye) for ref, _, b in places]
    xs = [eye / jnp.sum(part * eye, axis=1, keepdims=True) for part in parts]
    size = 1
    while size < tile:
        pick = (row // (2 * size) == col // (2 * size)) & (row // size > col // size)
        inner = [dot(jnp.where(pick, part, 0.0), x) for part, x in zip(parts, xs)]
        xs = [x - dot(x, y) for x, y in zip(xs, inner)]
        size *= 2
    own_out[...] = jnp.zeros_like(own_out)
    sib_out[...] = jnp.zeros_like(sib_out)
    for (_, out, b), x in zip(places, xs):
        out[b : b + tile, b : b + tile] = x
    size = tile
    while size < n:
        for ref, out in pairs:
            for b in range(0, n, 2 * size):
                mid, end = b + size, b + 2 * size
                inner = dot(ref[mid:end, b:mid], out[b:mid, b:mid])
                out[mid:end, b:mid] = -dot(out[mid:end, mid:end], inner)
        size *= 2


def invert_blocks(where, own, sib):
    shape = jax.ShapeDtypeStruct(own.shape, F32)
    vmem = pl.BlockSpec(memory_space=pltpu.VMEM)
    return pl.pallas_call(
        invert_kernel,
        in_specs=[pl.BlockSpec(memory_space=pltpu.SMEM), vmem, vmem],
        out_specs=(vmem, vmem),
        out_shape=(shape, shape),
        compiler_params=pltpu.CompilerParams(vmem_limit_bytes=16 << 20),
        cost_estimate=pl.CostEstimate(flops=8 << 30, transcendentals=0, bytes_accessed=1 << 22),
        name="invert_blocks",
    )(where, own, sib)


def weigh(hi_ref, lo_ref, halves):
    dims = (((1,), (1,)), ((), ()))
    total = None
    for half, x in halves:
        hi = x.astype(BF16)
        lo = (x - hi.astype(F32)).astype(BF16)
        n = x.shape[0]
        width = x.shape[1]
        columns = pl.ds(pl.multiple_of(half * width, width), width)
        both = lax.dot_general(
            jnp.concatenate([hi, lo]), hi_ref[:, columns], dims, preferred_element_type=F32
        )
        part = both[:n] + both[n:]
        if lo_ref is not None:
            part += lax.dot_general(hi, lo_ref[:, columns], dims, preferred_element_type=F32)
        total = part if total is None else total + part
    return total


def apply_kernel(where_ref, hi_ref, lo_ref, xa_ref, xb_ref, out_ref):
    core = where_ref[0]
    out_ref[...] = weigh(hi_ref, lo_ref, [(core, xa_ref[...]), (1 - core, xb_ref[...])])


def apply_weights(where, weights, xa, xb):
    return pl.pallas_call(
        apply_kernel,
        in_specs=[pl.BlockSpec(memory_space=pltpu.SMEM)] + [pl.BlockSpec(memory_space=pltpu.VMEM)] * 4,
        out_specs=pl.BlockSpec(memory_space=pltpu.VMEM),
        out_shape=jax.ShapeDtypeStruct(xa.shape, F32),
        compiler_params=pltpu.CompilerParams(vmem_limit_bytes=12 << 20),
        cost_estimate=pl.CostEstimate(flops=1 << 30, transcendentals=0, bytes_accessed=1 << 21),
        name="apply_weights",
    )(where, *weights, xa, xb)


def turn_kernel(count, where_ref, *refs):
    lefts, refs = refs[: 2 * count], refs[2 * count :]
    inv_hi, inv_lo, xa, xb, own_rest, sib_rest, out_ref, buffer, sems = refs
    core = where_ref[0]
    n = own_rest.shape[0]
    copies = [
        pltpu.make_async_copy(ref, buffer.at[i], sems.at[i]) for i, ref in enumerate(lefts)
    ]
    for copy in copies:
        copy.start()
    own, sib = own_rest[...], sib_rest[...]
    for i in range(count):
        d = count - i
        halves = [(core, xa[i * n : (i + 1) * n]), (1 - core, xb[i * n : (i + 1) * n])]
        copies[2 * d - 2].wait()
        own -= weigh(buffer.at[2 * d - 2], None, halves)
        copies[2 * d - 1].wait()
        sib -= weigh(buffer.at[2 * d - 1], None, halves)
    out_ref[: count * n] = xa[...]
    out_ref[count * n :] = weigh(inv_hi, inv_lo, [(core, own), (1 - core, sib)])


def turn(where, left_own, left_sib, inverse, xa, xb, own_rest, sib_rest):
    n, points = own_rest.shape
    count = xa.shape[0] // n
    lefts = []
    for d in range(1, count + 1):
        lefts += [left_own[d], left_sib[d]]
    return pl.pallas_call(
        functools.partial(turn_kernel, count),
        in_specs=[pl.BlockSpec(memory_space=pltpu.SMEM)]
        + [pl.BlockSpec(memory_space=pl.ANY)] * len(lefts)
        + [pl.BlockSpec(memory_space=pltpu.VMEM)] * 6,
        out_specs=pl.BlockSpec(memory_space=pltpu.VMEM),
        out_shape=jax.ShapeDtypeStruct(((count + 1) * n, points), F32),
        scratch_shapes=[
            pltpu.VMEM((len(lefts),) + lefts[0].shape, BF16),
            pltpu.SemaphoreType.DMA((len(lefts),)),
        ],
        compiler_params=pltpu.CompilerParams(vmem_limit_bytes=32 << 20),
        cost_estimate=pl.CostEstimate(flops=2 << 30, transcendentals=0, bytes_accessed=1 << 22),
        name="turn",
    )(where, *lefts, *inverse, xa, xb, own_rest, sib_rest)


def combine_kernel(count, turn_ref, inverse_ref, *refs):
    x_refs, out_refs = refs[:count], refs[count:]
    x = jnp.zeros(x_refs[0].shape, F32)
    n = x.shape[0]
    for t, ref in enumerate(x_refs):
        x = jnp.where(turn_ref[0] == t, ref[t * n :], x)
    inverse = inverse_ref[...]
    total = inverse[:, :1] * x[:1]
    for i in range(1, x.shape[0]):
        total += inverse[:, i : i + 1] * x[i : i + 1]
    rows = out_refs[0].shape[0]
    for n, ref in enumerate(out_refs):
        ref[...] = total[n * rows : (n + 1) * rows]


def combine(which, inverse, turns, rows):
    count = len(turns)
    share = jax.ShapeDtypeStruct((rows, turns[0].shape[1]), F32)
    return pl.pallas_call(
        functools.partial(combine_kernel, count),
        in_specs=[pl.BlockSpec(memory_space=pltpu.SMEM)]
        + [pl.BlockSpec(memory_space=pltpu.VMEM)] * (count + 1),
        out_shape=[share] * count,
        name="combine",
    )(which, inverse, *turns)


def on_device(raw_columns, pivot_pairs, collocation, metric_factor):
    vec_total, orb_block, pair_block = raw_columns.shape
    gen_count = lax.axis_size("gen")
    gen_index = lax.axis_index("gen")
    fit_index = lax.axis_index("fit")
    chip = fit_index // 2
    core = fit_index % 2
    points = metric_factor.shape[0]
    vec_dev = vec_total // gen_count
    move = mover(gen_count)
    others = range(1, gen_count)
    diagonal = gen_index == chip
    swap = lambda g, j, c: (g, j, 1 - c)

    part = points // gen_count
    across = lambda k: lambda g, j, c: (g, j ^ k, c)
    leftwards = lambda d: lambda g, j, c: (g + d, j, c) if j == g + d else None
    halves = collocation.reshape(2, orb_block // 2, points)
    spread = []
    for k in range(gen_count):
        piece = lax.dynamic_slice_in_dim(halves, (gen_index ^ k) * part, part, 2)
        spread.append(move(piece, lambda g, j, c, k=k: (g ^ k, j, c)) if k else piece)
    spread = jnp.stack(spread)
    early = 2
    half = points // 2
    early_parts = [move(collocation[:, :half], across(early))]
    sibling = move(raw_columns, swap)
    spread, sibling, early_parts, metric_late, first = lax.optimization_barrier(
        (spread, sibling, early_parts, metric_factor, collocation)
    )
    early_parts.append(move(first[:, half:], across(early)))
    own_block = lax.dynamic_slice_in_dim(metric_late, core * points, points, 1)
    sib_block = move(own_block, swap)
    own_rows = metric_late.astype(BF16)
    left_own = {d: move(own_rows, leftwards(d)) for d in (1, 2)}
    spread, early_parts, first, sib_block = lax.optimization_barrier(
        (spread, early_parts, first, sib_block)
    )
    own_parts = []
    for k in range(gen_count):
        piece = lax.dynamic_index_in_dim(spread, gen_index ^ chip ^ k, 0, keepdims=False)
        own_parts.append(move(piece, across(k)) if k else piece)
    own_parts, first, own_block, sib_block, left_own = lax.optimization_barrier(
        (own_parts, first, own_block, sib_block, left_own)
    )
    first_side = {0: [collocation], early: early_parts}
    for k in others:
        if k != early:
            first_side[k] = [move(first, across(k))]
    all_parts = [jnp.stack(own_parts)]
    for k in others:
        all_parts.append(move(all_parts[0], lambda g, j, c, k=k: (g ^ k, j, c)))

    def second_side(k):
        if part % 128 == 0:
            return all_parts
        whole = jnp.zeros(halves.shape, BF16)
        for n, x in enumerate(all_parts):
            whole = lax.dynamic_update_slice_in_dim(whole, x[k], (gen_index ^ n) * part, 2)
        return [whole[None]]

    own_raw = raw_columns.transpose(1, 0, 2)
    sib_raw = sibling.transpose(1, 0, 2)
    pivot_rows = pivot_pairs // NORB - gen_index * orb_block
    own_cols = pivot_pairs % NORB - fit_index * pair_block
    sib_cols = pivot_pairs % NORB - (fit_index ^ 1) * pair_block
    entries = pivot_entries(own_raw, sib_raw, pivot_rows, own_cols, sib_cols)

    own_inverse, upper = invert_blocks(
        jnp.stack([core, diagonal.astype(jnp.int32)]), own_block, sib_block
    )
    corner = jnp.dot(metric_factor[:, :points], upper, precision=HIGHEST)
    corner = -jnp.dot(own_inverse, corner, precision=HIGHEST)
    inverse_rows = split_hi_lo(
        jnp.concatenate(
            [
                jnp.where(core == 0, own_inverse, corner),
                jnp.where(core == 0, jnp.zeros_like(own_inverse), own_inverse),
            ],
            axis=1,
        )
    )

    _, inverse_rows, left_hi, left_own = lax.optimization_barrier(
        (all_parts, inverse_rows, own_rows, left_own)
    )
    for d in range(3, gen_count):
        left_own[d] = move(left_hi, leftwards(d))
    left_sib = {d: move(left_own[d], swap) for d in (1, 2)}

    own_raw = own_raw.reshape(orb_block * vec_total, pair_block)
    sib_raw = sib_raw.reshape(orb_block * vec_total, pair_block)
    where = jnp.stack([core] + [gen_index ^ k for k in range(gen_count)])
    total = None
    late = [k for k in others if k != early]
    for group in [[0, early]] + [late[i : i + 2] for i in range(0, len(late), 2)]:
        shares = project(
            where,
            own_raw,
            sib_raw,
            entries,
            [first_side[k] for k in group],
            [second_side(k) for k in group],
            [k if part % 128 == 0 else 0 for k in group],
        )
        for k, share in zip(group, shares):
            if k:
                share = move(share, across(k))
            total = share if total is None else total + share
    total = sum([move(total, lambda g, j, c, k=k: (g ^ k, j, c)) for k in others], total)
    for d in range(3, gen_count):
        total, left_own[d] = lax.optimization_barrier((total, left_own[d]))
        left_sib[d] = move(left_own[d], swap)
    rest = total[:, :points]
    pivot_block = total[:, points : points + vec_total]

    at_core = core[None]
    sib_rest = move(rest, swap)
    solved = apply_weights(at_core, inverse_rows, rest, sib_rest)
    turns = [solved]
    for t in range(1, gen_count):
        near = move(solved, lambda g, j, c: (t, t, c) if g == j == t - 1 else None)
        near_sib = move(solved, lambda g, j, c: (t, t, 1 - c) if g == j == t - 1 else None)
        solved = turn(at_core, left_own, left_sib, inverse_rows, near, near_sib, rest, sib_rest)
        turns.append(solved)

    inverse_factor = factor_inverse(pivot_block).reshape(gen_count, vec_dev, vec_total)
    order = jnp.stack([gen_index ^ k for k in range(gen_count)])
    inverse_factor = inverse_factor[order].reshape(vec_total, vec_total)
    shares = combine(jnp.where(diagonal, gen_index, -1)[None], inverse_factor, turns, vec_dev)
    result = shares[0]
    for k in others:
        result += move(shares[k], lambda g, j, c, k=k: (g ^ k, j, c) if g == j else None)
    return result


def solution(mesh):
    in_specs = (P(None, "gen", "fit"), P(), P("gen", "fit"), P("fit", "gen"))
    out_specs = P("gen", "fit")
    return jax.shard_map(
        on_device, mesh=mesh, in_specs=in_specs, out_specs=out_specs, check_vma=False
    )
```

```python
import functools

import jax
import jax.numpy as jnp
from jax import lax
from jax.experimental import pallas as pl
from jax.experimental.pallas import tpu as pltpu
from jax.sharding import PartitionSpec as P

NORB = 2000
F32 = jnp.float32
BF16 = jnp.bfloat16
BOTH = ("gen", "fit")
HIGHEST = lax.Precision.HIGHEST


def mover(gen_count):
    fit_count = 2 * gen_count

    def move(value, target):
        pairs = []
        for g in range(gen_count):
            for j in range(gen_count):
                for c in range(2):
                    to = target(g, j, c)
                    if to is not None:
                        pairs.append(
                            (g * fit_count + 2 * j + c, to[0] * fit_count + 2 * to[1] + to[2])
                        )
        return lax.ppermute(value, BOTH, pairs)

    return move


def split_hi_lo(x):
    hi = lax.reduce_precision(x, 8, 7)
    return hi.astype(BF16), (x - hi).astype(BF16)


def pivot_kernel(row_ref, own_ref, sib_ref, own_col_ref, sib_col_ref, out_ref, buffer, sems):
    count, orb = out_ref.shape[1], own_ref.shape[0]
    copies = []
    for i in range(count):
        row = jnp.clip(row_ref[i], 0, orb - 1)
        for n, ref in enumerate((own_ref, sib_ref)):
            copies.append(
                pltpu.make_async_copy(ref.at[row], buffer.at[2 * i + n], sems.at[2 * i + n])
            )
            copies[-1].start()
    lane = lax.broadcasted_iota(jnp.int32, buffer.shape[1:], 1)
    for i in range(count):
        copies[2 * i].wait()
        copies[2 * i + 1].wait()
        local = jnp.logical_and(row_ref[i] >= 0, row_ref[i] < orb)
        kept = jnp.where(lane == own_col_ref[i], buffer[2 * i].astype(F32), 0.0)
        kept += jnp.where(lane == sib_col_ref[i], buffer[2 * i + 1].astype(F32), 0.0)
        kept = jnp.where(local, kept, 0.0)
        out_ref[:, i : i + 1] = jnp.sum(kept, axis=1, keepdims=True)


def pivot_entries(own, sib, rows, own_cols, sib_cols):
    vec_total, pair = own.shape[1:]
    return pl.pallas_call(
        pivot_kernel,
        in_specs=[
            pl.BlockSpec(memory_space=pltpu.SMEM),
            pl.BlockSpec(memory_space=pl.ANY),
            pl.BlockSpec(memory_space=pl.ANY),
            pl.BlockSpec(memory_space=pltpu.SMEM),
            pl.BlockSpec(memory_space=pltpu.SMEM),
        ],
        out_specs=pl.BlockSpec(memory_space=pltpu.VMEM),
        out_shape=jax.ShapeDtypeStruct((vec_total, vec_total), F32),
        scratch_shapes=[
            pltpu.VMEM((2 * vec_total, vec_total, pair), BF16),
            pltpu.SemaphoreType.DMA((2 * vec_total,)),
        ],
        name="pivot_entries",
    )(rows, own, sib, own_cols, sib_cols)


def factor_inverse_kernel(block_ref, out_ref):
    n = block_ref.shape[0]
    a = block_ref[:, block_ref.shape[1] - 128 :][:, :n]
    row = lax.broadcasted_iota(jnp.int32, (n, n), 0)
    col = lax.broadcasted_iota(jnp.int32, (n, n), 1)
    w = (row == col).astype(F32)
    for i in range(n):
        pivot = a[i : i + 1, i : i + 1]
        scale = jnp.where(row[:, :1] > i, a[:, i : i + 1] / pivot, 0.0)
        w = w - scale * w[i : i + 1, :]
        a = a - scale * a[i : i + 1, :]
    diag = jnp.sum(jnp.where(row == col, a, 0.0), axis=1, keepdims=True)
    out_ref[...] = w / jnp.sqrt(diag)


def factor_inverse(block):
    return pl.pallas_call(
        factor_inverse_kernel,
        out_shape=jax.ShapeDtypeStruct((block.shape[0], block.shape[0]), F32),
        name="factor_inverse",
    )(block)


def project_kernel(vec_total, chunk, cp_counts, cq_count, where_ref, own_ref, sib_ref, entries_ref, *rest):
    blocks = len(cp_counts)
    cp_refs, rest = rest[: sum(cp_counts)], rest[sum(cp_counts) :]
    cq_refs, rest = rest[: blocks * cq_count], rest[blocks * cq_count :]
    out_refs, (cq, cp, acc) = rest[:blocks], rest[blocks:]
    points = cp.shape[2]
    step = pl.program_id(0)
    core = where_ref[0]

    @pl.when(step == 0)
    def _():
        for b in range(blocks):
            for n in range(cq_count):
                ref = cq_refs[b * cq_count + n]
                part = ref.shape[-1]
                start = 0
                if cq_count > 1:
                    start = pl.multiple_of(where_ref[1 + n] * part, part)
                cq[b, :, :, pl.ds(start, part)] = ref[0]
            start = 0
            for ref in cp_refs[sum(cp_counts[:b]) : sum(cp_counts[: b + 1])]:
                cp[b, :, start : start + ref.shape[1]] = ref[...].astype(F32)
                start += ref.shape[1]
            out_ref = out_refs[b]
            out_ref[:, points:] = jnp.zeros((vec_total, out_ref.shape[1] - points), F32)
            out_ref[:, points : points + vec_total] = entries_ref[...]
        acc[...] = jnp.zeros_like(acc)

    for b in range(blocks):
        mixed = jnp.dot(own_ref[...], cq[b, core], preferred_element_type=F32)
        mixed += jnp.dot(sib_ref[...], cq[b, 1 - core], preferred_element_type=F32)
        total = acc[b]
        for p in range(chunk):
            row = cp[b, pl.ds(step * chunk + p, 1), :]
            total += mixed[p * vec_total : (p + 1) * vec_total] * row
        acc[b] = total

    @pl.when(step == pl.num_programs(0) - 1)
    def _():
        for b in range(blocks):
            out_refs[b][:, :points] = acc[b]


def project(where, own, sib, entries, first, second, slots):
    orb = first[0][0].shape[0]
    points = sum(x.shape[1] for x in first[0])
    pair = own.shape[1]
    vec_total = own.shape[0] // orb
    chunk = 125
    blocks = len(first)
    whole = lambda i, s: (0, 0)
    specs, arrays = [], []
    for parts in first:
        for x in parts:
            specs.append(pl.BlockSpec(x.shape, whole))
            arrays.append(x)
    for parts, slot in zip(second, slots):
        for x in parts:
            specs.append(
                pl.BlockSpec((1,) + x.shape[1:], lambda i, s, slot=slot: (slot, 0, 0, 0))
            )
            arrays.append(x)
    kernel = functools.partial(
        project_kernel, vec_total, chunk, tuple(len(x) for x in first), len(second[0])
    )
    return pl.pallas_call(
        kernel,
        grid_spec=pltpu.PrefetchScalarGridSpec(
            num_scalar_prefetch=1,
            grid=(orb // chunk,),
            in_specs=[
                pl.BlockSpec((chunk * vec_total, pair), lambda i, s: (i, 0)),
                pl.BlockSpec((chunk * vec_total, pair), lambda i, s: (i, 0)),
                pl.BlockSpec((vec_total, vec_total), whole),
            ]
            + specs,
            out_specs=[pl.BlockSpec((vec_total, points + 128), whole)] * blocks,
            scratch_shapes=[
                pltpu.VMEM((blocks, 2, pair, points), BF16),
                pltpu.VMEM((blocks, orb, points), F32),
                pltpu.VMEM((blocks, vec_total, points), F32),
            ],
        ),
        out_shape=[jax.ShapeDtypeStruct((vec_total, points + 128), F32)] * blocks,
        compiler_params=pltpu.CompilerParams(vmem_limit_bytes=32 << 20),
        cost_estimate=pl.CostEstimate(
            flops=4 * orb * vec_total * pair * points * blocks,
            transcendentals=0,
            bytes_accessed=1 << 20,
        ),
        name="project",
    )(where, own, sib, entries, *arrays)


def invert_kernel(where_ref, own_ref, sib_ref, own_out, sib_out):
    n = own_ref.shape[0]
    tile = 128
    row = lax.broadcasted_iota(jnp.int32, (tile, tile), 0)
    col = lax.broadcasted_iota(jnp.int32, (tile, tile), 1)
    eye = (row == col).astype(F32)
    dot = functools.partial(jnp.dot, precision=HIGHEST, preferred_element_type=F32)
    pairs = ((own_ref, own_out), (sib_ref, sib_out))
    places = [(ref, out, b) for ref, out in pairs for b in range(0, n, tile)]
    holds = where_ref[1] == 1
    parts = [jnp.where(holds, ref[b : b + tile, b : b + tile], eye) for ref, _, b in places]
    xs = [eye / jnp.sum(part * eye, axis=1, keepdims=True) for part in parts]
    size = 1
    while size < tile:
        pick = (row // (2 * size) == col // (2 * size)) & (row // size > col // size)
        inner = [dot(jnp.where(pick, part, 0.0), x) for part, x in zip(parts, xs)]
        xs = [x - dot(x, y) for x, y in zip(xs, inner)]
        size *= 2
    own_out[...] = jnp.zeros_like(own_out)
    sib_out[...] = jnp.zeros_like(sib_out)
    for (_, out, b), x in zip(places, xs):
        out[b : b + tile, b : b + tile] = x
    size = tile
    while size < n:
        for ref, out in pairs:
            for b in range(0, n, 2 * size):
                mid, end = b + size, b + 2 * size
                inner = dot(ref[mid:end, b:mid], out[b:mid, b:mid])
                out[mid:end, b:mid] = -dot(out[mid:end, mid:end], inner)
        size *= 2


def invert_blocks(where, own, sib):
    shape = jax.ShapeDtypeStruct(own.shape, F32)
    vmem = pl.BlockSpec(memory_space=pltpu.VMEM)
    return pl.pallas_call(
        invert_kernel,
        in_specs=[pl.BlockSpec(memory_space=pltpu.SMEM), vmem, vmem],
        out_specs=(vmem, vmem),
        out_shape=(shape, shape),
        compiler_params=pltpu.CompilerParams(vmem_limit_bytes=16 << 20),
        cost_estimate=pl.CostEstimate(flops=8 << 30, transcendentals=0, bytes_accessed=1 << 22),
        name="invert_blocks",
    )(where, own, sib)


def weigh(hi_ref, lo_ref, halves):
    dims = (((1,), (1,)), ((), ()))
    total = None
    for half, x in halves:
        hi = x.astype(BF16)
        lo = (x - hi.astype(F32)).astype(BF16)
        n = x.shape[0]
        width = x.shape[1]
        columns = pl.ds(pl.multiple_of(half * width, width), width)
        both = lax.dot_general(
            jnp.concatenate([hi, lo]), hi_ref[:, columns], dims, preferred_element_type=F32
        )
        part = both[:n] + both[n:]
        if lo_ref is not None:
            part += lax.dot_general(hi, lo_ref[:, columns], dims, preferred_element_type=F32)
        total = part if total is None else total + part
    return total


def apply_kernel(where_ref, hi_ref, lo_ref, xa_ref, xb_ref, out_ref):
    core = where_ref[0]
    points = out_ref.shape[1]
    halves = [(core, xa_ref[:, :points]), (1 - core, xb_ref[:, :points])]
    out_ref[...] = weigh(hi_ref, lo_ref, halves)


def apply_weights(where, weights, xa, xb):
    return pl.pallas_call(
        apply_kernel,
        in_specs=[pl.BlockSpec(memory_space=pltpu.SMEM)] + [pl.BlockSpec(memory_space=pltpu.VMEM)] * 4,
        out_specs=pl.BlockSpec(memory_space=pltpu.VMEM),
        out_shape=jax.ShapeDtypeStruct((xa.shape[0], weights[0].shape[0]), F32),
        compiler_params=pltpu.CompilerParams(vmem_limit_bytes=12 << 20),
        cost_estimate=pl.CostEstimate(flops=1 << 30, transcendentals=0, bytes_accessed=1 << 21),
        name="apply_weights",
    )(where, *weights, xa, xb)


def turn_kernel(count, where_ref, *refs):
    lefts, refs = refs[: 2 * count], refs[2 * count :]
    inv_hi, inv_lo, xa, xb, own_rest, sib_rest, out_ref, buffer, sems = refs
    core = where_ref[0]
    n = own_rest.shape[0]
    copies = [
        pltpu.make_async_copy(ref, buffer.at[i], sems.at[i]) for i, ref in enumerate(lefts)
    ]
    for copy in copies:
        copy.start()
    points = xa.shape[1]
    own, sib = own_rest[:, :points], sib_rest[:, :points]
    for i in range(count):
        d = count - i
        halves = [(core, xa[i * n : (i + 1) * n]), (1 - core, xb[i * n : (i + 1) * n])]
        copies[2 * d - 2].wait()
        own -= weigh(buffer.at[2 * d - 2], None, halves)
        copies[2 * d - 1].wait()
        sib -= weigh(buffer.at[2 * d - 1], None, halves)
    out_ref[: count * n] = xa[...]
    out_ref[count * n :] = weigh(inv_hi, inv_lo, [(core, own), (1 - core, sib)])


def turn(where, lefts, inverse, xa, xb, own_rest, sib_rest):
    n, points = own_rest.shape[0], xa.shape[1]
    count = xa.shape[0] // n
    return pl.pallas_call(
        functools.partial(turn_kernel, count),
        in_specs=[pl.BlockSpec(memory_space=pltpu.SMEM)]
        + [pl.BlockSpec(memory_space=pl.ANY)] * len(lefts)
        + [pl.BlockSpec(memory_space=pltpu.VMEM)] * 6,
        out_specs=pl.BlockSpec(memory_space=pltpu.VMEM),
        out_shape=jax.ShapeDtypeStruct(((count + 1) * n, points), F32),
        scratch_shapes=[
            pltpu.VMEM((len(lefts),) + lefts[0].shape, BF16),
            pltpu.SemaphoreType.DMA((len(lefts),)),
        ],
        compiler_params=pltpu.CompilerParams(vmem_limit_bytes=32 << 20),
        cost_estimate=pl.CostEstimate(flops=2 << 30, transcendentals=0, bytes_accessed=1 << 22),
        name="turn",
    )(where, *lefts, *inverse, xa, xb, own_rest, sib_rest)


def combine_kernel(count, turn_ref, inverse_ref, *refs):
    x_refs, out_refs = refs[:count], refs[count:]
    x = jnp.zeros(x_refs[0].shape, F32)
    n = x.shape[0]
    for t, ref in enumerate(x_refs):
        x = jnp.where(turn_ref[0] == t, ref[t * n :], x)
    rows = out_refs[0].shape[0]
    for k, ref in enumerate(out_refs):
        inverse = inverse_ref[pl.ds(turn_ref[1 + k] * rows, rows), :]
        total = inverse[:, :1] * x[:1]
        for i in range(1, x.shape[0]):
            total += inverse[:, i : i + 1] * x[i : i + 1]
        ref[...] = total


def combine(which, inverse, turns, rows):
    count = len(turns)
    share = jax.ShapeDtypeStruct((rows, turns[0].shape[1]), F32)
    return pl.pallas_call(
        functools.partial(combine_kernel, count),
        in_specs=[pl.BlockSpec(memory_space=pltpu.SMEM)]
        + [pl.BlockSpec(memory_space=pltpu.VMEM)] * (count + 1),
        out_shape=[share] * count,
        name="combine",
    )(which, inverse, *turns)


def on_device(raw_columns, pivot_pairs, collocation, metric_factor):
    vec_total, orb_block, pair_block = raw_columns.shape
    gen_count = lax.axis_size("gen")
    gen_index = lax.axis_index("gen")
    fit_index = lax.axis_index("fit")
    chip = fit_index // 2
    core = fit_index % 2
    points = metric_factor.shape[0]
    vec_dev = vec_total // gen_count
    move = mover(gen_count)
    others = range(1, gen_count)
    diagonal = gen_index == chip
    swap = lambda g, j, c: (g, j, 1 - c)

    part = points // gen_count
    across = lambda k: lambda g, j, c: (g, j ^ k, c)
    halves = collocation.reshape(2, orb_block // 2, points)
    spread = []
    for k in range(gen_count):
        piece = lax.dynamic_slice_in_dim(halves, (gen_index ^ k) * part, part, 2)
        spread.append(move(piece, lambda g, j, c, k=k: (g ^ k, j, c)) if k else piece)
    spread = jnp.stack(spread)
    early = 2
    half = points // 2
    early_parts = [move(collocation[:, :half], across(early))]
    sibling = move(raw_columns, swap)
    sibling, metric_late = lax.optimization_barrier((sibling, metric_factor))
    own_block = lax.dynamic_slice_in_dim(metric_late, core * points, points, 1)
    own_rows = metric_late.astype(BF16)
    second_half = collocation[:, half:]
    spread, sibling, early_parts, own_block, own_rows, second_half, first = lax.optimization_barrier(
        (spread, sibling, early_parts, own_block, own_rows, second_half, collocation)
    )
    early_parts.append(move(second_half, across(early)))
    sib_block = move(own_block, swap)

    if gen_count == 4:
        bunches = [[(1, 1), (2, 1), (3, 1)], [(3, 2)], [(2, 2), (3, 3)]]
        soon = 2
    else:
        bunches = [[(j, d) for j in range(d, gen_count)] for d in others]
        soon = 1
    bunch_of = {place: n for n, bunch in enumerate(bunches) for place in bunch}

    def leftwards(n):
        away = dict(bunches[n])
        return lambda g, j, c: (j, j, c) if j in away and g == j - away[j] else None

    left_own = [move(own_rows, leftwards(n)) for n in range(soon)]
    spread, early_parts, first, sib_block, left_own[0] = lax.optimization_barrier(
        (spread, early_parts, first, sib_block, left_own[0])
    )
    own_parts = []
    for k in range(gen_count):
        piece = lax.dynamic_index_in_dim(spread, gen_index ^ chip ^ k, 0, keepdims=False)
        own_parts.append(move(piece, across(k)) if k else piece)
    own_parts, first, own_block, sib_block, left_own = lax.optimization_barrier(
        (own_parts, first, own_block, sib_block, left_own)
    )
    first_side = {0: [collocation], early: early_parts}
    for k in others:
        if k != early:
            first_side[k] = [move(first, across(k))]
    all_parts = [jnp.stack(own_parts)]
    for k in others:
        all_parts.append(move(all_parts[0], lambda g, j, c, k=k: (g ^ k, j, c)))

    def second_side(k):
        if part % 128 == 0:
            return all_parts
        whole = jnp.zeros(halves.shape, BF16)
        for n, x in enumerate(all_parts):
            whole = lax.dynamic_update_slice_in_dim(whole, x[k], (gen_index ^ n) * part, 2)
        return [whole[None]]

    own_raw = raw_columns.transpose(1, 0, 2)
    sib_raw = sibling.transpose(1, 0, 2)
    pivot_rows = pivot_pairs // NORB - gen_index * orb_block
    own_cols = pivot_pairs % NORB - fit_index * pair_block
    sib_cols = pivot_pairs % NORB - (fit_index ^ 1) * pair_block
    entries = pivot_entries(own_raw, sib_raw, pivot_rows, own_cols, sib_cols)

    own_inverse, upper = invert_blocks(
        jnp.stack([core, diagonal.astype(jnp.int32)]), own_block, sib_block
    )
    corner = jnp.dot(metric_factor[:, :points], upper, precision=HIGHEST)
    corner = -jnp.dot(own_inverse, corner, precision=HIGHEST)
    inverse_rows = split_hi_lo(
        jnp.concatenate(
            [
                jnp.where(core == 0, own_inverse, corner),
                jnp.where(core == 0, jnp.zeros_like(own_inverse), own_inverse),
            ],
            axis=1,
        )
    )

    _, _, inverse_rows, left_rows, left_own = lax.optimization_barrier(
        (all_parts, first_side, inverse_rows, own_rows, left_own)
    )
    for n in range(soon, len(bunches)):
        left_own.append(move(left_rows, leftwards(n)))
    left_sib = [move(left_own[n], swap) for n in range(soon)]

    own_raw = own_raw.reshape(orb_block * vec_total, pair_block)
    sib_raw = sib_raw.reshape(orb_block * vec_total, pair_block)
    where = jnp.stack([core] + [gen_index ^ k for k in range(gen_count)])
    total = None
    late = [k for k in others if k != early]
    for group in [[0, early]] + [late[i : i + 2] for i in range(0, len(late), 2)]:
        shares = project(
            where,
            own_raw,
            sib_raw,
            entries,
            [first_side[k] for k in group],
            [second_side(k) for k in group],
            [k if part % 128 == 0 else 0 for k in group],
        )
        if 0 in group:
            entries, left_sib = lax.optimization_barrier((entries, left_sib))
        for k, share in zip(group, shares):
            if k:
                share = move(share, across(k))
            total = share if total is None else total + share
    total = sum([move(total, lambda g, j, c, k=k: (g ^ k, j, c)) for k in others], total)
    at_core = core[None]
    sib_total = move(total, swap)
    solved = apply_weights(at_core, inverse_rows, total, sib_total)
    inverse_factor = factor_inverse(total)
    turns = [solved]
    for t in range(1, gen_count):
        near = move(solved, lambda g, j, c: (t, t, c) if g == j == t - 1 else None)
        near_sib = move(solved, lambda g, j, c: (t, t, 1 - c) if g == j == t - 1 else None)
        if t == 1:
            near, inverse_factor = lax.optimization_barrier((near, inverse_factor))
        lefts = []
        for d in range(1, t + 1):
            lefts += [left_own[bunch_of[t, d]], left_sib[bunch_of[t, d]]]
        solved = turn(at_core, lefts, inverse_rows, near, near_sib, total, sib_total)
        turns.append(solved)
        if t == 1:
            for n in range(soon, len(bunches)):
                _, left_own[n] = lax.optimization_barrier((solved, left_own[n]))
                left_sib.append(move(left_own[n], swap))

    which = jnp.stack([jnp.where(diagonal, gen_index, -1)] + [gen_index ^ k for k in range(gen_count)])
    shares = combine(which, inverse_factor, turns, vec_dev)
    result = shares[0]
    for k in others:
        result += move(shares[k], lambda g, j, c, k=k: (g ^ k, j, c) if g == j else None)
    return result


def solution(mesh):
    in_specs = (P(None, "gen", "fit"), P(), P("gen", "fit"), P("fit", "gen"))
    out_specs = P("gen", "fit")
    return jax.shard_map(
        on_device, mesh=mesh, in_specs=in_specs, out_specs=out_specs, check_vma=False
    )
```

```python
import functools

import jax
import jax.numpy as jnp
from jax import lax
from jax.experimental import pallas as pl
from jax.experimental.pallas import tpu as pltpu
from jax.sharding import PartitionSpec as P

NORB = 2000
F32 = jnp.float32
BF16 = jnp.bfloat16
BOTH = ("gen", "fit")
HIGHEST = lax.Precision.HIGHEST


def mover(gen_count):
    fit_count = 2 * gen_count

    def move(value, target):
        pairs = []
        for g in range(gen_count):
            for j in range(gen_count):
                for c in range(2):
                    to = target(g, j, c)
                    if to is not None:
                        pairs.append(
                            (g * fit_count + 2 * j + c, to[0] * fit_count + 2 * to[1] + to[2])
                        )
        return lax.ppermute(value, BOTH, pairs)

    return move


def split_hi_lo(x):
    hi = lax.reduce_precision(x, 8, 7)
    return hi.astype(BF16), (x - hi).astype(BF16)


def pivot_kernel(row_ref, own_ref, sib_ref, own_col_ref, sib_col_ref, out_ref, buffer, sems):
    count, orb = out_ref.shape[1], own_ref.shape[0]
    copies = []
    for i in range(count):
        row = jnp.clip(row_ref[i], 0, orb - 1)
        for n, ref in enumerate((own_ref, sib_ref)):
            copies.append(
                pltpu.make_async_copy(ref.at[row], buffer.at[2 * i + n], sems.at[2 * i + n])
            )
            copies[-1].start()
    lane = lax.broadcasted_iota(jnp.int32, buffer.shape[1:], 1)
    for i in range(count):
        copies[2 * i].wait()
        copies[2 * i + 1].wait()
        local = jnp.logical_and(row_ref[i] >= 0, row_ref[i] < orb)
        kept = jnp.where(lane == own_col_ref[i], buffer[2 * i].astype(F32), 0.0)
        kept += jnp.where(lane == sib_col_ref[i], buffer[2 * i + 1].astype(F32), 0.0)
        kept = jnp.where(local, kept, 0.0)
        out_ref[:, i : i + 1] = jnp.sum(kept, axis=1, keepdims=True)


def pivot_entries(own, sib, rows, own_cols, sib_cols):
    vec_total, pair = own.shape[1:]
    return pl.pallas_call(
        pivot_kernel,
        in_specs=[
            pl.BlockSpec(memory_space=pltpu.SMEM),
            pl.BlockSpec(memory_space=pltpu.HBM),
            pl.BlockSpec(memory_space=pltpu.HBM),
            pl.BlockSpec(memory_space=pltpu.SMEM),
            pl.BlockSpec(memory_space=pltpu.SMEM),
        ],
        out_specs=pl.BlockSpec(memory_space=pltpu.VMEM),
        out_shape=jax.ShapeDtypeStruct((vec_total, vec_total), F32),
        scratch_shapes=[
            pltpu.VMEM((2 * vec_total, vec_total, pair), BF16),
            pltpu.SemaphoreType.DMA((2 * vec_total,)),
        ],
        name="pivot_entries",
    )(rows, own, sib, own_cols, sib_cols)


def factor_inverse_kernel(block_ref, out_ref):
    n = block_ref.shape[0]
    a = block_ref[:, block_ref.shape[1] - 128 :][:, :n]
    row = lax.broadcasted_iota(jnp.int32, (n, n), 0)
    col = lax.broadcasted_iota(jnp.int32, (n, n), 1)
    w = (row == col).astype(F32)
    for i in range(n):
        pivot = a[i : i + 1, i : i + 1]
        scale = jnp.where(row[:, :1] > i, a[:, i : i + 1] / pivot, 0.0)
        w = w - scale * w[i : i + 1, :]
        a = a - scale * a[i : i + 1, :]
    diag = jnp.sum(jnp.where(row == col, a, 0.0), axis=1, keepdims=True)
    out_ref[...] = w / jnp.sqrt(diag)


def factor_inverse(block):
    return pl.pallas_call(
        factor_inverse_kernel,
        out_shape=jax.ShapeDtypeStruct((block.shape[0], block.shape[0]), F32),
        name="factor_inverse",
    )(block)


def project_kernel(vec_total, chunk, cp_counts, cq_count, where_ref, own_ref, sib_ref, entries_ref, *rest):
    blocks = len(cp_counts)
    cp_refs, rest = rest[: sum(cp_counts)], rest[sum(cp_counts) :]
    cq_refs, rest = rest[: blocks * cq_count], rest[blocks * cq_count :]
    out_refs, (cq, cp, acc) = rest[:blocks], rest[blocks:]
    points = cp.shape[2]
    step = pl.program_id(0)
    core = where_ref[0]

    @pl.when(step == 0)
    def _():
        for b in range(blocks):
            for n in range(cq_count):
                ref = cq_refs[b * cq_count + n]
                part = ref.shape[-1]
                start = 0
                if cq_count > 1:
                    start = pl.multiple_of(where_ref[1 + n] * part, part)
                cq[b, :, :, pl.ds(start, part)] = ref[0]
            start = 0
            for ref in cp_refs[sum(cp_counts[:b]) : sum(cp_counts[: b + 1])]:
                cp[b, :, start : start + ref.shape[1]] = ref[...].astype(F32)
                start += ref.shape[1]
            out_ref = out_refs[b]
            out_ref[:, points:] = jnp.zeros((vec_total, out_ref.shape[1] - points), F32)
            out_ref[:, points : points + vec_total] = entries_ref[...]
        acc[...] = jnp.zeros_like(acc)

    for b in range(blocks):
        mixed = jnp.dot(own_ref[...], cq[b, core], preferred_element_type=F32)
        mixed += jnp.dot(sib_ref[...], cq[b, 1 - core], preferred_element_type=F32)
        total = acc[b]
        for p in range(chunk):
            row = cp[b, pl.ds(step * chunk + p, 1), :]
            total += mixed[p * vec_total : (p + 1) * vec_total] * row
        acc[b] = total

    @pl.when(step == pl.num_programs(0) - 1)
    def _():
        for b in range(blocks):
            out_refs[b][:, :points] = acc[b]


def project(where, own, sib, entries, first, second, slots):
    orb = first[0][0].shape[0]
    points = sum(x.shape[1] for x in first[0])
    pair = own.shape[1]
    vec_total = own.shape[0] // orb
    chunk = 125
    blocks = len(first)
    whole = lambda i, s: (0, 0)
    specs, arrays = [], []
    for parts in first:
        for x in parts:
            specs.append(pl.BlockSpec(x.shape, whole))
            arrays.append(x)
    for parts, slot in zip(second, slots):
        for x in parts:
            specs.append(
                pl.BlockSpec((1,) + x.shape[1:], lambda i, s, slot=slot: (slot, 0, 0, 0))
            )
            arrays.append(x)
    kernel = functools.partial(
        project_kernel, vec_total, chunk, tuple(len(x) for x in first), len(second[0])
    )
    return pl.pallas_call(
        kernel,
        grid_spec=pltpu.PrefetchScalarGridSpec(
            num_scalar_prefetch=1,
            grid=(orb // chunk,),
            in_specs=[
                pl.BlockSpec((chunk * vec_total, pair), lambda i, s: (i, 0)),
                pl.BlockSpec((chunk * vec_total, pair), lambda i, s: (i, 0)),
                pl.BlockSpec((vec_total, vec_total), whole),
            ]
            + specs,
            out_specs=[pl.BlockSpec((vec_total, points + 128), whole)] * blocks,
            scratch_shapes=[
                pltpu.VMEM((blocks, 2, pair, points), BF16),
                pltpu.VMEM((blocks, orb, points), F32),
                pltpu.VMEM((blocks, vec_total, points), F32),
            ],
        ),
        out_shape=[jax.ShapeDtypeStruct((vec_total, points + 128), F32)] * blocks,
        compiler_params=pltpu.CompilerParams(vmem_limit_bytes=32 << 20),
        cost_estimate=pl.CostEstimate(
            flops=4 * orb * vec_total * pair * points * blocks,
            transcendentals=0,
            bytes_accessed=1 << 20,
        ),
        name="project",
    )(where, own, sib, entries, *arrays)


def invert_kernel(where_ref, block_ref, out_ref):
    n = block_ref.shape[0]
    tile = 128
    row = lax.broadcasted_iota(jnp.int32, (tile, tile), 0)
    col = lax.broadcasted_iota(jnp.int32, (tile, tile), 1)
    eye = (row == col).astype(F32)
    dot = functools.partial(jnp.dot, precision=HIGHEST, preferred_element_type=F32)
    holds = where_ref[1] == 1
    places = range(0, n, tile)
    parts = [jnp.where(holds, block_ref[b : b + tile, b : b + tile], eye) for b in places]
    xs = [eye / jnp.sum(part * eye, axis=1, keepdims=True) for part in parts]
    size = 1
    while size < tile:
        pick = (row // (2 * size) == col // (2 * size)) & (row // size > col // size)
        inner = [dot(jnp.where(pick, part, 0.0), x) for part, x in zip(parts, xs)]
        xs = [x - dot(x, y) for x, y in zip(xs, inner)]
        size *= 2
    out_ref[...] = jnp.zeros_like(out_ref)
    for b, x in zip(places, xs):
        out_ref[b : b + tile, b : b + tile] = x
    size = tile
    while size < n:
        for b in range(0, n, 2 * size):
            mid, end = b + size, b + 2 * size
            inner = dot(block_ref[mid:end, b:mid], out_ref[b:mid, b:mid])
            out_ref[mid:end, b:mid] = -dot(out_ref[mid:end, mid:end], inner)
        size *= 2


def invert_block(where, metric):
    n = metric.shape[0]
    return pl.pallas_call(
        invert_kernel,
        grid_spec=pltpu.PrefetchScalarGridSpec(
            num_scalar_prefetch=1,
            grid=(1,),
            in_specs=[pl.BlockSpec((n, n), lambda i, s: (0, s[0]))],
            out_specs=pl.BlockSpec((n, n), lambda i, s: (0, 0)),
        ),
        out_shape=jax.ShapeDtypeStruct((n, n), F32),
        compiler_params=pltpu.CompilerParams(vmem_limit_bytes=16 << 20),
        cost_estimate=pl.CostEstimate(flops=4 << 30, transcendentals=0, bytes_accessed=1 << 22),
        name="invert_block",
    )(where, metric)


def weigh(hi_ref, lo_ref, halves):
    dims = (((1,), (1,)), ((), ()))
    total = None
    for half, x in halves:
        hi = x.astype(BF16)
        lo = (x - hi.astype(F32)).astype(BF16)
        n = x.shape[0]
        width = x.shape[1]
        columns = pl.ds(pl.multiple_of(half * width, width), width)
        both = lax.dot_general(
            jnp.concatenate([hi, lo]), hi_ref[:, columns], dims, preferred_element_type=F32
        )
        part = both[:n] + both[n:]
        if lo_ref is not None:
            part += lax.dot_general(hi, lo_ref[:, columns], dims, preferred_element_type=F32)
        total = part if total is None else total + part
    return total


def apply_kernel(where_ref, *refs):
    weights, (xa_ref, xb_ref, out_ref) = refs[:-3], refs[-3:]
    core = where_ref[0]
    hi_ref, lo_ref = weights if len(weights) == 2 else (weights[0], None)
    points = out_ref.shape[1]
    halves = [(core, xa_ref[:, :points]), (1 - core, xb_ref[:, :points])]
    out_ref[...] = weigh(hi_ref, lo_ref, halves)


def apply_weights(where, weights, xa, xb):
    return pl.pallas_call(
        apply_kernel,
        in_specs=[pl.BlockSpec(memory_space=pltpu.SMEM)]
        + [pl.BlockSpec(memory_space=pltpu.VMEM)] * (len(weights) + 2),
        out_specs=pl.BlockSpec(memory_space=pltpu.VMEM),
        out_shape=jax.ShapeDtypeStruct((xa.shape[0], weights[0].shape[0]), F32),
        compiler_params=pltpu.CompilerParams(vmem_limit_bytes=12 << 20),
        cost_estimate=pl.CostEstimate(flops=1 << 30, transcendentals=0, bytes_accessed=1 << 21),
        name="apply_weights",
    )(where, *weights, xa, xb)


def turn_kernel(where_ref, *refs):
    left_own, left_sib, inv_hi, inv_lo, xa, xb, own_rest, sib_rest, out_ref, buffer, sems = refs
    core = where_ref[0]
    copies = [
        pltpu.make_async_copy(ref, buffer.at[i], sems.at[i])
        for i, ref in enumerate((left_own, left_sib))
    ]
    for copy in copies:
        copy.start()
    points = xa.shape[1]
    halves = [(core, xa[...]), (1 - core, xb[...])]
    copies[0].wait()
    own = own_rest[:, :points] - weigh(buffer.at[0], None, halves)
    copies[1].wait()
    sib = sib_rest[:, :points] - weigh(buffer.at[1], None, halves)
    out_ref[...] = weigh(inv_hi, inv_lo, [(core, own), (1 - core, sib)])


def turn(where, lefts, inverse, xa, xb, own_rest, sib_rest):
    vmem = pl.BlockSpec(memory_space=pltpu.VMEM)
    return pl.pallas_call(
        turn_kernel,
        in_specs=[pl.BlockSpec(memory_space=pltpu.SMEM)]
        + [pl.BlockSpec(memory_space=pl.ANY)] * 2
        + [vmem] * 6,
        out_specs=vmem,
        out_shape=jax.ShapeDtypeStruct(xa.shape, F32),
        scratch_shapes=[
            pltpu.VMEM((2,) + lefts[0].shape, BF16),
            pltpu.SemaphoreType.DMA((2,)),
        ],
        compiler_params=pltpu.CompilerParams(vmem_limit_bytes=16 << 20),
        cost_estimate=pl.CostEstimate(flops=2 << 30, transcendentals=0, bytes_accessed=1 << 22),
        name="turn",
    )(where, *lefts, *inverse, xa, xb, own_rest, sib_rest)


def combine_kernel(count, turn_ref, inverse_ref, *refs):
    x_refs, out_refs = refs[:count], refs[count:]
    x = jnp.zeros(x_refs[0].shape, F32)
    for t, ref in enumerate(x_refs):
        x = jnp.where(turn_ref[0] == t, ref[...], x)
    rows = out_refs[0].shape[0]
    for k, ref in enumerate(out_refs):
        inverse = inverse_ref[pl.ds(turn_ref[1 + k] * rows, rows), :]
        total = inverse[:, :1] * x[:1]
        for i in range(1, x.shape[0]):
            total += inverse[:, i : i + 1] * x[i : i + 1]
        ref[...] = total


def combine(which, inverse, turns, rows):
    count = len(turns)
    share = jax.ShapeDtypeStruct((rows, turns[0].shape[1]), F32)
    return pl.pallas_call(
        functools.partial(combine_kernel, count),
        in_specs=[pl.BlockSpec(memory_space=pltpu.SMEM)]
        + [pl.BlockSpec(memory_space=pltpu.VMEM)] * (count + 1),
        out_shape=[share] * count,
        name="combine",
    )(which, inverse, *turns)


def on_device(raw_columns, pivot_pairs, collocation, metric_factor):
    vec_total, orb_block, pair_block = raw_columns.shape
    gen_count = lax.axis_size("gen")
    gen_index = lax.axis_index("gen")
    fit_index = lax.axis_index("fit")
    chip = fit_index // 2
    core = fit_index % 2
    points = metric_factor.shape[0]
    vec_dev = vec_total // gen_count
    move = mover(gen_count)
    others = range(1, gen_count)
    diagonal = gen_index == chip
    swap = lambda g, j, c: (g, j, 1 - c)

    part = points // gen_count
    across = lambda k: lambda g, j, c: (g, j ^ k, c)
    halves = collocation.reshape(2, orb_block // 2, points)
    spread = []
    for k in range(gen_count):
        piece = lax.dynamic_slice_in_dim(halves, (gen_index ^ k) * part, part, 2)
        spread.append(move(piece, lambda g, j, c, k=k: (g ^ k, j, c)) if k else piece)
    spread = jnp.stack(spread)
    early, half = 2, points // 2
    sibling = move(raw_columns, swap)
    early_parts = [move(collocation[:, :half], across(early))]
    second_half = collocation[:, half:]
    spread, sibling, early_parts, second_half, metric_late = lax.optimization_barrier(
        (spread, sibling, early_parts, second_half, metric_factor)
    )
    early_parts.append(move(second_half, across(early)))
    own_rows = metric_late.astype(BF16)
    left_own = move(own_rows, lambda g, j, c: (g + 1, j, c) if j == g + 1 else None)
    own_parts = []
    for k in range(gen_count):
        piece = lax.dynamic_index_in_dim(spread, gen_index ^ chip ^ k, 0, keepdims=False)
        own_parts.append(move(piece, across(k)) if k else piece)
    own_parts, sibling, metric_late = lax.optimization_barrier((own_parts, sibling, metric_late))

    own_raw = raw_columns.transpose(1, 0, 2)
    sib_raw = sibling.transpose(1, 0, 2)
    pivot_rows = pivot_pairs // NORB - gen_index * orb_block
    own_cols = pivot_pairs % NORB - fit_index * pair_block
    sib_cols = pivot_pairs % NORB - (fit_index ^ 1) * pair_block
    entries = pivot_entries(own_raw, sib_raw, pivot_rows, own_cols, sib_cols)

    own_inverse = invert_block(jnp.stack([core, diagonal.astype(jnp.int32)]), metric_late)
    own_parts, first, early_parts, left_own, own_inverse, entries = lax.optimization_barrier(
        (own_parts, collocation, early_parts, left_own, own_inverse, entries)
    )
    upper = move(own_inverse, swap)
    first_side = {0: [collocation], early: early_parts}
    for k in others:
        if k != early:
            first_side[k] = [move(first, across(k))]
    all_parts = [jnp.stack(own_parts)]
    for k in others:
        all_parts.append(move(all_parts[0], lambda g, j, c, k=k: (g ^ k, j, c)))

    def second_side(k):
        if part % 128 == 0:
            return all_parts
        whole = jnp.zeros(halves.shape, BF16)
        for n, x in enumerate(all_parts):
            whole = lax.dynamic_update_slice_in_dim(whole, x[k], (gen_index ^ n) * part, 2)
        return [whole[None]]

    corner = jnp.dot(metric_factor[:, :points], upper, precision=HIGHEST)
    corner = -jnp.dot(own_inverse, corner, precision=HIGHEST)
    inverse_rows = split_hi_lo(
        jnp.concatenate(
            [
                jnp.where(core == 0, own_inverse, corner),
                jnp.where(core == 0, jnp.zeros_like(own_inverse), own_inverse),
            ],
            axis=1,
        )
    )

    all_parts, first_side, entries, inverse_rows = lax.optimization_barrier(
        (all_parts, first_side, entries, inverse_rows)
    )
    left_sib = move(left_own, swap)

    own_raw = own_raw.reshape(orb_block * vec_total, pair_block)
    sib_raw = sib_raw.reshape(orb_block * vec_total, pair_block)
    where = jnp.stack([core] + [gen_index ^ k for k in range(gen_count)])
    total = None
    for group in [list(range(i, min(i + 4, gen_count))) for i in range(0, gen_count, 4)]:
        shares = project(
            where,
            own_raw,
            sib_raw,
            entries,
            [first_side[k] for k in group],
            [second_side(k) for k in group],
            [k if part % 128 == 0 else 0 for k in group],
        )
        if group[0] == 0:
            shares, left_sib = lax.optimization_barrier((shares, left_sib))
        for k, share in zip(group, shares):
            if k:
                share = move(share, across(k))
            total = share if total is None else total + share
    total = sum([move(total, lambda g, j, c, k=k: (g ^ k, j, c)) for k in others], total)

    at_core = core[None]
    inverse_factor = factor_inverse(total)
    rest, sib_rest = total, move(total, swap)
    solved = apply_weights(at_core, inverse_rows, rest, sib_rest)
    turns = [solved]
    far = {}
    for t in range(gen_count - 1):
        near = move(solved, lambda g, j, c: (t + 1, t + 1, c) if g == j == t else None)
        near_sib = move(solved, lambda g, j, c: (t + 1, t + 1, 1 - c) if g == j == t else None)
        for z in range(t + 2, gen_count):
            one = move(solved, lambda g, j, c: (t, z, c) if g == j == t else None)
            far[t] = far[t] + one if t in far else one
        if t == 0:
            near, inverse_factor = lax.optimization_barrier((near, inverse_factor))
        if t - 1 in far:
            gone, _ = lax.optimization_barrier((far[t - 1], solved))
            brought = apply_weights(at_core, [own_rows], gone, move(gone, swap))
            brought = move(
                brought, lambda g, j, c: (j, j, c) if g == t - 1 and j >= t + 1 else None
            )
            rest = rest[:, :points] - brought
            sib_rest = move(rest, swap)
        solved = turn(at_core, (left_own, left_sib), inverse_rows, near, near_sib, rest, sib_rest)
        turns.append(solved)

    which = jnp.stack([jnp.where(diagonal, gen_index, -1)] + [gen_index ^ k for k in range(gen_count)])
    shares = combine(which, inverse_factor, turns, vec_dev)
    result = shares[0]
    for k in others:
        result += move(shares[k], lambda g, j, c, k=k: (g ^ k, j, c) if g == j else None)
    return result


def solution(mesh):
    in_specs = (P(None, "gen", "fit"), P(), P("gen", "fit"), P("fit", "gen"))
    out_specs = P("gen", "fit")
    return jax.shard_map(
        on_device, mesh=mesh, in_specs=in_specs, out_specs=out_specs, check_vma=False
    )
```

```python
import functools

import jax
import jax.numpy as jnp
from jax import lax
from jax.experimental import pallas as pl
from jax.experimental.pallas import tpu as pltpu
from jax.sharding import PartitionSpec as P

NORB = 2000
F32 = jnp.float32
BF16 = jnp.bfloat16
BOTH = ("gen", "fit")
HIGHEST = lax.Precision.HIGHEST


def mover(gen_count):
    fit_count = 2 * gen_count

    def move(value, target):
        pairs = []
        for g in range(gen_count):
            for j in range(gen_count):
                for c in range(2):
                    to = target(g, j, c)
                    if to is not None:
                        pairs.append(
                            (g * fit_count + 2 * j + c, to[0] * fit_count + 2 * to[1] + to[2])
                        )
        return lax.ppermute(value, BOTH, pairs)

    return move


def split_hi_lo(x):
    hi = lax.reduce_precision(x, 8, 7)
    return hi.astype(BF16), (x - hi).astype(BF16)


def pivot_kernel(row_ref, own_ref, sib_ref, own_col_ref, sib_col_ref, out_ref, buffer, sems):
    count, orb = out_ref.shape[1], own_ref.shape[0]
    copies = []
    for i in range(count):
        row = jnp.clip(row_ref[i], 0, orb - 1)
        for n, ref in enumerate((own_ref, sib_ref)):
            copies.append(
                pltpu.make_async_copy(ref.at[row], buffer.at[2 * i + n], sems.at[2 * i + n])
            )
            copies[-1].start()
    lane = lax.broadcasted_iota(jnp.int32, buffer.shape[1:], 1)
    for i in range(count):
        copies[2 * i].wait()
        copies[2 * i + 1].wait()
        local = jnp.logical_and(row_ref[i] >= 0, row_ref[i] < orb)
        kept = jnp.where(lane == own_col_ref[i], buffer[2 * i].astype(F32), 0.0)
        kept += jnp.where(lane == sib_col_ref[i], buffer[2 * i + 1].astype(F32), 0.0)
        kept = jnp.where(local, kept, 0.0)
        out_ref[:, i : i + 1] = jnp.sum(kept, axis=1, keepdims=True)


def pivot_entries(own, sib, rows, own_cols, sib_cols):
    vec_total, pair = own.shape[1:]
    return pl.pallas_call(
        pivot_kernel,
        in_specs=[
            pl.BlockSpec(memory_space=pltpu.SMEM),
            pl.BlockSpec(memory_space=pltpu.HBM),
            pl.BlockSpec(memory_space=pltpu.HBM),
            pl.BlockSpec(memory_space=pltpu.SMEM),
            pl.BlockSpec(memory_space=pltpu.SMEM),
        ],
        out_specs=pl.BlockSpec(memory_space=pltpu.VMEM),
        out_shape=jax.ShapeDtypeStruct((vec_total, vec_total), F32),
        scratch_shapes=[
            pltpu.VMEM((2 * vec_total, vec_total, pair), BF16),
            pltpu.SemaphoreType.DMA((2 * vec_total,)),
        ],
        name="pivot_entries",
    )(rows, own, sib, own_cols, sib_cols)


def factor_inverse_kernel(block_ref, out_ref):
    n = block_ref.shape[0]
    a = block_ref[:, block_ref.shape[1] - 128 :][:, :n]
    row = lax.broadcasted_iota(jnp.int32, (n, n), 0)
    col = lax.broadcasted_iota(jnp.int32, (n, n), 1)
    w = (row == col).astype(F32)
    for i in range(n):
        pivot = a[i : i + 1, i : i + 1]
        scale = jnp.where(row[:, :1] > i, a[:, i : i + 1] / pivot, 0.0)
        w = w - scale * w[i : i + 1, :]
        a = a - scale * a[i : i + 1, :]
    diag = jnp.sum(jnp.where(row == col, a, 0.0), axis=1, keepdims=True)
    out_ref[...] = w / jnp.sqrt(diag)


def factor_inverse(block):
    return pl.pallas_call(
        factor_inverse_kernel,
        out_shape=jax.ShapeDtypeStruct((block.shape[0], block.shape[0]), F32),
        name="factor_inverse",
    )(block)


def project_kernel(vec_total, chunk, cp_counts, cq_count, where_ref, own_ref, sib_ref, entries_ref, *rest):
    blocks = len(cp_counts)
    cp_refs, rest = rest[: sum(cp_counts)], rest[sum(cp_counts) :]
    cq_refs, rest = rest[: blocks * cq_count], rest[blocks * cq_count :]
    out_refs, (cq, cp, acc) = rest[:blocks], rest[blocks:]
    points = cp.shape[2]
    step = pl.program_id(0)
    core = where_ref[0]

    @pl.when(step == 0)
    def _():
        for b in range(blocks):
            for n in range(cq_count):
                ref = cq_refs[b * cq_count + n]
                part = ref.shape[-1]
                start = 0
                if cq_count > 1:
                    start = pl.multiple_of(where_ref[1 + n] * part, part)
                cq[b, :, :, pl.ds(start, part)] = ref[0]
            start = 0
            for ref in cp_refs[sum(cp_counts[:b]) : sum(cp_counts[: b + 1])]:
                cp[b, :, start : start + ref.shape[1]] = ref[...].astype(F32)
                start += ref.shape[1]
            out_ref = out_refs[b]
            out_ref[:, points:] = jnp.zeros((vec_total, out_ref.shape[1] - points), F32)
            out_ref[:, points : points + vec_total] = entries_ref[...]
        acc[...] = jnp.zeros_like(acc)

    for b in range(blocks):
        mixed = jnp.dot(own_ref[...], cq[b, core], preferred_element_type=F32)
        mixed += jnp.dot(sib_ref[...], cq[b, 1 - core], preferred_element_type=F32)
        total = acc[b]
        for p in range(chunk):
            row = cp[b, pl.ds(step * chunk + p, 1), :]
            total += mixed[p * vec_total : (p + 1) * vec_total] * row
        acc[b] = total

    @pl.when(step == pl.num_programs(0) - 1)
    def _():
        for b in range(blocks):
            out_refs[b][:, :points] = acc[b]


def project(where, own, sib, entries, first, second, slots):
    orb = first[0][0].shape[0]
    points = sum(x.shape[1] for x in first[0])
    pair = own.shape[1]
    vec_total = own.shape[0] // orb
    chunk = 125
    blocks = len(first)
    whole = lambda i, s: (0, 0)
    specs, arrays = [], []
    for parts in first:
        for x in parts:
            specs.append(pl.BlockSpec(x.shape, whole))
            arrays.append(x)
    for parts, slot in zip(second, slots):
        for x in parts:
            specs.append(
                pl.BlockSpec((1,) + x.shape[1:], lambda i, s, slot=slot: (slot, 0, 0, 0))
            )
            arrays.append(x)
    kernel = functools.partial(
        project_kernel, vec_total, chunk, tuple(len(x) for x in first), len(second[0])
    )
    return pl.pallas_call(
        kernel,
        grid_spec=pltpu.PrefetchScalarGridSpec(
            num_scalar_prefetch=1,
            grid=(orb // chunk,),
            in_specs=[
                pl.BlockSpec((chunk * vec_total, pair), lambda i, s: (i, 0)),
                pl.BlockSpec((chunk * vec_total, pair), lambda i, s: (i, 0)),
                pl.BlockSpec((vec_total, vec_total), whole),
            ]
            + specs,
            out_specs=[pl.BlockSpec((vec_total, points + 128), whole)] * blocks,
            scratch_shapes=[
                pltpu.VMEM((blocks, 2, pair, points), BF16),
                pltpu.VMEM((blocks, orb, points), F32),
                pltpu.VMEM((blocks, vec_total, points), F32),
            ],
        ),
        out_shape=[jax.ShapeDtypeStruct((vec_total, points + 128), F32)] * blocks,
        compiler_params=pltpu.CompilerParams(vmem_limit_bytes=32 << 20),
        cost_estimate=pl.CostEstimate(
            flops=4 * orb * vec_total * pair * points * blocks,
            transcendentals=0,
            bytes_accessed=1 << 20,
        ),
        name="project",
    )(where, own, sib, entries, *arrays)


def invert_kernel(where_ref, block_ref, out_ref):
    n = block_ref.shape[0]
    tile = 128
    row = lax.broadcasted_iota(jnp.int32, (tile, tile), 0)
    col = lax.broadcasted_iota(jnp.int32, (tile, tile), 1)
    eye = (row == col).astype(F32)
    dot = functools.partial(jnp.dot, precision=HIGHEST, preferred_element_type=F32)
    holds = where_ref[1] == 1
    places = range(0, n, tile)
    parts = [jnp.where(holds, block_ref[b : b + tile, b : b + tile], eye) for b in places]
    xs = [eye / jnp.sum(part * eye, axis=1, keepdims=True) for part in parts]
    size = 1
    while size < tile:
        pick = (row // (2 * size) == col // (2 * size)) & (row // size > col // size)
        inner = [dot(jnp.where(pick, part, 0.0), x) for part, x in zip(parts, xs)]
        xs = [x - dot(x, y) for x, y in zip(xs, inner)]
        size *= 2
    out_ref[...] = jnp.zeros_like(out_ref)
    for b, x in zip(places, xs):
        out_ref[b : b + tile, b : b + tile] = x
    size = tile
    while size < n:
        for b in range(0, n, 2 * size):
            mid, end = b + size, b + 2 * size
            inner = dot(block_ref[mid:end, b:mid], out_ref[b:mid, b:mid])
            out_ref[mid:end, b:mid] = -dot(out_ref[mid:end, mid:end], inner)
        size *= 2


def invert_block(where, metric):
    n = metric.shape[0]
    return pl.pallas_call(
        invert_kernel,
        grid_spec=pltpu.PrefetchScalarGridSpec(
            num_scalar_prefetch=1,
            grid=(1,),
            in_specs=[pl.BlockSpec((n, n), lambda i, s: (0, s[0]))],
            out_specs=pl.BlockSpec((n, n), lambda i, s: (0, 0)),
        ),
        out_shape=jax.ShapeDtypeStruct((n, n), F32),
        compiler_params=pltpu.CompilerParams(vmem_limit_bytes=16 << 20),
        cost_estimate=pl.CostEstimate(flops=4 << 30, transcendentals=0, bytes_accessed=1 << 22),
        name="invert_block",
    )(where, metric)


def weigh(hi_ref, lo_ref, halves):
    dims = (((1,), (1,)), ((), ()))
    total = None
    for half, x in halves:
        hi = x.astype(BF16)
        lo = (x - hi.astype(F32)).astype(BF16)
        n = x.shape[0]
        width = x.shape[1]
        columns = pl.ds(pl.multiple_of(half * width, width), width)
        both = lax.dot_general(
            jnp.concatenate([hi, lo]), hi_ref[:, columns], dims, preferred_element_type=F32
        )
        part = both[:n] + both[n:]
        if lo_ref is not None:
            part += lax.dot_general(hi, lo_ref[:, columns], dims, preferred_element_type=F32)
        total = part if total is None else total + part
    return total


def apply_kernel(where_ref, *refs):
    weights, (xa_ref, xb_ref, out_ref) = refs[:-3], refs[-3:]
    core = where_ref[0]
    hi_ref, lo_ref = weights if len(weights) == 2 else (weights[0], None)
    points = out_ref.shape[1]
    halves = [(core, xa_ref[:, :points]), (1 - core, xb_ref[:, :points])]
    out_ref[...] = weigh(hi_ref, lo_ref, halves)


def apply_weights(where, weights, xa, xb):
    return pl.pallas_call(
        apply_kernel,
        in_specs=[pl.BlockSpec(memory_space=pltpu.SMEM)]
        + [pl.BlockSpec(memory_space=pltpu.VMEM)] * (len(weights) + 2),
        out_specs=pl.BlockSpec(memory_space=pltpu.VMEM),
        out_shape=jax.ShapeDtypeStruct((xa.shape[0], weights[0].shape[0]), F32),
        compiler_params=pltpu.CompilerParams(vmem_limit_bytes=12 << 20),
        cost_estimate=pl.CostEstimate(flops=1 << 30, transcendentals=0, bytes_accessed=1 << 21),
        name="apply_weights",
    )(where, *weights, xa, xb)


def turn_kernel(count, where_ref, *refs):
    weights, refs = refs[: 2 * count + 2], refs[2 * count + 2 :]
    xa, xb, own_rest, sib_rest, out_ref, buffer, sems = refs
    core = where_ref[0]
    copies = [
        pltpu.make_async_copy(ref, buffer.at[i], sems.at[i]) for i, ref in enumerate(weights)
    ]
    for copy in copies:
        copy.start()
    points = xa.shape[1]
    n = own_rest.shape[0]
    own, sib = own_rest[:, :points], sib_rest[:, :points]
    for i in range(count):
        halves = [(core, xa[i * n : (i + 1) * n]), (1 - core, xb[i * n : (i + 1) * n])]
        copies[2 * i].wait()
        own -= weigh(buffer.at[2 * i], None, halves)
        copies[2 * i + 1].wait()
        sib -= weigh(buffer.at[2 * i + 1], None, halves)
    copies[-2].wait()
    copies[-1].wait()
    solved = weigh(
        buffer.at[2 * count], buffer.at[2 * count + 1], [(core, own), (1 - core, sib)]
    )
    if out_ref.shape[0] > n:
        out_ref[: count * n] = xa[...]
    out_ref[out_ref.shape[0] - n :] = solved


def turn(where, lefts, inverse, xa, xb, own_rest, sib_rest, keep):
    vmem = pl.BlockSpec(memory_space=pltpu.VMEM)
    weights = [*lefts, *inverse]
    n, points = own_rest.shape[0], xa.shape[1]
    count = len(lefts) // 2
    return pl.pallas_call(
        functools.partial(turn_kernel, count),
        in_specs=[pl.BlockSpec(memory_space=pltpu.SMEM)]
        + [pl.BlockSpec(memory_space=pltpu.HBM)] * len(weights)
        + [vmem] * 4,
        out_specs=vmem,
        out_shape=jax.ShapeDtypeStruct(((count + 1) * n if keep else n, points), F32),
        scratch_shapes=[
            pltpu.VMEM((len(weights),) + weights[0].shape, BF16),
            pltpu.SemaphoreType.DMA((len(weights),)),
        ],
        compiler_params=pltpu.CompilerParams(vmem_limit_bytes=32 << 20),
        cost_estimate=pl.CostEstimate(flops=1 << 20, transcendentals=0, bytes_accessed=1 << 16),
        name="turn",
    )(where, *weights, xa, xb, own_rest, sib_rest)


def combine_kernel(count, turn_ref, inverse_ref, *refs):
    x_refs, out_refs = refs[:count], refs[count:]
    x = jnp.zeros(x_refs[0].shape, F32)
    for t, ref in enumerate(x_refs):
        x = jnp.where(turn_ref[0] == t, ref[ref.shape[0] - x.shape[0] :], x)
    rows = out_refs[0].shape[0]
    for k, ref in enumerate(out_refs):
        inverse = inverse_ref[pl.ds(turn_ref[1 + k] * rows, rows), :]
        total = inverse[:, :1] * x[:1]
        for i in range(1, x.shape[0]):
            total += inverse[:, i : i + 1] * x[i : i + 1]
        ref[...] = total


def combine(which, inverse, turns, rows):
    count = len(turns)
    share = jax.ShapeDtypeStruct((rows, turns[0].shape[1]), F32)
    return pl.pallas_call(
        functools.partial(combine_kernel, count),
        in_specs=[pl.BlockSpec(memory_space=pltpu.SMEM)]
        + [pl.BlockSpec(memory_space=pltpu.VMEM)] * (count + 1),
        out_shape=[share] * count,
        name="combine",
    )(which, inverse, *turns)


def on_device(raw_columns, pivot_pairs, collocation, metric_factor):
    vec_total, orb_block, pair_block = raw_columns.shape
    gen_count = lax.axis_size("gen")
    gen_index = lax.axis_index("gen")
    fit_index = lax.axis_index("fit")
    chip = fit_index // 2
    core = fit_index % 2
    points = metric_factor.shape[0]
    vec_dev = vec_total // gen_count
    move = mover(gen_count)
    others = range(1, gen_count)
    diagonal = gen_index == chip
    swap = lambda g, j, c: (g, j, 1 - c)

    part = points // gen_count
    across = lambda k: lambda g, j, c: (g, j ^ k, c)
    halves = collocation.reshape(2, orb_block // 2, points)
    spread = []
    for k in range(gen_count):
        piece = lax.dynamic_slice_in_dim(halves, (gen_index ^ k) * part, part, 2)
        spread.append(move(piece, lambda g, j, c, k=k: (g ^ k, j, c)) if k else piece)
    spread = jnp.stack(spread)
    early, half = 2, points // 2
    sibling = move(raw_columns, swap)
    early_parts = [move(collocation[:, :half], across(early))]
    second_half = collocation[:, half:]
    spread, sibling, early_parts, second_half, metric_late = lax.optimization_barrier(
        (spread, sibling, early_parts, second_half, metric_factor)
    )
    early_parts.append(move(second_half, across(early)))
    own_rows = metric_late.astype(BF16)
    left_own = move(own_rows, lambda g, j, c: (g + 1, j, c) if j == g + 1 else None)
    own_parts = []
    for k in range(gen_count):
        piece = lax.dynamic_index_in_dim(spread, gen_index ^ chip ^ k, 0, keepdims=False)
        own_parts.append(move(piece, across(k)) if k else piece)
    own_raw = raw_columns.transpose(1, 0, 2)
    sib_raw = sibling.transpose(1, 0, 2)
    pivot_rows = pivot_pairs // NORB - gen_index * orb_block
    own_cols = pivot_pairs % NORB - fit_index * pair_block
    sib_cols = pivot_pairs % NORB - (fit_index ^ 1) * pair_block
    entries = pivot_entries(own_raw, sib_raw, pivot_rows, own_cols, sib_cols)

    own_inverse = invert_block(jnp.stack([core, diagonal.astype(jnp.int32)]), metric_late)
    own_parts, first, early_parts, left_own, own_inverse, entries = lax.optimization_barrier(
        (own_parts, collocation, early_parts, left_own, own_inverse, entries)
    )
    upper = move(own_inverse, swap)
    first_side = {0: [collocation], early: early_parts}
    for k in others:
        if k != early:
            first_side[k] = [move(first, across(k))]
    all_parts = [jnp.stack(own_parts)]
    for k in others:
        all_parts.append(move(all_parts[0], lambda g, j, c, k=k: (g ^ k, j, c)))

    def second_side(k):
        if part % 128 == 0:
            return all_parts
        whole = jnp.zeros(halves.shape, BF16)
        for n, x in enumerate(all_parts):
            whole = lax.dynamic_update_slice_in_dim(whole, x[k], (gen_index ^ n) * part, 2)
        return [whole[None]]

    corner = jnp.dot(metric_factor[:, :points], upper, precision=HIGHEST)
    corner = -jnp.dot(own_inverse, corner, precision=HIGHEST)
    inverse_rows = split_hi_lo(
        jnp.concatenate(
            [
                jnp.where(core == 0, own_inverse, corner),
                jnp.where(core == 0, jnp.zeros_like(own_inverse), own_inverse),
            ],
            axis=1,
        )
    )

    all_parts, first_side, entries, inverse_rows, left_rows = lax.optimization_barrier(
        (all_parts, first_side, entries, inverse_rows, own_rows)
    )
    left_own, left_sib = {1: left_own}, {1: move(left_own, swap)}
    for d in range(2, gen_count - 1):
        left_own[d] = move(left_rows, lambda g, j, c: (j, j, c) if g >= 1 and j == g + d else None)

    own_raw = own_raw.reshape(orb_block * vec_total, pair_block)
    sib_raw = sib_raw.reshape(orb_block * vec_total, pair_block)
    where = jnp.stack([core] + [gen_index ^ k for k in range(gen_count)])
    total = None
    for group in [list(range(i, min(i + 4, gen_count))) for i in range(0, gen_count, 4)]:
        shares = project(
            where,
            own_raw,
            sib_raw,
            entries,
            [first_side[k] for k in group],
            [second_side(k) for k in group],
            [k if part % 128 == 0 else 0 for k in group],
        )
        if group[0] == 0:
            shares, left_sib[1] = lax.optimization_barrier((shares, left_sib[1]))
        for k, share in zip(group, shares):
            if k:
                share = move(share, across(k))
            total = share if total is None else total + share
    total = sum([move(total, lambda g, j, c, k=k: (g ^ k, j, c)) for k in others], total)

    at_core = core[None]
    inverse_factor = factor_inverse(total)
    rest, sib_rest = total, move(total, swap)
    solved = apply_weights(at_core, inverse_rows, rest, sib_rest)
    turns = [solved]
    for t in range(1, gen_count):
        near = move(solved, lambda g, j, c: (t, t, c) if g == j == t - 1 else None)
        near_sib = move(solved, lambda g, j, c: (t, t, 1 - c) if g == j == t - 1 else None)
        if t == 1 and gen_count > 2:
            far = [
                move(solved, lambda g, j, c: (0, z, c) if g == j == 0 else None)
                for z in range(2, gen_count)
            ]
            far = sum(far[1:], far[0])
            acted = apply_weights(at_core, [own_rows], far, move(far, swap))
            brought = move(acted, lambda g, j, c: (j, j, c) if g == 0 and j >= 2 else None)
            near, near_sib, acted = lax.optimization_barrier((near, near_sib, acted))
        if t == 2:
            rest = rest[:, :points] - brought
            sib_rest = move(rest, swap)
            near, inverse_factor = lax.optimization_barrier((near, inverse_factor))
        lefts = []
        for g in range(min(1, t - 1), t):
            lefts += [left_own[t - g], left_sib[t - g]]
        solved = turn(at_core, lefts, inverse_rows, near, near_sib, rest, sib_rest, t > 1)
        turns.append(solved)
        if t == 1:
            for d in range(2, gen_count - 1):
                _, left_own[d] = lax.optimization_barrier((solved, left_own[d]))
                left_sib[d] = move(left_own[d], swap)

    which = jnp.stack([jnp.where(diagonal, gen_index, -1)] + [gen_index ^ k for k in range(gen_count)])
    shares = combine(which, inverse_factor, turns, vec_dev)
    result = shares[0]
    for k in others:
        result += move(shares[k], lambda g, j, c, k=k: (g ^ k, j, c) if g == j else None)
    return result


def solution(mesh):
    in_specs = (P(None, "gen", "fit"), P(), P("gen", "fit"), P("fit", "gen"))
    out_specs = P("gen", "fit")
    return jax.shard_map(
        on_device, mesh=mesh, in_specs=in_specs, out_specs=out_specs, check_vma=False
    )
```

```python
import functools

import jax
import jax.numpy as jnp
from jax import lax
from jax.experimental import pallas as pl
from jax.experimental.pallas import tpu as pltpu
from jax.sharding import PartitionSpec as P

NORB = 2000
F32 = jnp.float32
BF16 = jnp.bfloat16
BOTH = ("gen", "fit")
HIGHEST = lax.Precision.HIGHEST


def mover(gen_count):
    fit_count = 2 * gen_count

    def move(value, target):
        pairs = []
        for g in range(gen_count):
            for j in range(gen_count):
                for c in range(2):
                    to = target(g, j, c)
                    if to is not None:
                        pairs.append(
                            (g * fit_count + 2 * j + c, to[0] * fit_count + 2 * to[1] + to[2])
                        )
        return lax.ppermute(value, BOTH, pairs)

    return move


def split_hi_lo(x):
    hi = lax.reduce_precision(x, 8, 7)
    return hi.astype(BF16), (x - hi).astype(BF16)


def pivot_kernel(row_ref, own_ref, sib_ref, own_col_ref, sib_col_ref, out_ref, buffer, sems):
    count, orb = out_ref.shape[1], own_ref.shape[0]
    copies = []
    for i in range(count):
        row = jnp.clip(row_ref[i], 0, orb - 1)
        for n, ref in enumerate((own_ref, sib_ref)):
            copies.append(
                pltpu.make_async_copy(ref.at[row], buffer.at[2 * i + n], sems.at[2 * i + n])
            )
            copies[-1].start()
    lane = lax.broadcasted_iota(jnp.int32, buffer.shape[1:], 1)
    for i in range(count):
        copies[2 * i].wait()
        copies[2 * i + 1].wait()
        local = jnp.logical_and(row_ref[i] >= 0, row_ref[i] < orb)
        kept = jnp.where(lane == own_col_ref[i], buffer[2 * i].astype(F32), 0.0)
        kept += jnp.where(lane == sib_col_ref[i], buffer[2 * i + 1].astype(F32), 0.0)
        kept = jnp.where(local, kept, 0.0)
        out_ref[:, i : i + 1] = jnp.sum(kept, axis=1, keepdims=True)


def pivot_entries(own, sib, rows, own_cols, sib_cols):
    vec_total, pair = own.shape[1:]
    return pl.pallas_call(
        pivot_kernel,
        in_specs=[
            pl.BlockSpec(memory_space=pltpu.SMEM),
            pl.BlockSpec(memory_space=pltpu.HBM),
            pl.BlockSpec(memory_space=pltpu.HBM),
            pl.BlockSpec(memory_space=pltpu.SMEM),
            pl.BlockSpec(memory_space=pltpu.SMEM),
        ],
        out_specs=pl.BlockSpec(memory_space=pltpu.VMEM),
        out_shape=jax.ShapeDtypeStruct((vec_total, vec_total), F32),
        scratch_shapes=[
            pltpu.VMEM((2 * vec_total, vec_total, pair), BF16),
            pltpu.SemaphoreType.DMA((2 * vec_total,)),
        ],
        name="pivot_entries",
    )(rows, own, sib, own_cols, sib_cols)


def factor_inverse_kernel(block_ref, out_ref):
    n = block_ref.shape[0]
    a = block_ref[:, block_ref.shape[1] - 128 :][:, :n]
    row = lax.broadcasted_iota(jnp.int32, (n, n), 0)
    col = lax.broadcasted_iota(jnp.int32, (n, n), 1)
    w = (row == col).astype(F32)
    for i in range(n):
        pivot = a[i : i + 1, i : i + 1]
        scale = jnp.where(row[:, :1] > i, a[:, i : i + 1] / pivot, 0.0)
        w = w - scale * w[i : i + 1, :]
        a = a - scale * a[i : i + 1, :]
    diag = jnp.sum(jnp.where(row == col, a, 0.0), axis=1, keepdims=True)
    out_ref[...] = w / jnp.sqrt(diag)


def factor_inverse(block):
    return pl.pallas_call(
        factor_inverse_kernel,
        out_shape=jax.ShapeDtypeStruct((block.shape[0], block.shape[0]), F32),
        name="factor_inverse",
    )(block)


def project_kernel(vec_total, chunk, cp_counts, cq_count, where_ref, own_ref, sib_ref, entries_ref, *rest):
    blocks = len(cp_counts)
    cp_refs, rest = rest[: sum(cp_counts)], rest[sum(cp_counts) :]
    cq_refs, rest = rest[: blocks * cq_count], rest[blocks * cq_count :]
    out_refs, (cq, cp, acc) = rest[:blocks], rest[blocks:]
    points = cp.shape[2]
    step = pl.program_id(0)
    core = where_ref[0]

    @pl.when(step == 0)
    def _():
        for b in range(blocks):
            for n in range(cq_count):
                ref = cq_refs[b * cq_count + n]
                part = ref.shape[-1]
                start = 0
                if cq_count > 1:
                    start = pl.multiple_of(where_ref[1 + n] * part, part)
                cq[b, :, :, pl.ds(start, part)] = ref[0]
            start = 0
            for ref in cp_refs[sum(cp_counts[:b]) : sum(cp_counts[: b + 1])]:
                cp[b, :, start : start + ref.shape[1]] = ref[...].astype(F32)
                start += ref.shape[1]
            out_ref = out_refs[b]
            out_ref[:, points:] = jnp.zeros((vec_total, out_ref.shape[1] - points), F32)
            out_ref[:, points : points + vec_total] = entries_ref[...]
        acc[...] = jnp.zeros_like(acc)

    for b in range(blocks):
        mixed = jnp.dot(own_ref[...], cq[b, core], preferred_element_type=F32)
        mixed += jnp.dot(sib_ref[...], cq[b, 1 - core], preferred_element_type=F32)
        total = acc[b]
        for p in range(chunk):
            row = cp[b, pl.ds(step * chunk + p, 1), :]
            total += mixed[p * vec_total : (p + 1) * vec_total] * row
        acc[b] = total

    @pl.when(step == pl.num_programs(0) - 1)
    def _():
        for b in range(blocks):
            out_refs[b][:, :points] = acc[b]


def project(where, own, sib, entries, first, second, slots):
    orb = first[0][0].shape[0]
    points = sum(x.shape[1] for x in first[0])
    pair = own.shape[1]
    vec_total = own.shape[0] // orb
    chunk = 125
    blocks = len(first)
    whole = lambda i, s: (0, 0)
    specs, arrays = [], []
    for parts in first:
        for x in parts:
            specs.append(pl.BlockSpec(x.shape, whole))
            arrays.append(x)
    for parts, slot in zip(second, slots):
        for x in parts:
            specs.append(
                pl.BlockSpec((1,) + x.shape[1:], lambda i, s, slot=slot: (slot, 0, 0, 0))
            )
            arrays.append(x)
    kernel = functools.partial(
        project_kernel, vec_total, chunk, tuple(len(x) for x in first), len(second[0])
    )
    return pl.pallas_call(
        kernel,
        grid_spec=pltpu.PrefetchScalarGridSpec(
            num_scalar_prefetch=1,
            grid=(orb // chunk,),
            in_specs=[
                pl.BlockSpec((chunk * vec_total, pair), lambda i, s: (i, 0)),
                pl.BlockSpec((chunk * vec_total, pair), lambda i, s: (i, 0)),
                pl.BlockSpec((vec_total, vec_total), whole),
            ]
            + specs,
            out_specs=[pl.BlockSpec((vec_total, points + 128), whole)] * blocks,
            scratch_shapes=[
                pltpu.VMEM((blocks, 2, pair, points), BF16),
                pltpu.VMEM((blocks, orb, points), F32),
                pltpu.VMEM((blocks, vec_total, points), F32),
            ],
        ),
        out_shape=[jax.ShapeDtypeStruct((vec_total, points + 128), F32)] * blocks,
        compiler_params=pltpu.CompilerParams(vmem_limit_bytes=32 << 20),
        cost_estimate=pl.CostEstimate(
            flops=4 * orb * vec_total * pair * points * blocks,
            transcendentals=0,
            bytes_accessed=1 << 20,
        ),
        name="project",
    )(where, own, sib, entries, *arrays)


def invert_kernel(where_ref, block_ref, out_ref):
    n = block_ref.shape[0]
    tile = 128
    row = lax.broadcasted_iota(jnp.int32, (tile, tile), 0)
    col = lax.broadcasted_iota(jnp.int32, (tile, tile), 1)
    eye = (row == col).astype(F32)
    dot = functools.partial(jnp.dot, precision=HIGHEST, preferred_element_type=F32)
    holds = where_ref[1] == 1
    places = range(0, n, tile)
    parts = [jnp.where(holds, block_ref[b : b + tile, b : b + tile], eye) for b in places]
    xs = [eye / jnp.sum(part * eye, axis=1, keepdims=True) for part in parts]
    size = 1
    while size < tile:
        pick = (row // (2 * size) == col // (2 * size)) & (row // size > col // size)
        inner = [dot(jnp.where(pick, part, 0.0), x) for part, x in zip(parts, xs)]
        xs = [x - dot(x, y) for x, y in zip(xs, inner)]
        size *= 2
    out_ref[...] = jnp.zeros_like(out_ref)
    for b, x in zip(places, xs):
        out_ref[b : b + tile, b : b + tile] = x
    size = tile
    while size < n:
        for b in range(0, n, 2 * size):
            mid, end = b + size, b + 2 * size
            inner = dot(block_ref[mid:end, b:mid], out_ref[b:mid, b:mid])
            out_ref[mid:end, b:mid] = -dot(out_ref[mid:end, mid:end], inner)
        size *= 2


def invert_block(where, metric):
    n = metric.shape[0]
    return pl.pallas_call(
        invert_kernel,
        grid_spec=pltpu.PrefetchScalarGridSpec(
            num_scalar_prefetch=1,
            grid=(1,),
            in_specs=[pl.BlockSpec((n, n), lambda i, s: (0, s[0]))],
            out_specs=pl.BlockSpec((n, n), lambda i, s: (0, 0)),
        ),
        out_shape=jax.ShapeDtypeStruct((n, n), F32),
        compiler_params=pltpu.CompilerParams(vmem_limit_bytes=16 << 20),
        cost_estimate=pl.CostEstimate(flops=4 << 30, transcendentals=0, bytes_accessed=1 << 22),
        name="invert_block",
    )(where, metric)


def weigh(hi_ref, lo_ref, halves):
    dims = (((1,), (1,)), ((), ()))
    total = None
    for half, x in halves:
        hi = x.astype(BF16)
        lo = (x - hi.astype(F32)).astype(BF16)
        n = x.shape[0]
        width = x.shape[1]
        columns = pl.ds(pl.multiple_of(half * width, width), width)
        both = lax.dot_general(
            jnp.concatenate([hi, lo]), hi_ref[:, columns], dims, preferred_element_type=F32
        )
        part = both[:n] + both[n:]
        if lo_ref is not None:
            part += lax.dot_general(hi, lo_ref[:, columns], dims, preferred_element_type=F32)
        total = part if total is None else total + part
    return total


def apply_kernel(where_ref, *refs):
    weights, (xa_ref, xb_ref, out_ref) = refs[:-3], refs[-3:]
    core = where_ref[0]
    hi_ref, lo_ref = weights if len(weights) == 2 else (weights[0], None)
    points = out_ref.shape[1]
    halves = [(core, xa_ref[:, :points]), (1 - core, xb_ref[:, :points])]
    out_ref[...] = weigh(hi_ref, lo_ref, halves)


def apply_weights(where, weights, xa, xb):
    return pl.pallas_call(
        apply_kernel,
        in_specs=[pl.BlockSpec(memory_space=pltpu.SMEM)]
        + [pl.BlockSpec(memory_space=pltpu.VMEM)] * (len(weights) + 2),
        out_specs=pl.BlockSpec(memory_space=pltpu.VMEM),
        out_shape=jax.ShapeDtypeStruct((xa.shape[0], weights[0].shape[0]), F32),
        compiler_params=pltpu.CompilerParams(vmem_limit_bytes=12 << 20),
        cost_estimate=pl.CostEstimate(flops=1 << 30, transcendentals=0, bytes_accessed=1 << 21),
        name="apply_weights",
    )(where, *weights, xa, xb)


def turn_kernel(count, where_ref, *refs):
    weights, refs = refs[: 2 * count + 2], refs[2 * count + 2 :]
    xa, xb, own_rest, sib_rest, out_ref, buffer, sems = refs
    core = where_ref[0]
    copies = [
        pltpu.make_async_copy(ref, buffer.at[i], sems.at[i]) for i, ref in enumerate(weights)
    ]
    for copy in copies:
        copy.start()
    points = xa.shape[1]
    n = own_rest.shape[0]
    own, sib = own_rest[:, :points], sib_rest[:, :points]
    for i in range(count):
        halves = [(core, xa[i * n : (i + 1) * n]), (1 - core, xb[i * n : (i + 1) * n])]
        copies[2 * i].wait()
        own -= weigh(buffer.at[2 * i], None, halves)
        copies[2 * i + 1].wait()
        sib -= weigh(buffer.at[2 * i + 1], None, halves)
    copies[-2].wait()
    copies[-1].wait()
    solved = weigh(
        buffer.at[2 * count], buffer.at[2 * count + 1], [(core, own), (1 - core, sib)]
    )
    if out_ref.shape[0] > n:
        out_ref[: count * n] = xa[...]
    out_ref[out_ref.shape[0] - n :] = solved


def turn(where, lefts, inverse, xa, xb, own_rest, sib_rest, keep):
    vmem = pl.BlockSpec(memory_space=pltpu.VMEM)
    weights = [*lefts, *inverse]
    n, points = own_rest.shape[0], xa.shape[1]
    count = len(lefts) // 2
    return pl.pallas_call(
        functools.partial(turn_kernel, count),
        in_specs=[pl.BlockSpec(memory_space=pltpu.SMEM)]
        + [pl.BlockSpec(memory_space=pl.ANY)] * len(weights)
        + [vmem] * 4,
        out_specs=vmem,
        out_shape=jax.ShapeDtypeStruct(((count + 1) * n if keep else n, points), F32),
        scratch_shapes=[
            pltpu.VMEM((len(weights),) + weights[0].shape, BF16),
            pltpu.SemaphoreType.DMA((len(weights),)),
        ],
        compiler_params=pltpu.CompilerParams(vmem_limit_bytes=32 << 20),
        cost_estimate=pl.CostEstimate(flops=1 << 20, transcendentals=0, bytes_accessed=1 << 16),
        name="turn",
    )(where, *weights, xa, xb, own_rest, sib_rest)


def combine_kernel(count, turn_ref, inverse_ref, *refs):
    x_refs, out_refs = refs[:count], refs[count:]
    x = jnp.zeros(x_refs[0].shape, F32)
    for t, ref in enumerate(x_refs):
        x = jnp.where(turn_ref[0] == t, ref[ref.shape[0] - x.shape[0] :], x)
    rows = out_refs[0].shape[0]
    for k, ref in enumerate(out_refs):
        inverse = inverse_ref[pl.ds(turn_ref[1 + k] * rows, rows), :]
        total = inverse[:, :1] * x[:1]
        for i in range(1, x.shape[0]):
            total += inverse[:, i : i + 1] * x[i : i + 1]
        ref[...] = total


def combine(which, inverse, turns, rows):
    count = len(turns)
    share = jax.ShapeDtypeStruct((rows, turns[0].shape[1]), F32)
    return pl.pallas_call(
        functools.partial(combine_kernel, count),
        in_specs=[pl.BlockSpec(memory_space=pltpu.SMEM)]
        + [pl.BlockSpec(memory_space=pltpu.VMEM)] * (count + 1),
        out_shape=[share] * count,
        name="combine",
    )(which, inverse, *turns)


def on_device(raw_columns, pivot_pairs, collocation, metric_factor):
    vec_total, orb_block, pair_block = raw_columns.shape
    gen_count = lax.axis_size("gen")
    gen_index = lax.axis_index("gen")
    fit_index = lax.axis_index("fit")
    chip = fit_index // 2
    core = fit_index % 2
    points = metric_factor.shape[0]
    vec_dev = vec_total // gen_count
    move = mover(gen_count)
    others = range(1, gen_count)
    diagonal = gen_index == chip
    swap = lambda g, j, c: (g, j, 1 - c)

    part = points // gen_count
    across = lambda k: lambda g, j, c: (g, j ^ k, c)
    halves = collocation.reshape(2, orb_block // 2, points)
    spread = []
    for k in range(gen_count):
        piece = lax.dynamic_slice_in_dim(halves, (gen_index ^ k) * part, part, 2)
        spread.append(move(piece, lambda g, j, c, k=k: (g ^ k, j, c)) if k else piece)
    spread = jnp.stack(spread)
    early, half = 2, points // 2
    sibling = move(raw_columns, swap)
    early_parts = [move(collocation[:, :half], across(early))]
    second_half = collocation[:, half:]
    spread, sibling, early_parts, second_half, metric_late = lax.optimization_barrier(
        (spread, sibling, early_parts, second_half, metric_factor)
    )
    early_parts.append(move(second_half, across(early)))
    own_rows = metric_late.astype(BF16)
    left_own = move(own_rows, lambda g, j, c: (g + 1, j, c) if j == g + 1 else None)
    own_parts = []
    for k in range(gen_count):
        piece = lax.dynamic_index_in_dim(spread, gen_index ^ chip ^ k, 0, keepdims=False)
        own_parts.append(move(piece, across(k)) if k else piece)
    own_raw = raw_columns.transpose(1, 0, 2)
    sib_raw = sibling.transpose(1, 0, 2)
    pivot_rows = pivot_pairs // NORB - gen_index * orb_block
    own_cols = pivot_pairs % NORB - fit_index * pair_block
    sib_cols = pivot_pairs % NORB - (fit_index ^ 1) * pair_block
    entries = pivot_entries(own_raw, sib_raw, pivot_rows, own_cols, sib_cols)

    own_inverse = invert_block(jnp.stack([core, diagonal.astype(jnp.int32)]), metric_late)
    own_parts, first, early_parts, left_own, own_inverse, entries = lax.optimization_barrier(
        (own_parts, collocation, early_parts, left_own, own_inverse, entries)
    )
    upper = move(own_inverse, swap)
    first_side = {0: [collocation], early: early_parts}
    for k in others:
        if k != early:
            first_side[k] = [move(first, across(k))]
    all_parts = [jnp.stack(own_parts)]
    for k in others:
        all_parts.append(move(all_parts[0], lambda g, j, c, k=k: (g ^ k, j, c)))

    def second_side(k):
        if part % 128 == 0:
            return all_parts
        whole = jnp.zeros(halves.shape, BF16)
        for n, x in enumerate(all_parts):
            whole = lax.dynamic_update_slice_in_dim(whole, x[k], (gen_index ^ n) * part, 2)
        return [whole[None]]

    corner = jnp.dot(metric_factor[:, :points], upper, precision=HIGHEST)
    corner = -jnp.dot(own_inverse, corner, precision=HIGHEST)
    inverse_rows = split_hi_lo(
        jnp.concatenate(
            [
                jnp.where(core == 0, own_inverse, corner),
                jnp.where(core == 0, jnp.zeros_like(own_inverse), own_inverse),
            ],
            axis=1,
        )
    )

    all_parts, first_side, entries, inverse_rows, left_rows = lax.optimization_barrier(
        (all_parts, first_side, entries, inverse_rows, own_rows)
    )
    left_own, left_sib = {1: left_own}, {1: move(left_own, swap)}
    for d in range(2, gen_count - 1):
        left_own[d] = move(left_rows, lambda g, j, c: (j, j, c) if g >= 1 and j == g + d else None)

    own_raw = own_raw.reshape(orb_block * vec_total, pair_block)
    sib_raw = sib_raw.reshape(orb_block * vec_total, pair_block)
    where = jnp.stack([core] + [gen_index ^ k for k in range(gen_count)])
    total = None
    for group in [list(range(i, min(i + 4, gen_count))) for i in range(0, gen_count, 4)]:
        shares = project(
            where,
            own_raw,
            sib_raw,
            entries,
            [first_side[k] for k in group],
            [second_side(k) for k in group],
            [k if part % 128 == 0 else 0 for k in group],
        )
        if group[0] == 0:
            shares, left_sib[1] = lax.optimization_barrier((shares, left_sib[1]))
        for k, share in zip(group, shares):
            if k:
                share = move(share, across(k))
            total = share if total is None else total + share
    total = sum([move(total, lambda g, j, c, k=k: (g ^ k, j, c)) for k in others], total)

    at_core = core[None]
    inverse_factor = factor_inverse(total)
    rest, sib_rest = total, move(total, swap)
    solved = apply_weights(at_core, inverse_rows, rest, sib_rest)
    turns = [solved]
    for t in range(1, gen_count):
        near = move(solved, lambda g, j, c: (t, t, c) if g == j == t - 1 else None)
        near_sib = move(solved, lambda g, j, c: (t, t, 1 - c) if g == j == t - 1 else None)
        if t == 1 and gen_count > 2:
            far = [
                move(solved, lambda g, j, c: (0, z, c) if g == j == 0 else None)
                for z in range(2, gen_count)
            ]
            near, near_sib, far = lax.optimization_barrier((near, near_sib, far))
        if t == 2:
            far = sum(far[1:], far[0])
            acted = apply_weights(at_core, [own_rows], far, move(far, swap))
            brought = move(acted, lambda g, j, c: (j, j, c) if g == 0 and j >= 2 else None)
            near, near_sib, brought = lax.optimization_barrier((near, near_sib, brought))
            rest = rest[:, :points] - brought
            sib_rest = move(rest, swap)
        if t == gen_count - 1:
            near, inverse_factor = lax.optimization_barrier((near, inverse_factor))
        lefts = []
        for g in range(min(1, t - 1), t):
            lefts += [left_own[t - g], left_sib[t - g]]
        solved = turn(at_core, lefts, inverse_rows, near, near_sib, rest, sib_rest, t > 1)
        turns.append(solved)
        if t == 1:
            for d in range(2, gen_count - 1):
                _, left_own[d] = lax.optimization_barrier((solved, left_own[d]))
                left_sib[d] = move(left_own[d], swap)

    which = jnp.stack([jnp.where(diagonal, gen_index, -1)] + [gen_index ^ k for k in range(gen_count)])
    shares = combine(which, inverse_factor, turns, vec_dev)
    result = shares[0]
    for k in others:
        result += move(shares[k], lambda g, j, c, k=k: (g ^ k, j, c) if g == j else None)
    return result


def solution(mesh):
    in_specs = (P(None, "gen", "fit"), P(), P("gen", "fit"), P("fit", "gen"))
    out_specs = P("gen", "fit")
    return jax.shard_map(
        on_device, mesh=mesh, in_specs=in_specs, out_specs=out_specs, check_vma=False
    )
```

```python
import functools

import jax
import jax.numpy as jnp
from jax import lax
from jax.experimental import pallas as pl
from jax.experimental.pallas import tpu as pltpu
from jax.sharding import PartitionSpec as P

NORB = 2000
F32 = jnp.float32
BF16 = jnp.bfloat16
BOTH = ("gen", "fit")
HIGHEST = lax.Precision.HIGHEST


def mover(gen_count):
    fit_count = 2 * gen_count

    def move(value, target):
        pairs = []
        for g in range(gen_count):
            for j in range(gen_count):
                for c in range(2):
                    to = target(g, j, c)
                    if to is not None:
                        pairs.append(
                            (g * fit_count + 2 * j + c, to[0] * fit_count + 2 * to[1] + to[2])
                        )
        return lax.ppermute(value, BOTH, pairs)

    return move


def split_hi_lo(x):
    hi = lax.reduce_precision(x, 8, 7)
    return hi.astype(BF16), (x - hi).astype(BF16)


def pivot_kernel(row_ref, own_ref, sib_ref, own_col_ref, sib_col_ref, out_ref, buffer, sems):
    count, orb = out_ref.shape[1], own_ref.shape[0]
    copies = []
    for i in range(count):
        row = jnp.clip(row_ref[i], 0, orb - 1)
        for n, ref in enumerate((own_ref, sib_ref)):
            copies.append(
                pltpu.make_async_copy(ref.at[row], buffer.at[2 * i + n], sems.at[2 * i + n])
            )
            copies[-1].start()
    lane = lax.broadcasted_iota(jnp.int32, buffer.shape[1:], 1)
    for i in range(count):
        copies[2 * i].wait()
        copies[2 * i + 1].wait()
        local = jnp.logical_and(row_ref[i] >= 0, row_ref[i] < orb)
        kept = jnp.where(lane == own_col_ref[i], buffer[2 * i].astype(F32), 0.0)
        kept += jnp.where(lane == sib_col_ref[i], buffer[2 * i + 1].astype(F32), 0.0)
        kept = jnp.where(local, kept, 0.0)
        out_ref[:, i : i + 1] = jnp.sum(kept, axis=1, keepdims=True)


def pivot_entries(own, sib, rows, own_cols, sib_cols):
    vec_total, pair = own.shape[1:]
    return pl.pallas_call(
        pivot_kernel,
        in_specs=[
            pl.BlockSpec(memory_space=pltpu.SMEM),
            pl.BlockSpec(memory_space=pltpu.HBM),
            pl.BlockSpec(memory_space=pltpu.HBM),
            pl.BlockSpec(memory_space=pltpu.SMEM),
            pl.BlockSpec(memory_space=pltpu.SMEM),
        ],
        out_specs=pl.BlockSpec(memory_space=pltpu.VMEM),
        out_shape=jax.ShapeDtypeStruct((vec_total, vec_total), F32),
        scratch_shapes=[
            pltpu.VMEM((2 * vec_total, vec_total, pair), BF16),
            pltpu.SemaphoreType.DMA((2 * vec_total,)),
        ],
        name="pivot_entries",
    )(rows, own, sib, own_cols, sib_cols)


def factor_inverse_kernel(block_ref, out_ref):
    n = block_ref.shape[0]
    a = block_ref[:, block_ref.shape[1] - 128 :][:, :n]
    row = lax.broadcasted_iota(jnp.int32, (n, n), 0)
    col = lax.broadcasted_iota(jnp.int32, (n, n), 1)
    w = (row == col).astype(F32)
    for i in range(n):
        pivot = a[i : i + 1, i : i + 1]
        scale = jnp.where(row[:, :1] > i, a[:, i : i + 1] / pivot, 0.0)
        w = w - scale * w[i : i + 1, :]
        a = a - scale * a[i : i + 1, :]
    diag = jnp.sum(jnp.where(row == col, a, 0.0), axis=1, keepdims=True)
    out_ref[...] = w / jnp.sqrt(diag)


def factor_inverse(block):
    return pl.pallas_call(
        factor_inverse_kernel,
        out_shape=jax.ShapeDtypeStruct((block.shape[0], block.shape[0]), F32),
        name="factor_inverse",
    )(block)


def project_kernel(vec_total, chunk, cp_counts, cq_count, where_ref, own_ref, sib_ref, entries_ref, *rest):
    blocks = len(cp_counts)
    cp_refs, rest = rest[: sum(cp_counts)], rest[sum(cp_counts) :]
    cq_refs, rest = rest[: blocks * cq_count], rest[blocks * cq_count :]
    out_refs, (cq, cp, acc) = rest[:blocks], rest[blocks:]
    points = cp.shape[2]
    step = pl.program_id(0)
    core = where_ref[0]

    @pl.when(step == 0)
    def _():
        for b in range(blocks):
            for n in range(cq_count):
                ref = cq_refs[b * cq_count + n]
                part = ref.shape[-1]
                start = 0
                if cq_count > 1:
                    start = pl.multiple_of(where_ref[1 + n] * part, part)
                cq[b, :, :, pl.ds(start, part)] = ref[0]
            start = 0
            for ref in cp_refs[sum(cp_counts[:b]) : sum(cp_counts[: b + 1])]:
                cp[b, :, start : start + ref.shape[1]] = ref[...].astype(F32)
                start += ref.shape[1]
            out_ref = out_refs[b]
            out_ref[:, points:] = jnp.zeros((vec_total, out_ref.shape[1] - points), F32)
            out_ref[:, points : points + vec_total] = entries_ref[...]
        acc[...] = jnp.zeros_like(acc)

    for b in range(blocks):
        mixed = jnp.dot(own_ref[...], cq[b, core], preferred_element_type=F32)
        mixed += jnp.dot(sib_ref[...], cq[b, 1 - core], preferred_element_type=F32)
        total = acc[b]
        for p in range(chunk):
            row = cp[b, pl.ds(step * chunk + p, 1), :]
            total += mixed[p * vec_total : (p + 1) * vec_total] * row
        acc[b] = total

    @pl.when(step == pl.num_programs(0) - 1)
    def _():
        for b in range(blocks):
            out_refs[b][:, :points] = acc[b]


def project(where, own, sib, entries, first, second, slots):
    orb = first[0][0].shape[0]
    points = sum(x.shape[1] for x in first[0])
    pair = own.shape[1]
    vec_total = own.shape[0] // orb
    chunk = 125
    blocks = len(first)
    whole = lambda i, s: (0, 0)
    specs, arrays = [], []
    for parts in first:
        for x in parts:
            specs.append(pl.BlockSpec(x.shape, whole))
            arrays.append(x)
    for parts, slot in zip(second, slots):
        for x in parts:
            specs.append(
                pl.BlockSpec((1,) + x.shape[1:], lambda i, s, slot=slot: (slot, 0, 0, 0))
            )
            arrays.append(x)
    kernel = functools.partial(
        project_kernel, vec_total, chunk, tuple(len(x) for x in first), len(second[0])
    )
    return pl.pallas_call(
        kernel,
        grid_spec=pltpu.PrefetchScalarGridSpec(
            num_scalar_prefetch=1,
            grid=(orb // chunk,),
            in_specs=[
                pl.BlockSpec((chunk * vec_total, pair), lambda i, s: (i, 0)),
                pl.BlockSpec((chunk * vec_total, pair), lambda i, s: (i, 0)),
                pl.BlockSpec((vec_total, vec_total), whole),
            ]
            + specs,
            out_specs=[pl.BlockSpec((vec_total, points + 128), whole)] * blocks,
            scratch_shapes=[
                pltpu.VMEM((blocks, 2, pair, points), BF16),
                pltpu.VMEM((blocks, orb, points), F32),
                pltpu.VMEM((blocks, vec_total, points), F32),
            ],
        ),
        out_shape=[jax.ShapeDtypeStruct((vec_total, points + 128), F32)] * blocks,
        compiler_params=pltpu.CompilerParams(vmem_limit_bytes=32 << 20),
        cost_estimate=pl.CostEstimate(
            flops=4 * orb * vec_total * pair * points * blocks,
            transcendentals=0,
            bytes_accessed=1 << 20,
        ),
        name="project",
    )(where, own, sib, entries, *arrays)


def invert_kernel(where_ref, block_ref, out_ref):
    n = block_ref.shape[0]
    tile = 128
    row = lax.broadcasted_iota(jnp.int32, (tile, tile), 0)
    col = lax.broadcasted_iota(jnp.int32, (tile, tile), 1)
    eye = (row == col).astype(F32)
    dot = functools.partial(jnp.dot, precision=HIGHEST, preferred_element_type=F32)
    holds = where_ref[1] == 1
    places = range(0, n, tile)
    parts = [jnp.where(holds, block_ref[b : b + tile, b : b + tile], eye) for b in places]
    xs = [eye / jnp.sum(part * eye, axis=1, keepdims=True) for part in parts]
    size = 1
    while size < tile:
        pick = (row // (2 * size) == col // (2 * size)) & (row // size > col // size)
        inner = [dot(jnp.where(pick, part, 0.0), x) for part, x in zip(parts, xs)]
        xs = [x - dot(x, y) for x, y in zip(xs, inner)]
        size *= 2
    out_ref[...] = jnp.zeros_like(out_ref)
    for b, x in zip(places, xs):
        out_ref[b : b + tile, b : b + tile] = x
    size = tile
    while size < n:
        for b in range(0, n, 2 * size):
            mid, end = b + size, b + 2 * size
            inner = dot(block_ref[mid:end, b:mid], out_ref[b:mid, b:mid])
            out_ref[mid:end, b:mid] = -dot(out_ref[mid:end, mid:end], inner)
        size *= 2


def invert_block(where, metric):
    n = metric.shape[0]
    return pl.pallas_call(
        invert_kernel,
        grid_spec=pltpu.PrefetchScalarGridSpec(
            num_scalar_prefetch=1,
            grid=(1,),
            in_specs=[pl.BlockSpec((n, n), lambda i, s: (0, s[0]))],
            out_specs=pl.BlockSpec((n, n), lambda i, s: (0, 0)),
        ),
        out_shape=jax.ShapeDtypeStruct((n, n), F32),
        compiler_params=pltpu.CompilerParams(vmem_limit_bytes=16 << 20),
        cost_estimate=pl.CostEstimate(flops=4 << 30, transcendentals=0, bytes_accessed=1 << 22),
        name="invert_block",
    )(where, metric)


def weigh(hi_ref, lo_ref, halves):
    dims = (((1,), (1,)), ((), ()))
    total = None
    for half, x in halves:
        hi = x.astype(BF16)
        lo = (x - hi.astype(F32)).astype(BF16)
        n = x.shape[0]
        width = x.shape[1]
        columns = pl.ds(pl.multiple_of(half * width, width), width)
        both = lax.dot_general(
            jnp.concatenate([hi, lo]), hi_ref[:, columns], dims, preferred_element_type=F32
        )
        part = both[:n] + both[n:]
        if lo_ref is not None:
            part += lax.dot_general(hi, lo_ref[:, columns], dims, preferred_element_type=F32)
        total = part if total is None else total + part
    return total


def apply_kernel(where_ref, *refs):
    weights, (xa_ref, xb_ref, out_ref) = refs[:-3], refs[-3:]
    core = where_ref[0]
    hi_ref, lo_ref = weights if len(weights) == 2 else (weights[0], None)
    points = out_ref.shape[1]
    halves = [(core, xa_ref[:, :points]), (1 - core, xb_ref[:, :points])]
    out_ref[...] = weigh(hi_ref, lo_ref, halves)


def apply_weights(where, weights, xa, xb):
    return pl.pallas_call(
        apply_kernel,
        in_specs=[pl.BlockSpec(memory_space=pltpu.SMEM)]
        + [pl.BlockSpec(memory_space=pltpu.VMEM)] * (len(weights) + 2),
        out_specs=pl.BlockSpec(memory_space=pltpu.VMEM),
        out_shape=jax.ShapeDtypeStruct((xa.shape[0], weights[0].shape[0]), F32),
        compiler_params=pltpu.CompilerParams(vmem_limit_bytes=12 << 20),
        cost_estimate=pl.CostEstimate(flops=1 << 30, transcendentals=0, bytes_accessed=1 << 21),
        name="apply_weights",
    )(where, *weights, xa, xb)


def turn_kernel(count, where_ref, *refs):
    weights, refs = refs[: 2 * count + 2], refs[2 * count + 2 :]
    xa, xb, own_rest, sib_rest, out_ref, buffer, sems = refs
    core = where_ref[0]
    copies = [
        pltpu.make_async_copy(ref, buffer.at[i], sems.at[i]) for i, ref in enumerate(weights)
    ]
    for copy in copies:
        copy.start()
    points = xa.shape[1]
    n = own_rest.shape[0]
    own, sib = own_rest[:, :points], sib_rest[:, :points]
    for i in range(count):
        halves = [(core, xa[i * n : (i + 1) * n]), (1 - core, xb[i * n : (i + 1) * n])]
        copies[2 * i].wait()
        own -= weigh(buffer.at[2 * i], None, halves)
        copies[2 * i + 1].wait()
        sib -= weigh(buffer.at[2 * i + 1], None, halves)
    copies[-2].wait()
    copies[-1].wait()
    solved = weigh(
        buffer.at[2 * count], buffer.at[2 * count + 1], [(core, own), (1 - core, sib)]
    )
    if out_ref.shape[0] > n:
        out_ref[: count * n] = xa[...]
    out_ref[out_ref.shape[0] - n :] = solved


def turn(where, lefts, inverse, xa, xb, own_rest, sib_rest, keep):
    vmem = pl.BlockSpec(memory_space=pltpu.VMEM)
    weights = [*lefts, *inverse]
    n, points = own_rest.shape[0], xa.shape[1]
    count = len(lefts) // 2
    return pl.pallas_call(
        functools.partial(turn_kernel, count),
        in_specs=[pl.BlockSpec(memory_space=pltpu.SMEM)]
        + [pl.BlockSpec(memory_space=pl.ANY)] * len(weights)
        + [vmem] * 4,
        out_specs=vmem,
        out_shape=jax.ShapeDtypeStruct(((count + 1) * n if keep else n, points), F32),
        scratch_shapes=[
            pltpu.VMEM((len(weights),) + weights[0].shape, BF16),
            pltpu.SemaphoreType.DMA((len(weights),)),
        ],
        compiler_params=pltpu.CompilerParams(vmem_limit_bytes=32 << 20),
        cost_estimate=pl.CostEstimate(flops=1 << 20, transcendentals=0, bytes_accessed=1 << 16),
        name="turn",
    )(where, *weights, xa, xb, own_rest, sib_rest)


def combine_kernel(count, turn_ref, inverse_ref, *refs):
    x_refs, out_refs = refs[:count], refs[count:]
    x = jnp.zeros(x_refs[0].shape, F32)
    for t, ref in enumerate(x_refs):
        x = jnp.where(turn_ref[0] == t, ref[ref.shape[0] - x.shape[0] :], x)
    rows = out_refs[0].shape[0]
    for k, ref in enumerate(out_refs):
        inverse = inverse_ref[pl.ds(turn_ref[1 + k] * rows, rows), :]
        total = inverse[:, :1] * x[:1]
        for i in range(1, x.shape[0]):
            total += inverse[:, i : i + 1] * x[i : i + 1]
        ref[...] = total


def combine(which, inverse, turns, rows):
    count = len(turns)
    share = jax.ShapeDtypeStruct((rows, turns[0].shape[1]), F32)
    return pl.pallas_call(
        functools.partial(combine_kernel, count),
        in_specs=[pl.BlockSpec(memory_space=pltpu.SMEM)]
        + [pl.BlockSpec(memory_space=pltpu.VMEM)] * (count + 1),
        out_shape=[share] * count,
        name="combine",
    )(which, inverse, *turns)


def on_device(raw_columns, pivot_pairs, collocation, metric_factor):
    vec_total, orb_block, pair_block = raw_columns.shape
    gen_count = lax.axis_size("gen")
    gen_index = lax.axis_index("gen")
    fit_index = lax.axis_index("fit")
    chip = fit_index // 2
    core = fit_index % 2
    points = metric_factor.shape[0]
    vec_dev = vec_total // gen_count
    move = mover(gen_count)
    others = range(1, gen_count)
    diagonal = gen_index == chip
    swap = lambda g, j, c: (g, j, 1 - c)

    part = points // gen_count
    across = lambda k: lambda g, j, c: (g, j ^ k, c)
    halves = collocation.reshape(2, orb_block // 2, points)
    spread = []
    for k in range(gen_count):
        piece = lax.dynamic_slice_in_dim(halves, (gen_index ^ k) * part, part, 2)
        spread.append(move(piece, lambda g, j, c, k=k: (g ^ k, j, c)) if k else piece)
    spread = jnp.stack(spread)
    early, half = 2, points // 2
    sibling = move(raw_columns, swap)
    early_parts = [move(collocation[:, :half], across(early))]
    second_half = collocation[:, half:]
    spread, sibling, early_parts, second_half, metric_late = lax.optimization_barrier(
        (spread, sibling, early_parts, second_half, metric_factor)
    )
    early_parts.append(move(second_half, across(early)))
    own_rows = metric_late.astype(BF16)
    left_own = move(own_rows, lambda g, j, c: (g + 1, j, c) if j == g + 1 else None)
    own_parts = []
    for k in range(gen_count):
        piece = lax.dynamic_index_in_dim(spread, gen_index ^ chip ^ k, 0, keepdims=False)
        own_parts.append(move(piece, across(k)) if k else piece)
    own_raw = raw_columns.transpose(1, 0, 2)
    sib_raw = sibling.transpose(1, 0, 2)
    pivot_rows = pivot_pairs // NORB - gen_index * orb_block
    own_cols = pivot_pairs % NORB - fit_index * pair_block
    sib_cols = pivot_pairs % NORB - (fit_index ^ 1) * pair_block
    entries = pivot_entries(own_raw, sib_raw, pivot_rows, own_cols, sib_cols)

    own_inverse = invert_block(jnp.stack([core, diagonal.astype(jnp.int32)]), metric_late)
    own_parts, first, early_parts, left_own, own_inverse, entries = lax.optimization_barrier(
        (own_parts, collocation, early_parts, left_own, own_inverse, entries)
    )
    upper = move(own_inverse, swap)
    first_side = {0: [collocation], early: early_parts}
    for k in others:
        if k != early:
            first_side[k] = [move(first, across(k))]
    all_parts = [jnp.stack(own_parts)]
    for k in others:
        all_parts.append(move(all_parts[0], lambda g, j, c, k=k: (g ^ k, j, c)))

    def second_side(k):
        if part % 128 == 0:
            return all_parts
        whole = jnp.zeros(halves.shape, BF16)
        for n, x in enumerate(all_parts):
            whole = lax.dynamic_update_slice_in_dim(whole, x[k], (gen_index ^ n) * part, 2)
        return [whole[None]]

    corner = jnp.dot(metric_factor[:, :points], upper, precision=HIGHEST)
    corner = -jnp.dot(own_inverse, corner, precision=HIGHEST)
    inverse_rows = split_hi_lo(
        jnp.concatenate(
            [
                jnp.where(core == 0, own_inverse, corner),
                jnp.where(core == 0, jnp.zeros_like(own_inverse), own_inverse),
            ],
            axis=1,
        )
    )

    all_parts, first_side, entries, inverse_rows, left_rows = lax.optimization_barrier(
        (all_parts, first_side, entries, inverse_rows, own_rows)
    )
    left_own, left_sib = {1: left_own}, {1: move(left_own, swap)}
    for d in range(2, gen_count - 1):
        left_own[d] = move(left_rows, lambda g, j, c: (j, j, c) if g >= 1 and j == g + d else None)

    own_raw = own_raw.reshape(orb_block * vec_total, pair_block)
    sib_raw = sib_raw.reshape(orb_block * vec_total, pair_block)
    where = jnp.stack([core] + [gen_index ^ k for k in range(gen_count)])
    total = None
    for group in [list(range(i, min(i + 4, gen_count))) for i in range(0, gen_count, 4)]:
        shares = project(
            where,
            own_raw,
            sib_raw,
            entries,
            [first_side[k] for k in group],
            [second_side(k) for k in group],
            [k if part % 128 == 0 else 0 for k in group],
        )
        if group[0] == 0:
            shares, left_sib[1] = lax.optimization_barrier((shares, left_sib[1]))
        for k, share in zip(group, shares):
            if k:
                share = move(share, across(k))
            total = share if total is None else total + share
    total = sum([move(total, lambda g, j, c, k=k: (g ^ k, j, c)) for k in others], total)

    at_core = core[None]
    inverse_factor = factor_inverse(total)
    rest, sib_rest = total, move(total, swap)
    solved = apply_weights(at_core, inverse_rows, rest, sib_rest)
    turns = [solved]
    for t in range(1, gen_count):
        near = move(solved, lambda g, j, c: (t, t, c) if g == j == t - 1 else None)
        near_sib = move(solved, lambda g, j, c: (t, t, 1 - c) if g == j == t - 1 else None)
        if t == 1 and gen_count > 2:
            far = [
                move(solved, lambda g, j, c: (0, z, c) if g == j == 0 else None)
                for z in range(2, gen_count)
            ]
            near, near_sib, far = lax.optimization_barrier((near, near_sib, far))
        if t == 2:
            far = sum(far[1:], far[0])
            acted = apply_weights(at_core, [own_rows], far, move(far, swap))
            brought = {
                z: move(acted, lambda g, j, c: (j, j, c) if g == 0 and j == z else None)
                for z in range(2, gen_count)
            }
        if t >= 2:
            if t == 2:
                near, near_sib, brought[t] = lax.optimization_barrier((near, near_sib, brought[t]))
            rest = rest[:, :points] - brought[t]
            sib_rest = move(rest, swap)
        if t == gen_count - 1:
            near, inverse_factor = lax.optimization_barrier((near, inverse_factor))
        lefts = []
        for g in range(min(1, t - 1), t):
            lefts += [left_own[t - g], left_sib[t - g]]
        solved = turn(at_core, lefts, inverse_rows, near, near_sib, rest, sib_rest, t > 1)
        turns.append(solved)
        if t == 1:
            for d in range(2, gen_count - 1):
                _, left_own[d] = lax.optimization_barrier((solved, left_own[d]))
                left_sib[d] = move(left_own[d], swap)

    which = jnp.stack([jnp.where(diagonal, gen_index, -1)] + [gen_index ^ k for k in range(gen_count)])
    shares = combine(which, inverse_factor, turns, vec_dev)
    result = shares[0]
    for k in others:
        result += move(shares[k], lambda g, j, c, k=k: (g ^ k, j, c) if g == j else None)
    return result


def solution(mesh):
    in_specs = (P(None, "gen", "fit"), P(), P("gen", "fit"), P("fit", "gen"))
    out_specs = P("gen", "fit")
    return jax.shard_map(
        on_device, mesh=mesh, in_specs=in_specs, out_specs=out_specs, check_vma=False
    )
```

```python
import functools

import jax
import jax.numpy as jnp
from jax import lax
from jax.experimental import pallas as pl
from jax.experimental.pallas import tpu as pltpu
from jax.sharding import PartitionSpec as P

NORB = 2000
F32 = jnp.float32
BF16 = jnp.bfloat16
BOTH = ("gen", "fit")
HIGHEST = lax.Precision.HIGHEST


def mover(gen_count):
    fit_count = 2 * gen_count

    def move(value, target):
        pairs = []
        for g in range(gen_count):
            for j in range(gen_count):
                for c in range(2):
                    to = target(g, j, c)
                    if to is not None:
                        pairs.append(
                            (g * fit_count + 2 * j + c, to[0] * fit_count + 2 * to[1] + to[2])
                        )
        return lax.ppermute(value, BOTH, pairs)

    return move


def split_hi_lo(x):
    hi = lax.reduce_precision(x, 8, 7)
    return hi.astype(BF16), (x - hi).astype(BF16)


def pivot_kernel(row_ref, own_ref, sib_ref, own_col_ref, sib_col_ref, out_ref, buffer, sems):
    count, orb = out_ref.shape[1], own_ref.shape[0]
    copies = []
    for i in range(count):
        row = jnp.clip(row_ref[i], 0, orb - 1)
        for n, ref in enumerate((own_ref, sib_ref)):
            copies.append(
                pltpu.make_async_copy(ref.at[row], buffer.at[2 * i + n], sems.at[2 * i + n])
            )
            copies[-1].start()
    lane = lax.broadcasted_iota(jnp.int32, buffer.shape[1:], 1)
    for i in range(count):
        copies[2 * i].wait()
        copies[2 * i + 1].wait()
        local = jnp.logical_and(row_ref[i] >= 0, row_ref[i] < orb)
        kept = jnp.where(lane == own_col_ref[i], buffer[2 * i].astype(F32), 0.0)
        kept += jnp.where(lane == sib_col_ref[i], buffer[2 * i + 1].astype(F32), 0.0)
        kept = jnp.where(local, kept, 0.0)
        out_ref[:, i : i + 1] = jnp.sum(kept, axis=1, keepdims=True)


def pivot_entries(own, sib, rows, own_cols, sib_cols):
    vec_total, pair = own.shape[1:]
    return pl.pallas_call(
        pivot_kernel,
        in_specs=[
            pl.BlockSpec(memory_space=pltpu.SMEM),
            pl.BlockSpec(memory_space=pltpu.HBM),
            pl.BlockSpec(memory_space=pltpu.HBM),
            pl.BlockSpec(memory_space=pltpu.SMEM),
            pl.BlockSpec(memory_space=pltpu.SMEM),
        ],
        out_specs=pl.BlockSpec(memory_space=pltpu.VMEM),
        out_shape=jax.ShapeDtypeStruct((vec_total, vec_total), F32),
        scratch_shapes=[
            pltpu.VMEM((2 * vec_total, vec_total, pair), BF16),
            pltpu.SemaphoreType.DMA((2 * vec_total,)),
        ],
        name="pivot_entries",
    )(rows, own, sib, own_cols, sib_cols)


def factor_inverse_kernel(block_ref, out_ref):
    n = block_ref.shape[0]
    a = block_ref[:, block_ref.shape[1] - 128 :][:, :n]
    row = lax.broadcasted_iota(jnp.int32, (n, n), 0)
    col = lax.broadcasted_iota(jnp.int32, (n, n), 1)
    w = (row == col).astype(F32)
    for i in range(n):
        pivot = a[i : i + 1, i : i + 1]
        scale = jnp.where(row[:, :1] > i, a[:, i : i + 1] / pivot, 0.0)
        w = w - scale * w[i : i + 1, :]
        a = a - scale * a[i : i + 1, :]
    diag = jnp.sum(jnp.where(row == col, a, 0.0), axis=1, keepdims=True)
    out_ref[...] = w / jnp.sqrt(diag)


def factor_inverse(block):
    return pl.pallas_call(
        factor_inverse_kernel,
        out_shape=jax.ShapeDtypeStruct((block.shape[0], block.shape[0]), F32),
        name="factor_inverse",
    )(block)


def project_kernel(vec_total, chunk, cp_counts, cq_count, where_ref, own_ref, sib_ref, entries_ref, *rest):
    blocks = len(cp_counts)
    cp_refs, rest = rest[: sum(cp_counts)], rest[sum(cp_counts) :]
    cq_refs, rest = rest[: blocks * cq_count], rest[blocks * cq_count :]
    out_refs, (cq, cp, acc) = rest[:blocks], rest[blocks:]
    points = cp.shape[2]
    step = pl.program_id(0)
    core = where_ref[0]

    @pl.when(step == 0)
    def _():
        for b in range(blocks):
            for n in range(cq_count):
                ref = cq_refs[b * cq_count + n]
                part = ref.shape[-1]
                start = 0
                if cq_count > 1:
                    start = pl.multiple_of(where_ref[1 + n] * part, part)
                cq[b, :, :, pl.ds(start, part)] = ref[0]
            start = 0
            for ref in cp_refs[sum(cp_counts[:b]) : sum(cp_counts[: b + 1])]:
                cp[b, :, start : start + ref.shape[1]] = ref[...].astype(F32)
                start += ref.shape[1]
            out_ref = out_refs[b]
            out_ref[:, points:] = jnp.zeros((vec_total, out_ref.shape[1] - points), F32)
            out_ref[:, points : points + vec_total] = entries_ref[...]
        acc[...] = jnp.zeros_like(acc)

    for b in range(blocks):
        mixed = jnp.dot(own_ref[...], cq[b, core], preferred_element_type=F32)
        mixed += jnp.dot(sib_ref[...], cq[b, 1 - core], preferred_element_type=F32)
        total = acc[b]
        for p in range(chunk):
            row = cp[b, pl.ds(step * chunk + p, 1), :]
            total += mixed[p * vec_total : (p + 1) * vec_total] * row
        acc[b] = total

    @pl.when(step == pl.num_programs(0) - 1)
    def _():
        for b in range(blocks):
            out_refs[b][:, :points] = acc[b]


def project(where, own, sib, entries, first, second, slots):
    orb = first[0][0].shape[0]
    points = sum(x.shape[1] for x in first[0])
    pair = own.shape[1]
    vec_total = own.shape[0] // orb
    chunk = 125
    blocks = len(first)
    whole = lambda i, s: (0, 0)
    specs, arrays = [], []
    for parts in first:
        for x in parts:
            specs.append(pl.BlockSpec(x.shape, whole))
            arrays.append(x)
    for parts, slot in zip(second, slots):
        for x in parts:
            specs.append(
                pl.BlockSpec((1,) + x.shape[1:], lambda i, s, slot=slot: (slot, 0, 0, 0))
            )
            arrays.append(x)
    kernel = functools.partial(
        project_kernel, vec_total, chunk, tuple(len(x) for x in first), len(second[0])
    )
    return pl.pallas_call(
        kernel,
        grid_spec=pltpu.PrefetchScalarGridSpec(
            num_scalar_prefetch=1,
            grid=(orb // chunk,),
            in_specs=[
                pl.BlockSpec((chunk * vec_total, pair), lambda i, s: (i, 0)),
                pl.BlockSpec((chunk * vec_total, pair), lambda i, s: (i, 0)),
                pl.BlockSpec((vec_total, vec_total), whole),
            ]
            + specs,
            out_specs=[pl.BlockSpec((vec_total, points + 128), whole)] * blocks,
            scratch_shapes=[
                pltpu.VMEM((blocks, 2, pair, points), BF16),
                pltpu.VMEM((blocks, orb, points), F32),
                pltpu.VMEM((blocks, vec_total, points), F32),
            ],
        ),
        out_shape=[jax.ShapeDtypeStruct((vec_total, points + 128), F32)] * blocks,
        compiler_params=pltpu.CompilerParams(vmem_limit_bytes=32 << 20),
        cost_estimate=pl.CostEstimate(
            flops=4 * orb * vec_total * pair * points * blocks,
            transcendentals=0,
            bytes_accessed=1 << 20,
        ),
        name="project",
    )(where, own, sib, entries, *arrays)


def invert_kernel(where_ref, block_ref, out_ref):
    n = block_ref.shape[0]
    tile = 128
    row = lax.broadcasted_iota(jnp.int32, (tile, tile), 0)
    col = lax.broadcasted_iota(jnp.int32, (tile, tile), 1)
    eye = (row == col).astype(F32)
    dot = functools.partial(jnp.dot, precision=HIGHEST, preferred_element_type=F32)
    holds = where_ref[1] == 1
    places = range(0, n, tile)
    parts = [jnp.where(holds, block_ref[b : b + tile, b : b + tile], eye) for b in places]
    xs = [eye / jnp.sum(part * eye, axis=1, keepdims=True) for part in parts]
    size = 1
    while size < tile:
        pick = (row // (2 * size) == col // (2 * size)) & (row // size > col // size)
        inner = [dot(jnp.where(pick, part, 0.0), x) for part, x in zip(parts, xs)]
        xs = [x - dot(x, y) for x, y in zip(xs, inner)]
        size *= 2
    out_ref[...] = jnp.zeros_like(out_ref)
    for b, x in zip(places, xs):
        out_ref[b : b + tile, b : b + tile] = x
    size = tile
    while size < n:
        for b in range(0, n, 2 * size):
            mid, end = b + size, b + 2 * size
            inner = dot(block_ref[mid:end, b:mid], out_ref[b:mid, b:mid])
            out_ref[mid:end, b:mid] = -dot(out_ref[mid:end, mid:end], inner)
        size *= 2


def invert_block(where, metric):
    n = metric.shape[0]
    return pl.pallas_call(
        invert_kernel,
        grid_spec=pltpu.PrefetchScalarGridSpec(
            num_scalar_prefetch=1,
            grid=(1,),
            in_specs=[pl.BlockSpec((n, n), lambda i, s: (0, s[0]))],
            out_specs=pl.BlockSpec((n, n), lambda i, s: (0, 0)),
        ),
        out_shape=jax.ShapeDtypeStruct((n, n), F32),
        compiler_params=pltpu.CompilerParams(vmem_limit_bytes=16 << 20),
        cost_estimate=pl.CostEstimate(flops=4 << 30, transcendentals=0, bytes_accessed=1 << 22),
        name="invert_block",
    )(where, metric)


def weigh(hi_ref, lo_ref, halves):
    dims = (((1,), (1,)), ((), ()))
    total = None
    for half, x in halves:
        hi = x.astype(BF16)
        lo = (x - hi.astype(F32)).astype(BF16)
        n = x.shape[0]
        width = x.shape[1]
        columns = pl.ds(pl.multiple_of(half * width, width), width)
        both = lax.dot_general(
            jnp.concatenate([hi, lo]), hi_ref[:, columns], dims, preferred_element_type=F32
        )
        part = both[:n] + both[n:]
        if lo_ref is not None:
            part += lax.dot_general(hi, lo_ref[:, columns], dims, preferred_element_type=F32)
        total = part if total is None else total + part
    return total


def apply_kernel(where_ref, *refs):
    weights, (xa_ref, xb_ref, out_ref) = refs[:-3], refs[-3:]
    core = where_ref[0]
    hi_ref, lo_ref = weights if len(weights) == 2 else (weights[0], None)
    points = out_ref.shape[1]
    halves = [(core, xa_ref[:, :points]), (1 - core, xb_ref[:, :points])]
    out_ref[...] = weigh(hi_ref, lo_ref, halves)


def apply_weights(where, weights, xa, xb):
    return pl.pallas_call(
        apply_kernel,
        in_specs=[pl.BlockSpec(memory_space=pltpu.SMEM)]
        + [pl.BlockSpec(memory_space=pltpu.VMEM)] * (len(weights) + 2),
        out_specs=pl.BlockSpec(memory_space=pltpu.VMEM),
        out_shape=jax.ShapeDtypeStruct((xa.shape[0], weights[0].shape[0]), F32),
        compiler_params=pltpu.CompilerParams(vmem_limit_bytes=12 << 20),
        cost_estimate=pl.CostEstimate(flops=1 << 30, transcendentals=0, bytes_accessed=1 << 21),
        name="apply_weights",
    )(where, *weights, xa, xb)


def turn_kernel(count, where_ref, *refs):
    weights, refs = refs[: 2 * count + 2], refs[2 * count + 2 :]
    xa, xb, own_rest, sib_rest, out_ref, buffer, sems = refs
    core = where_ref[0]
    copies = [
        pltpu.make_async_copy(ref, buffer.at[i], sems.at[i]) for i, ref in enumerate(weights)
    ]
    for copy in copies:
        copy.start()
    points = xa.shape[1]
    n = own_rest.shape[0]
    own, sib = own_rest[:, :points], sib_rest[:, :points]
    for i in range(count):
        halves = [(core, xa[i * n : (i + 1) * n]), (1 - core, xb[i * n : (i + 1) * n])]
        copies[2 * i].wait()
        own -= weigh(buffer.at[2 * i], None, halves)
        copies[2 * i + 1].wait()
        sib -= weigh(buffer.at[2 * i + 1], None, halves)
    copies[-2].wait()
    copies[-1].wait()
    solved = weigh(
        buffer.at[2 * count], buffer.at[2 * count + 1], [(core, own), (1 - core, sib)]
    )
    if out_ref.shape[0] > n:
        out_ref[: count * n] = xa[...]
    out_ref[out_ref.shape[0] - n :] = solved


def turn(where, lefts, inverse, xa, xb, own_rest, sib_rest, keep):
    vmem = pl.BlockSpec(memory_space=pltpu.VMEM)
    weights = [*lefts, *inverse]
    n, points = own_rest.shape[0], xa.shape[1]
    count = len(lefts) // 2
    return pl.pallas_call(
        functools.partial(turn_kernel, count),
        in_specs=[pl.BlockSpec(memory_space=pltpu.SMEM)]
        + [pl.BlockSpec(memory_space=pl.ANY)] * len(weights)
        + [vmem] * 4,
        out_specs=vmem,
        out_shape=jax.ShapeDtypeStruct(((count + 1) * n if keep else n, points), F32),
        scratch_shapes=[
            pltpu.VMEM((len(weights),) + weights[0].shape, BF16),
            pltpu.SemaphoreType.DMA((len(weights),)),
        ],
        compiler_params=pltpu.CompilerParams(vmem_limit_bytes=32 << 20),
        cost_estimate=pl.CostEstimate(flops=1 << 20, transcendentals=0, bytes_accessed=1 << 16),
        name="turn",
    )(where, *weights, xa, xb, own_rest, sib_rest)


def combine_kernel(count, turn_ref, inverse_ref, *refs):
    x_refs, out_refs = refs[:count], refs[count:]
    x = jnp.zeros(x_refs[0].shape, F32)
    for t, ref in enumerate(x_refs):
        x = jnp.where(turn_ref[0] == t, ref[ref.shape[0] - x.shape[0] :], x)
    rows = out_refs[0].shape[0]
    for k, ref in enumerate(out_refs):
        inverse = inverse_ref[pl.ds(turn_ref[1 + k] * rows, rows), :]
        total = inverse[:, :1] * x[:1]
        for i in range(1, x.shape[0]):
            total += inverse[:, i : i + 1] * x[i : i + 1]
        ref[...] = total


def combine(which, inverse, turns, rows):
    count = len(turns)
    share = jax.ShapeDtypeStruct((rows, turns[0].shape[1]), F32)
    return pl.pallas_call(
        functools.partial(combine_kernel, count),
        in_specs=[pl.BlockSpec(memory_space=pltpu.SMEM)]
        + [pl.BlockSpec(memory_space=pltpu.VMEM)] * (count + 1),
        out_shape=[share] * count,
        name="combine",
    )(which, inverse, *turns)


def on_device(raw_columns, pivot_pairs, collocation, metric_factor):
    vec_total, orb_block, pair_block = raw_columns.shape
    gen_count = lax.axis_size("gen")
    gen_index = lax.axis_index("gen")
    fit_index = lax.axis_index("fit")
    chip = fit_index // 2
    core = fit_index % 2
    points = metric_factor.shape[0]
    vec_dev = vec_total // gen_count
    move = mover(gen_count)
    others = range(1, gen_count)
    diagonal = gen_index == chip
    swap = lambda g, j, c: (g, j, 1 - c)

    part = points // gen_count
    across = lambda k: lambda g, j, c: (g, j ^ k, c)
    halves = collocation.reshape(2, orb_block // 2, points)
    spread = []
    for k in range(gen_count):
        piece = lax.dynamic_slice_in_dim(halves, (gen_index ^ k) * part, part, 2)
        spread.append(move(piece, lambda g, j, c, k=k: (g ^ k, j, c)) if k else piece)
    spread = jnp.stack(spread)
    early, half = 2, points // 2
    sibling = move(raw_columns, swap)
    early_parts = [move(collocation[:, :half], across(early))]
    second_half = collocation[:, half:]
    spread, sibling, early_parts, second_half, metric_late = lax.optimization_barrier(
        (spread, sibling, early_parts, second_half, metric_factor)
    )
    early_parts.append(move(second_half, across(early)))
    own_rows = metric_late.astype(BF16)
    left_own = move(own_rows, lambda g, j, c: (g + 1, j, c) if j == g + 1 else None)
    own_parts = []
    for k in range(gen_count):
        piece = lax.dynamic_index_in_dim(spread, gen_index ^ chip ^ k, 0, keepdims=False)
        own_parts.append(move(piece, across(k)) if k else piece)
    own_raw = raw_columns.transpose(1, 0, 2)
    sib_raw = sibling.transpose(1, 0, 2)
    pivot_rows = pivot_pairs // NORB - gen_index * orb_block
    own_cols = pivot_pairs % NORB - fit_index * pair_block
    sib_cols = pivot_pairs % NORB - (fit_index ^ 1) * pair_block
    entries = pivot_entries(own_raw, sib_raw, pivot_rows, own_cols, sib_cols)

    own_inverse = invert_block(jnp.stack([core, diagonal.astype(jnp.int32)]), metric_late)
    own_parts, first, early_parts, left_own, own_inverse, entries = lax.optimization_barrier(
        (own_parts, collocation, early_parts, left_own, own_inverse, entries)
    )
    upper = move(own_inverse, swap)
    first_side = {0: [collocation], early: early_parts}
    for k in others:
        if k != early:
            first_side[k] = [move(first, across(k))]
    all_parts = [jnp.stack(own_parts)]
    for k in others:
        all_parts.append(move(all_parts[0], lambda g, j, c, k=k: (g ^ k, j, c)))

    def second_side(k):
        if part % 128 == 0:
            return all_parts
        whole = jnp.zeros(halves.shape, BF16)
        for n, x in enumerate(all_parts):
            whole = lax.dynamic_update_slice_in_dim(whole, x[k], (gen_index ^ n) * part, 2)
        return [whole[None]]

    corner = jnp.dot(metric_factor[:, :points], upper, precision=HIGHEST)
    corner = -jnp.dot(own_inverse, corner, precision=HIGHEST)
    inverse_rows = split_hi_lo(
        jnp.concatenate(
            [
                jnp.where(core == 0, own_inverse, corner),
                jnp.where(core == 0, jnp.zeros_like(own_inverse), own_inverse),
            ],
            axis=1,
        )
    )

    all_parts, first_side, entries, inverse_rows, left_rows = lax.optimization_barrier(
        (all_parts, first_side, entries, inverse_rows, own_rows)
    )
    left_own, left_sib = {1: left_own}, {1: move(left_own, swap)}
    for d in range(2, gen_count - 1):
        left_own[d] = move(left_rows, lambda g, j, c: (j, j, c) if g >= 1 and j == g + d else None)

    own_raw = own_raw.reshape(orb_block * vec_total, pair_block)
    sib_raw = sib_raw.reshape(orb_block * vec_total, pair_block)
    where = jnp.stack([core] + [gen_index ^ k for k in range(gen_count)])
    total = None
    for group in [list(range(i, min(i + 4, gen_count))) for i in range(0, gen_count, 4)]:
        shares = project(
            where,
            own_raw,
            sib_raw,
            entries,
            [first_side[k] for k in group],
            [second_side(k) for k in group],
            [k if part % 128 == 0 else 0 for k in group],
        )
        if group[0] == 0:
            shares, left_sib[1] = lax.optimization_barrier((shares, left_sib[1]))
        for k, share in zip(group, shares):
            if k:
                share = move(share, across(k))
            total = share if total is None else total + share
    total = sum([move(total, lambda g, j, c, k=k: (g ^ k, j, c)) for k in others], total)

    at_core = core[None]
    inverse_factor = factor_inverse(total)
    rest, sib_rest = total, move(total, swap)
    solved = apply_weights(at_core, inverse_rows, rest, sib_rest)
    turns = [solved]
    for t in range(1, gen_count):
        near = move(solved, lambda g, j, c: (t, t, c) if g == j == t - 1 else None)
        near_sib = move(solved, lambda g, j, c: (t, t, 1 - c) if g == j == t - 1 else None)
        if t == 1 and gen_count > 2:
            far = [
                move(solved, lambda g, j, c: (0, z, c) if g == j == 0 else None)
                for z in range(2, gen_count)
            ]
            near, near_sib, far = lax.optimization_barrier((near, near_sib, far))
        if t == 2:
            far = sum(far[1:], far[0])
            acted = apply_weights(at_core, [own_rows], far, move(far, swap))
            brought = {
                z: move(acted, lambda g, j, c: (j, j, c) if g == 0 and j == z else None)
                for z in range(2, gen_count)
            }
        if t >= 2:
            if t == 2:
                near, near_sib, brought[t] = lax.optimization_barrier((near, near_sib, brought[t]))
            else:
                brought[t], _ = lax.optimization_barrier((brought[t], solved))
            rest = rest[:, :points] - brought[t]
            sib_rest = move(rest, swap)
        if t == gen_count - 1:
            near, inverse_factor = lax.optimization_barrier((near, inverse_factor))
        lefts = []
        for g in range(min(1, t - 1), t):
            lefts += [left_own[t - g], left_sib[t - g]]
        solved = turn(at_core, lefts, inverse_rows, near, near_sib, rest, sib_rest, t > 1)
        turns.append(solved)
        if t == 1:
            for d in range(2, gen_count - 1):
                _, left_own[d] = lax.optimization_barrier((solved, left_own[d]))
                left_sib[d] = move(left_own[d], swap)

    which = jnp.stack([jnp.where(diagonal, gen_index, -1)] + [gen_index ^ k for k in range(gen_count)])
    shares = combine(which, inverse_factor, turns, vec_dev)
    result = shares[0]
    for k in others:
        result += move(shares[k], lambda g, j, c, k=k: (g ^ k, j, c) if g == j else None)
    return result


def solution(mesh):
    in_specs = (P(None, "gen", "fit"), P(), P("gen", "fit"), P("fit", "gen"))
    out_specs = P("gen", "fit")
    return jax.shard_map(
        on_device, mesh=mesh, in_specs=in_specs, out_specs=out_specs, check_vma=False
    )
```

```python
import functools

import jax
import jax.numpy as jnp
from jax import lax
from jax.experimental import pallas as pl
from jax.experimental.pallas import tpu as pltpu
from jax.sharding import PartitionSpec as P

NORB = 2000
F32 = jnp.float32
BF16 = jnp.bfloat16
BOTH = ("gen", "fit")
HIGHEST = lax.Precision.HIGHEST


def mover(gen_count):
    fit_count = 2 * gen_count

    def move(value, target):
        pairs = []
        for g in range(gen_count):
            for j in range(gen_count):
                for c in range(2):
                    to = target(g, j, c)
                    if to is not None:
                        pairs.append(
                            (g * fit_count + 2 * j + c, to[0] * fit_count + 2 * to[1] + to[2])
                        )
        return lax.ppermute(value, BOTH, pairs)

    return move


def split_hi_lo(x):
    hi = lax.reduce_precision(x, 8, 7)
    return hi.astype(BF16), (x - hi).astype(BF16)


def pivot_kernel(row_ref, own_ref, sib_ref, own_col_ref, sib_col_ref, out_ref, buffer, sems):
    count, orb = out_ref.shape[1], own_ref.shape[0]
    copies = []
    for i in range(count):
        row = jnp.clip(row_ref[i], 0, orb - 1)
        for n, ref in enumerate((own_ref, sib_ref)):
            copies.append(
                pltpu.make_async_copy(ref.at[row], buffer.at[2 * i + n], sems.at[2 * i + n])
            )
            copies[-1].start()
    lane = lax.broadcasted_iota(jnp.int32, buffer.shape[1:], 1)
    for i in range(count):
        copies[2 * i].wait()
        copies[2 * i + 1].wait()
        local = jnp.logical_and(row_ref[i] >= 0, row_ref[i] < orb)
        kept = jnp.where(lane == own_col_ref[i], buffer[2 * i].astype(F32), 0.0)
        kept += jnp.where(lane == sib_col_ref[i], buffer[2 * i + 1].astype(F32), 0.0)
        kept = jnp.where(local, kept, 0.0)
        out_ref[:, i : i + 1] = jnp.sum(kept, axis=1, keepdims=True)


def pivot_entries(own, sib, rows, own_cols, sib_cols):
    vec_total, pair = own.shape[1:]
    return pl.pallas_call(
        pivot_kernel,
        in_specs=[
            pl.BlockSpec(memory_space=pltpu.SMEM),
            pl.BlockSpec(memory_space=pltpu.HBM),
            pl.BlockSpec(memory_space=pltpu.HBM),
            pl.BlockSpec(memory_space=pltpu.SMEM),
            pl.BlockSpec(memory_space=pltpu.SMEM),
        ],
        out_specs=pl.BlockSpec(memory_space=pltpu.VMEM),
        out_shape=jax.ShapeDtypeStruct((vec_total, vec_total), F32),
        scratch_shapes=[
            pltpu.VMEM((2 * vec_total, vec_total, pair), BF16),
            pltpu.SemaphoreType.DMA((2 * vec_total,)),
        ],
        name="pivot_entries",
    )(rows, own, sib, own_cols, sib_cols)


def factor_inverse_kernel(block_ref, out_ref):
    n = block_ref.shape[0]
    a = block_ref[:, block_ref.shape[1] - 128 :][:, :n]
    row = lax.broadcasted_iota(jnp.int32, (n, n), 0)
    col = lax.broadcasted_iota(jnp.int32, (n, n), 1)
    w = (row == col).astype(F32)
    for i in range(n):
        pivot = a[i : i + 1, i : i + 1]
        scale = jnp.where(row[:, :1] > i, a[:, i : i + 1] / pivot, 0.0)
        w = w - scale * w[i : i + 1, :]
        a = a - scale * a[i : i + 1, :]
    diag = jnp.sum(jnp.where(row == col, a, 0.0), axis=1, keepdims=True)
    out_ref[...] = w / jnp.sqrt(diag)


def factor_inverse(block):
    return pl.pallas_call(
        factor_inverse_kernel,
        out_shape=jax.ShapeDtypeStruct((block.shape[0], block.shape[0]), F32),
        name="factor_inverse",
    )(block)


def project_kernel(vec_total, chunk, cp_counts, cq_count, where_ref, own_ref, sib_ref, entries_ref, *rest):
    blocks = len(cp_counts)
    cp_refs, rest = rest[: sum(cp_counts)], rest[sum(cp_counts) :]
    cq_refs, rest = rest[: blocks * cq_count], rest[blocks * cq_count :]
    out_refs, (cq, cp, acc) = rest[:blocks], rest[blocks:]
    points = cp.shape[2]
    step = pl.program_id(0)
    core = where_ref[0]

    @pl.when(step == 0)
    def _():
        for b in range(blocks):
            for n in range(cq_count):
                ref = cq_refs[b * cq_count + n]
                part = ref.shape[-1]
                start = 0
                if cq_count > 1:
                    start = pl.multiple_of(where_ref[1 + n] * part, part)
                cq[b, :, :, pl.ds(start, part)] = ref[0]
            start = 0
            for ref in cp_refs[sum(cp_counts[:b]) : sum(cp_counts[: b + 1])]:
                cp[b, :, start : start + ref.shape[1]] = ref[...].astype(F32)
                start += ref.shape[1]
            out_ref = out_refs[b]
            out_ref[:, points:] = jnp.zeros((vec_total, out_ref.shape[1] - points), F32)
            out_ref[:, points : points + vec_total] = entries_ref[...]
        acc[...] = jnp.zeros_like(acc)

    for b in range(blocks):
        mixed = jnp.dot(own_ref[...], cq[b, core], preferred_element_type=F32)
        mixed += jnp.dot(sib_ref[...], cq[b, 1 - core], preferred_element_type=F32)
        total = acc[b]
        for p in range(chunk):
            row = cp[b, pl.ds(step * chunk + p, 1), :]
            total += mixed[p * vec_total : (p + 1) * vec_total] * row
        acc[b] = total

    @pl.when(step == pl.num_programs(0) - 1)
    def _():
        for b in range(blocks):
            out_refs[b][:, :points] = acc[b]


def project(where, own, sib, entries, first, second, slots):
    orb = first[0][0].shape[0]
    points = sum(x.shape[1] for x in first[0])
    pair = own.shape[1]
    vec_total = own.shape[0] // orb
    chunk = 125
    blocks = len(first)
    whole = lambda i, s: (0, 0)
    specs, arrays = [], []
    for parts in first:
        for x in parts:
            specs.append(pl.BlockSpec(x.shape, whole))
            arrays.append(x)
    for parts, slot in zip(second, slots):
        for x in parts:
            specs.append(
                pl.BlockSpec((1,) + x.shape[1:], lambda i, s, slot=slot: (slot, 0, 0, 0))
            )
            arrays.append(x)
    kernel = functools.partial(
        project_kernel, vec_total, chunk, tuple(len(x) for x in first), len(second[0])
    )
    return pl.pallas_call(
        kernel,
        grid_spec=pltpu.PrefetchScalarGridSpec(
            num_scalar_prefetch=1,
            grid=(orb // chunk,),
            in_specs=[
                pl.BlockSpec((chunk * vec_total, pair), lambda i, s: (i, 0)),
                pl.BlockSpec((chunk * vec_total, pair), lambda i, s: (i, 0)),
                pl.BlockSpec((vec_total, vec_total), whole),
            ]
            + specs,
            out_specs=[pl.BlockSpec((vec_total, points + 128), whole)] * blocks,
            scratch_shapes=[
                pltpu.VMEM((blocks, 2, pair, points), BF16),
                pltpu.VMEM((blocks, orb, points), F32),
                pltpu.VMEM((blocks, vec_total, points), F32),
            ],
        ),
        out_shape=[jax.ShapeDtypeStruct((vec_total, points + 128), F32)] * blocks,
        compiler_params=pltpu.CompilerParams(vmem_limit_bytes=32 << 20),
        cost_estimate=pl.CostEstimate(
            flops=4 * orb * vec_total * pair * points * blocks,
            transcendentals=0,
            bytes_accessed=1 << 20,
        ),
        name="project",
    )(where, own, sib, entries, *arrays)


def invert_kernel(where_ref, block_ref, out_ref):
    n = block_ref.shape[0]
    tile = 128
    row = lax.broadcasted_iota(jnp.int32, (tile, tile), 0)
    col = lax.broadcasted_iota(jnp.int32, (tile, tile), 1)
    eye = (row == col).astype(F32)
    dot = functools.partial(jnp.dot, precision=HIGHEST, preferred_element_type=F32)
    holds = where_ref[1] == 1
    places = range(0, n, tile)
    parts = [jnp.where(holds, block_ref[b : b + tile, b : b + tile], eye) for b in places]
    xs = [eye / jnp.sum(part * eye, axis=1, keepdims=True) for part in parts]
    size = 1
    while size < tile:
        pick = (row // (2 * size) == col // (2 * size)) & (row // size > col // size)
        inner = [dot(jnp.where(pick, part, 0.0), x) for part, x in zip(parts, xs)]
        xs = [x - dot(x, y) for x, y in zip(xs, inner)]
        size *= 2
    out_ref[...] = jnp.zeros_like(out_ref)
    for b, x in zip(places, xs):
        out_ref[b : b + tile, b : b + tile] = x
    size = tile
    while size < n:
        for b in range(0, n, 2 * size):
            mid, end = b + size, b + 2 * size
            inner = dot(block_ref[mid:end, b:mid], out_ref[b:mid, b:mid])
            out_ref[mid:end, b:mid] = -dot(out_ref[mid:end, mid:end], inner)
        size *= 2


def invert_block(where, metric):
    n = metric.shape[0]
    return pl.pallas_call(
        invert_kernel,
        grid_spec=pltpu.PrefetchScalarGridSpec(
            num_scalar_prefetch=1,
            grid=(1,),
            in_specs=[pl.BlockSpec((n, n), lambda i, s: (0, s[0]))],
            out_specs=pl.BlockSpec((n, n), lambda i, s: (0, 0)),
        ),
        out_shape=jax.ShapeDtypeStruct((n, n), F32),
        compiler_params=pltpu.CompilerParams(vmem_limit_bytes=16 << 20),
        cost_estimate=pl.CostEstimate(flops=4 << 30, transcendentals=0, bytes_accessed=1 << 22),
        name="invert_block",
    )(where, metric)


def weigh(hi_ref, lo_ref, halves):
    dims = (((1,), (1,)), ((), ()))
    total = None
    for half, x in halves:
        hi = x.astype(BF16)
        lo = (x - hi.astype(F32)).astype(BF16)
        n = x.shape[0]
        width = x.shape[1]
        columns = pl.ds(pl.multiple_of(half * width, width), width)
        both = lax.dot_general(
            jnp.concatenate([hi, lo]), hi_ref[:, columns], dims, preferred_element_type=F32
        )
        part = both[:n] + both[n:]
        if lo_ref is not None:
            part += lax.dot_general(hi, lo_ref[:, columns], dims, preferred_element_type=F32)
        total = part if total is None else total + part
    return total


def apply_kernel(where_ref, *refs):
    weights, (xa_ref, xb_ref, out_ref) = refs[:-3], refs[-3:]
    core = where_ref[0]
    hi_ref, lo_ref = weights if len(weights) == 2 else (weights[0], None)
    points = out_ref.shape[1]
    halves = [(core, xa_ref[:, :points]), (1 - core, xb_ref[:, :points])]
    out_ref[...] = weigh(hi_ref, lo_ref, halves)


def apply_weights(where, weights, xa, xb):
    return pl.pallas_call(
        apply_kernel,
        in_specs=[pl.BlockSpec(memory_space=pltpu.SMEM)]
        + [pl.BlockSpec(memory_space=pltpu.VMEM)] * (len(weights) + 2),
        out_specs=pl.BlockSpec(memory_space=pltpu.VMEM),
        out_shape=jax.ShapeDtypeStruct((xa.shape[0], weights[0].shape[0]), F32),
        compiler_params=pltpu.CompilerParams(vmem_limit_bytes=12 << 20),
        cost_estimate=pl.CostEstimate(flops=1 << 30, transcendentals=0, bytes_accessed=1 << 21),
        name="apply_weights",
    )(where, *weights, xa, xb)


def turn_kernel(count, where_ref, *refs):
    weights, refs = refs[: 2 * count + 2], refs[2 * count + 2 :]
    xa, xb, own_rest, sib_rest, out_ref, buffer, sems = refs
    core = where_ref[0]
    copies = [
        pltpu.make_async_copy(ref, buffer.at[i], sems.at[i]) for i, ref in enumerate(weights)
    ]
    for copy in copies:
        copy.start()
    points = xa.shape[1]
    n = own_rest.shape[0]
    own, sib = own_rest[:, :points], sib_rest[:, :points]
    for i in range(count):
        halves = [(core, xa[i * n : (i + 1) * n]), (1 - core, xb[i * n : (i + 1) * n])]
        copies[2 * i].wait()
        own -= weigh(buffer.at[2 * i], None, halves)
        copies[2 * i + 1].wait()
        sib -= weigh(buffer.at[2 * i + 1], None, halves)
    copies[-2].wait()
    copies[-1].wait()
    solved = weigh(
        buffer.at[2 * count], buffer.at[2 * count + 1], [(core, own), (1 - core, sib)]
    )
    if out_ref.shape[0] > n:
        out_ref[: count * n] = xa[...]
    out_ref[out_ref.shape[0] - n :] = solved


def turn(where, lefts, inverse, xa, xb, own_rest, sib_rest, keep):
    vmem = pl.BlockSpec(memory_space=pltpu.VMEM)
    weights = [*lefts, *inverse]
    n, points = own_rest.shape[0], xa.shape[1]
    count = len(lefts) // 2
    return pl.pallas_call(
        functools.partial(turn_kernel, count),
        in_specs=[pl.BlockSpec(memory_space=pltpu.SMEM)]
        + [pl.BlockSpec(memory_space=pl.ANY)] * len(weights)
        + [vmem] * 4,
        out_specs=vmem,
        out_shape=jax.ShapeDtypeStruct(((count + 1) * n if keep else n, points), F32),
        scratch_shapes=[
            pltpu.VMEM((len(weights),) + weights[0].shape, BF16),
            pltpu.SemaphoreType.DMA((len(weights),)),
        ],
        compiler_params=pltpu.CompilerParams(vmem_limit_bytes=32 << 20),
        cost_estimate=pl.CostEstimate(flops=1 << 20, transcendentals=0, bytes_accessed=1 << 16),
        name="turn",
    )(where, *weights, xa, xb, own_rest, sib_rest)


def combine_kernel(count, turn_ref, inverse_ref, *refs):
    x_refs, out_refs = refs[:count], refs[count:]
    x = jnp.zeros(x_refs[0].shape, F32)
    for t, ref in enumerate(x_refs):
        x = jnp.where(turn_ref[0] == t, ref[ref.shape[0] - x.shape[0] :], x)
    rows = out_refs[0].shape[0]
    for k, ref in enumerate(out_refs):
        inverse = inverse_ref[pl.ds(turn_ref[1 + k] * rows, rows), :]
        total = inverse[:, :1] * x[:1]
        for i in range(1, x.shape[0]):
            total += inverse[:, i : i + 1] * x[i : i + 1]
        ref[...] = total


def combine(which, inverse, turns, rows):
    count = len(turns)
    share = jax.ShapeDtypeStruct((rows, turns[0].shape[1]), F32)
    return pl.pallas_call(
        functools.partial(combine_kernel, count),
        in_specs=[pl.BlockSpec(memory_space=pltpu.SMEM)]
        + [pl.BlockSpec(memory_space=pltpu.VMEM)] * (count + 1),
        out_shape=[share] * count,
        name="combine",
    )(which, inverse, *turns)


def on_device(raw_columns, pivot_pairs, collocation, metric_factor):
    vec_total, orb_block, pair_block = raw_columns.shape
    gen_count = lax.axis_size("gen")
    gen_index = lax.axis_index("gen")
    fit_index = lax.axis_index("fit")
    chip = fit_index // 2
    core = fit_index % 2
    points = metric_factor.shape[0]
    vec_dev = vec_total // gen_count
    move = mover(gen_count)
    others = range(1, gen_count)
    diagonal = gen_index == chip
    swap = lambda g, j, c: (g, j, 1 - c)

    part = points // gen_count
    across = lambda k: lambda g, j, c: (g, j ^ k, c)
    halves = collocation.reshape(2, orb_block // 2, points)
    spread = []
    for k in range(gen_count):
        piece = lax.dynamic_slice_in_dim(halves, (gen_index ^ k) * part, part, 2)
        spread.append(move(piece, lambda g, j, c, k=k: (g ^ k, j, c)) if k else piece)
    spread = jnp.stack(spread)
    early, half = 2, points // 2
    sibling = move(raw_columns, swap)
    early_parts = [move(collocation[:, :half], across(early))]
    spread, sibling, early_parts, own_rows, first, metric_late = lax.optimization_barrier(
        (spread, sibling, early_parts, metric_factor.astype(BF16), collocation, metric_factor)
    )
    early_parts.append(move(first[:, half:], across(early)))
    left_own = move(own_rows, lambda g, j, c: (g + 1, j, c) if j == g + 1 else None)
    own_parts = []
    for k in range(gen_count):
        piece = lax.dynamic_index_in_dim(spread, gen_index ^ chip ^ k, 0, keepdims=False)
        own_parts.append(move(piece, across(k)) if k else piece)
    own_raw = raw_columns.transpose(1, 0, 2)
    sib_raw = sibling.transpose(1, 0, 2)
    pivot_rows = pivot_pairs // NORB - gen_index * orb_block
    own_cols = pivot_pairs % NORB - fit_index * pair_block
    sib_cols = pivot_pairs % NORB - (fit_index ^ 1) * pair_block
    entries = pivot_entries(own_raw, sib_raw, pivot_rows, own_cols, sib_cols)

    own_inverse = invert_block(jnp.stack([core, diagonal.astype(jnp.int32)]), metric_late)
    own_parts, first, early_parts, left_own, own_inverse, entries = lax.optimization_barrier(
        (own_parts, collocation, early_parts, left_own, own_inverse, entries)
    )
    upper = move(own_inverse, swap)
    first_side = {0: [collocation], early: early_parts}
    for k in others:
        if k != early:
            first_side[k] = [move(first, across(k))]
    all_parts = [jnp.stack(own_parts)]
    for k in others:
        all_parts.append(move(all_parts[0], lambda g, j, c, k=k: (g ^ k, j, c)))

    def second_side(k):
        if part % 128 == 0:
            return all_parts
        whole = jnp.zeros(halves.shape, BF16)
        for n, x in enumerate(all_parts):
            whole = lax.dynamic_update_slice_in_dim(whole, x[k], (gen_index ^ n) * part, 2)
        return [whole[None]]

    corner = jnp.dot(metric_factor[:, :points], upper, precision=HIGHEST)
    corner = -jnp.dot(own_inverse, corner, precision=HIGHEST)
    inverse_rows = split_hi_lo(
        jnp.concatenate(
            [
                jnp.where(core == 0, own_inverse, corner),
                jnp.where(core == 0, jnp.zeros_like(own_inverse), own_inverse),
            ],
            axis=1,
        )
    )

    all_parts, first_side, entries, inverse_rows, left_rows = lax.optimization_barrier(
        (all_parts, first_side, entries, inverse_rows, own_rows)
    )
    left_own, left_sib = {1: left_own}, {1: move(left_own, swap)}
    for d in range(2, gen_count - 1):
        left_own[d] = move(left_rows, lambda g, j, c: (j, j, c) if g >= 1 and j == g + d else None)

    own_raw = own_raw.reshape(orb_block * vec_total, pair_block)
    sib_raw = sib_raw.reshape(orb_block * vec_total, pair_block)
    where = jnp.stack([core] + [gen_index ^ k for k in range(gen_count)])
    total = None
    for group in [list(range(i, min(i + 4, gen_count))) for i in range(0, gen_count, 4)]:
        shares = project(
            where,
            own_raw,
            sib_raw,
            entries,
            [first_side[k] for k in group],
            [second_side(k) for k in group],
            [k if part % 128 == 0 else 0 for k in group],
        )
        if group[0] == 0:
            shares, left_sib[1] = lax.optimization_barrier((shares, left_sib[1]))
        for k, share in zip(group, shares):
            if k:
                share = move(share, across(k))
            total = share if total is None else total + share
    total = sum([move(total, lambda g, j, c, k=k: (g ^ k, j, c)) for k in others], total)

    at_core = core[None]
    inverse_factor = factor_inverse(total)
    rest, sib_rest = total, move(total, swap)
    solved = apply_weights(at_core, inverse_rows, rest, sib_rest)
    turns = [solved]
    for t in range(1, gen_count):
        near = move(solved, lambda g, j, c: (t, t, c) if g == j == t - 1 else None)
        near_sib = move(solved, lambda g, j, c: (t, t, 1 - c) if g == j == t - 1 else None)
        if t == 1 and gen_count > 2:
            far = [
                move(solved, lambda g, j, c: (0, z, c) if g == j == 0 else None)
                for z in range(2, gen_count)
            ]
            near, near_sib, far = lax.optimization_barrier((near, near_sib, far))
        if t == 2:
            far = sum(far[1:], far[0])
            acted = apply_weights(at_core, [own_rows], far, move(far, swap))
            brought = {
                z: move(acted, lambda g, j, c: (j, j, c) if g == 0 and j == z else None)
                for z in range(2, gen_count)
            }
        if t >= 2:
            if t == 2:
                near, near_sib, brought[t] = lax.optimization_barrier((near, near_sib, brought[t]))
            else:
                brought[t], _ = lax.optimization_barrier((brought[t], solved))
            rest = rest[:, :points] - brought[t]
            sib_rest = move(rest, swap)
        if t == gen_count - 1:
            near, inverse_factor = lax.optimization_barrier((near, inverse_factor))
        lefts = []
        for g in range(min(1, t - 1), t):
            lefts += [left_own[t - g], left_sib[t - g]]
        solved = turn(at_core, lefts, inverse_rows, near, near_sib, rest, sib_rest, t > 1)
        turns.append(solved)
        if t == 1:
            for d in range(2, gen_count - 1):
                _, left_own[d] = lax.optimization_barrier((solved, left_own[d]))
                left_sib[d] = move(left_own[d], swap)

    which = jnp.stack([jnp.where(diagonal, gen_index, -1)] + [gen_index ^ k for k in range(gen_count)])
    shares = combine(which, inverse_factor, turns, vec_dev)
    result = shares[0]
    for k in others:
        result += move(shares[k], lambda g, j, c, k=k: (g ^ k, j, c) if g == j else None)
    return result


def solution(mesh):
    in_specs = (P(None, "gen", "fit"), P(), P("gen", "fit"), P("fit", "gen"))
    out_specs = P("gen", "fit")
    return jax.shard_map(
        on_device, mesh=mesh, in_specs=in_specs, out_specs=out_specs, check_vma=False
    )
```

```python
import functools

import jax
import jax.numpy as jnp
from jax import lax
from jax.experimental import pallas as pl
from jax.experimental.pallas import tpu as pltpu
from jax.sharding import PartitionSpec as P

NORB = 2000
F32 = jnp.float32
BF16 = jnp.bfloat16
BOTH = ("gen", "fit")
HIGHEST = lax.Precision.HIGHEST


def mover(gen_count):
    fit_count = 2 * gen_count

    def move(value, target):
        pairs = []
        for g in range(gen_count):
            for j in range(gen_count):
                for c in range(2):
                    to = target(g, j, c)
                    if to is not None:
                        pairs.append(
                            (g * fit_count + 2 * j + c, to[0] * fit_count + 2 * to[1] + to[2])
                        )
        return lax.ppermute(value, BOTH, pairs)

    return move


def split_hi_lo(x):
    hi = lax.reduce_precision(x, 8, 7)
    return hi.astype(BF16), (x - hi).astype(BF16)


def pivot_kernel(row_ref, own_ref, sib_ref, own_col_ref, sib_col_ref, out_ref, buffer, sems):
    count, orb = out_ref.shape[1], own_ref.shape[0]
    copies = []
    for i in range(count):
        row = jnp.clip(row_ref[i], 0, orb - 1)
        for n, ref in enumerate((own_ref, sib_ref)):
            copies.append(
                pltpu.make_async_copy(ref.at[row], buffer.at[2 * i + n], sems.at[2 * i + n])
            )
            copies[-1].start()
    lane = lax.broadcasted_iota(jnp.int32, buffer.shape[1:], 1)
    for i in range(count):
        copies[2 * i].wait()
        copies[2 * i + 1].wait()
        local = jnp.logical_and(row_ref[i] >= 0, row_ref[i] < orb)
        kept = jnp.where(lane == own_col_ref[i], buffer[2 * i].astype(F32), 0.0)
        kept += jnp.where(lane == sib_col_ref[i], buffer[2 * i + 1].astype(F32), 0.0)
        kept = jnp.where(local, kept, 0.0)
        out_ref[:, i : i + 1] = jnp.sum(kept, axis=1, keepdims=True)


def pivot_entries(own, sib, rows, own_cols, sib_cols):
    vec_total, pair = own.shape[1:]
    return pl.pallas_call(
        pivot_kernel,
        in_specs=[
            pl.BlockSpec(memory_space=pltpu.SMEM),
            pl.BlockSpec(memory_space=pltpu.HBM),
            pl.BlockSpec(memory_space=pltpu.HBM),
            pl.BlockSpec(memory_space=pltpu.SMEM),
            pl.BlockSpec(memory_space=pltpu.SMEM),
        ],
        out_specs=pl.BlockSpec(memory_space=pltpu.VMEM),
        out_shape=jax.ShapeDtypeStruct((vec_total, vec_total), F32),
        scratch_shapes=[
            pltpu.VMEM((2 * vec_total, vec_total, pair), BF16),
            pltpu.SemaphoreType.DMA((2 * vec_total,)),
        ],
        name="pivot_entries",
    )(rows, own, sib, own_cols, sib_cols)


def factor_inverse_kernel(block_ref, out_ref):
    n = block_ref.shape[0]
    a = block_ref[:, block_ref.shape[1] - 128 :][:, :n]
    row = lax.broadcasted_iota(jnp.int32, (n, n), 0)
    col = lax.broadcasted_iota(jnp.int32, (n, n), 1)
    w = (row == col).astype(F32)
    for i in range(n):
        pivot = a[i : i + 1, i : i + 1]
        scale = jnp.where(row[:, :1] > i, a[:, i : i + 1] / pivot, 0.0)
        w = w - scale * w[i : i + 1, :]
        a = a - scale * a[i : i + 1, :]
    diag = jnp.sum(jnp.where(row == col, a, 0.0), axis=1, keepdims=True)
    out_ref[...] = w / jnp.sqrt(diag)


def factor_inverse(block):
    return pl.pallas_call(
        factor_inverse_kernel,
        out_shape=jax.ShapeDtypeStruct((block.shape[0], block.shape[0]), F32),
        name="factor_inverse",
    )(block)


def project_kernel(vec_total, chunk, cp_counts, cq_count, where_ref, own_ref, sib_ref, entries_ref, *rest):
    blocks = len(cp_counts)
    cp_refs, rest = rest[: sum(cp_counts)], rest[sum(cp_counts) :]
    cq_refs, rest = rest[: blocks * cq_count], rest[blocks * cq_count :]
    out_refs, (cq, cp, acc) = rest[:blocks], rest[blocks:]
    points = cp.shape[2]
    step = pl.program_id(0)
    core = where_ref[0]

    @pl.when(step == 0)
    def _():
        for b in range(blocks):
            for n in range(cq_count):
                ref = cq_refs[b * cq_count + n]
                part = ref.shape[-1]
                start = 0
                if cq_count > 1:
                    start = pl.multiple_of(where_ref[1 + n] * part, part)
                cq[b, :, :, pl.ds(start, part)] = ref[0]
            start = 0
            for ref in cp_refs[sum(cp_counts[:b]) : sum(cp_counts[: b + 1])]:
                cp[b, :, start : start + ref.shape[1]] = ref[...].astype(F32)
                start += ref.shape[1]
            out_ref = out_refs[b]
            out_ref[:, points:] = jnp.zeros((vec_total, out_ref.shape[1] - points), F32)
            out_ref[:, points : points + vec_total] = entries_ref[...]
        acc[...] = jnp.zeros_like(acc)

    for b in range(blocks):
        mixed = jnp.dot(own_ref[...], cq[b, core], preferred_element_type=F32)
        mixed += jnp.dot(sib_ref[...], cq[b, 1 - core], preferred_element_type=F32)
        total = acc[b]
        for p in range(chunk):
            row = cp[b, pl.ds(step * chunk + p, 1), :]
            total += mixed[p * vec_total : (p + 1) * vec_total] * row
        acc[b] = total

    @pl.when(step == pl.num_programs(0) - 1)
    def _():
        for b in range(blocks):
            out_refs[b][:, :points] = acc[b]


def project(where, own, sib, entries, first, second, slots):
    orb = first[0][0].shape[0]
    points = sum(x.shape[1] for x in first[0])
    pair = own.shape[1]
    vec_total = own.shape[0] // orb
    chunk = 125
    blocks = len(first)
    whole = lambda i, s: (0, 0)
    specs, arrays = [], []
    for parts in first:
        for x in parts:
            specs.append(pl.BlockSpec(x.shape, whole))
            arrays.append(x)
    for parts, slot in zip(second, slots):
        for x in parts:
            specs.append(
                pl.BlockSpec((1,) + x.shape[1:], lambda i, s, slot=slot: (slot, 0, 0, 0))
            )
            arrays.append(x)
    kernel = functools.partial(
        project_kernel, vec_total, chunk, tuple(len(x) for x in first), len(second[0])
    )
    return pl.pallas_call(
        kernel,
        grid_spec=pltpu.PrefetchScalarGridSpec(
            num_scalar_prefetch=1,
            grid=(orb // chunk,),
            in_specs=[
                pl.BlockSpec((chunk * vec_total, pair), lambda i, s: (i, 0)),
                pl.BlockSpec((chunk * vec_total, pair), lambda i, s: (i, 0)),
                pl.BlockSpec((vec_total, vec_total), whole),
            ]
            + specs,
            out_specs=[pl.BlockSpec((vec_total, points + 128), whole)] * blocks,
            scratch_shapes=[
                pltpu.VMEM((blocks, 2, pair, points), BF16),
                pltpu.VMEM((blocks, orb, points), F32),
                pltpu.VMEM((blocks, vec_total, points), F32),
            ],
        ),
        out_shape=[jax.ShapeDtypeStruct((vec_total, points + 128), F32)] * blocks,
        compiler_params=pltpu.CompilerParams(vmem_limit_bytes=32 << 20),
        cost_estimate=pl.CostEstimate(
            flops=4 * orb * vec_total * pair * points * blocks,
            transcendentals=0,
            bytes_accessed=1 << 20,
        ),
        name="project",
    )(where, own, sib, entries, *arrays)


def invert_kernel(where_ref, block_ref, out_ref):
    n = block_ref.shape[0]
    tile = 128
    row = lax.broadcasted_iota(jnp.int32, (tile, tile), 0)
    col = lax.broadcasted_iota(jnp.int32, (tile, tile), 1)
    eye = (row == col).astype(F32)
    dot = functools.partial(jnp.dot, precision=HIGHEST, preferred_element_type=F32)
    holds = where_ref[1] == 1
    places = range(0, n, tile)
    parts = [jnp.where(holds, block_ref[b : b + tile, b : b + tile], eye) for b in places]
    xs = [eye / jnp.sum(part * eye, axis=1, keepdims=True) for part in parts]
    size = 1
    while size < tile:
        pick = (row // (2 * size) == col // (2 * size)) & (row // size > col // size)
        inner = [dot(jnp.where(pick, part, 0.0), x) for part, x in zip(parts, xs)]
        xs = [x - dot(x, y) for x, y in zip(xs, inner)]
        size *= 2
    out_ref[...] = jnp.zeros_like(out_ref)
    for b, x in zip(places, xs):
        out_ref[b : b + tile, b : b + tile] = x
    size = tile
    while size < n:
        for b in range(0, n, 2 * size):
            mid, end = b + size, b + 2 * size
            inner = dot(block_ref[mid:end, b:mid], out_ref[b:mid, b:mid])
            out_ref[mid:end, b:mid] = -dot(out_ref[mid:end, mid:end], inner)
        size *= 2


def invert_block(where, metric):
    n = metric.shape[0]
    return pl.pallas_call(
        invert_kernel,
        grid_spec=pltpu.PrefetchScalarGridSpec(
            num_scalar_prefetch=1,
            grid=(1,),
            in_specs=[pl.BlockSpec((n, n), lambda i, s: (0, s[0]))],
            out_specs=pl.BlockSpec((n, n), lambda i, s: (0, 0)),
        ),
        out_shape=jax.ShapeDtypeStruct((n, n), F32),
        compiler_params=pltpu.CompilerParams(vmem_limit_bytes=16 << 20),
        cost_estimate=pl.CostEstimate(flops=4 << 30, transcendentals=0, bytes_accessed=1 << 22),
        name="invert_block",
    )(where, metric)


def weigh(hi_ref, lo_ref, halves):
    dims = (((1,), (1,)), ((), ()))
    total = None
    for half, x in halves:
        hi = x.astype(BF16)
        lo = (x - hi.astype(F32)).astype(BF16)
        n = x.shape[0]
        width = x.shape[1]
        columns = pl.ds(pl.multiple_of(half * width, width), width)
        both = lax.dot_general(
            jnp.concatenate([hi, lo]), hi_ref[:, columns], dims, preferred_element_type=F32
        )
        part = both[:n] + both[n:]
        if lo_ref is not None:
            part += lax.dot_general(hi, lo_ref[:, columns], dims, preferred_element_type=F32)
        total = part if total is None else total + part
    return total


def apply_kernel(where_ref, *refs):
    weights, (xa_ref, xb_ref, out_ref) = refs[:-3], refs[-3:]
    core = where_ref[0]
    hi_ref, lo_ref = weights if len(weights) == 2 else (weights[0], None)
    points = out_ref.shape[1]
    halves = [(core, xa_ref[:, :points]), (1 - core, xb_ref[:, :points])]
    out_ref[...] = weigh(hi_ref, lo_ref, halves)


def apply_weights(where, weights, xa, xb):
    return pl.pallas_call(
        apply_kernel,
        in_specs=[pl.BlockSpec(memory_space=pltpu.SMEM)]
        + [pl.BlockSpec(memory_space=pltpu.VMEM)] * (len(weights) + 2),
        out_specs=pl.BlockSpec(memory_space=pltpu.VMEM),
        out_shape=jax.ShapeDtypeStruct((xa.shape[0], weights[0].shape[0]), F32),
        compiler_params=pltpu.CompilerParams(vmem_limit_bytes=12 << 20),
        cost_estimate=pl.CostEstimate(flops=1 << 30, transcendentals=0, bytes_accessed=1 << 21),
        name="apply_weights",
    )(where, *weights, xa, xb)


def turn_kernel(count, where_ref, *refs):
    weights, refs = refs[: 2 * count + 2], refs[2 * count + 2 :]
    xa, xb, own_rest, sib_rest, out_ref, buffer, sems = refs
    core = where_ref[0]
    copies = [
        pltpu.make_async_copy(ref, buffer.at[i], sems.at[i]) for i, ref in enumerate(weights)
    ]
    for copy in copies:
        copy.start()
    points = xa.shape[1]
    n = own_rest.shape[0]
    own, sib = own_rest[:, :points], sib_rest[:, :points]
    for i in range(count):
        halves = [(core, xa[i * n : (i + 1) * n]), (1 - core, xb[i * n : (i + 1) * n])]
        copies[2 * i].wait()
        own -= weigh(buffer.at[2 * i], None, halves)
        copies[2 * i + 1].wait()
        sib -= weigh(buffer.at[2 * i + 1], None, halves)
    copies[-2].wait()
    copies[-1].wait()
    solved = weigh(
        buffer.at[2 * count], buffer.at[2 * count + 1], [(core, own), (1 - core, sib)]
    )
    if out_ref.shape[0] > n:
        out_ref[: count * n] = xa[...]
    out_ref[out_ref.shape[0] - n :] = solved


def turn(where, lefts, inverse, xa, xb, own_rest, sib_rest, keep):
    vmem = pl.BlockSpec(memory_space=pltpu.VMEM)
    weights = [*lefts, *inverse]
    n, points = own_rest.shape[0], xa.shape[1]
    count = len(lefts) // 2
    return pl.pallas_call(
        functools.partial(turn_kernel, count),
        in_specs=[pl.BlockSpec(memory_space=pltpu.SMEM)]
        + [pl.BlockSpec(memory_space=pl.ANY)] * len(weights)
        + [vmem] * 4,
        out_specs=vmem,
        out_shape=jax.ShapeDtypeStruct(((count + 1) * n if keep else n, points), F32),
        scratch_shapes=[
            pltpu.VMEM((len(weights),) + weights[0].shape, BF16),
            pltpu.SemaphoreType.DMA((len(weights),)),
        ],
        compiler_params=pltpu.CompilerParams(vmem_limit_bytes=32 << 20),
        cost_estimate=pl.CostEstimate(flops=1 << 20, transcendentals=0, bytes_accessed=1 << 16),
        name="turn",
    )(where, *weights, xa, xb, own_rest, sib_rest)


def combine_kernel(count, turn_ref, inverse_ref, *refs):
    x_refs, out_refs = refs[:count], refs[count:]
    x = jnp.zeros(x_refs[0].shape, F32)
    for t, ref in enumerate(x_refs):
        x = jnp.where(turn_ref[0] == t, ref[ref.shape[0] - x.shape[0] :], x)
    rows = out_refs[0].shape[0]
    for k, ref in enumerate(out_refs):
        inverse = inverse_ref[pl.ds(turn_ref[1 + k] * rows, rows), :]
        total = inverse[:, :1] * x[:1]
        for i in range(1, x.shape[0]):
            total += inverse[:, i : i + 1] * x[i : i + 1]
        ref[...] = total


def combine(which, inverse, turns, rows):
    count = len(turns)
    share = jax.ShapeDtypeStruct((rows, turns[0].shape[1]), F32)
    return pl.pallas_call(
        functools.partial(combine_kernel, count),
        in_specs=[pl.BlockSpec(memory_space=pltpu.SMEM)]
        + [pl.BlockSpec(memory_space=pltpu.VMEM)] * (count + 1),
        out_shape=[share] * count,
        name="combine",
    )(which, inverse, *turns)


def on_device(raw_columns, pivot_pairs, collocation, metric_factor):
    vec_total, orb_block, pair_block = raw_columns.shape
    gen_count = lax.axis_size("gen")
    gen_index = lax.axis_index("gen")
    fit_index = lax.axis_index("fit")
    chip = fit_index // 2
    core = fit_index % 2
    points = metric_factor.shape[0]
    vec_dev = vec_total // gen_count
    move = mover(gen_count)
    others = range(1, gen_count)
    diagonal = gen_index == chip
    swap = lambda g, j, c: (g, j, 1 - c)

    part = points // gen_count
    across = lambda k: lambda g, j, c: (g, j ^ k, c)
    halves = collocation.reshape(2, orb_block // 2, points)
    spread = []
    for k in range(gen_count):
        piece = lax.dynamic_slice_in_dim(halves, (gen_index ^ k) * part, part, 2)
        spread.append(move(piece, lambda g, j, c, k=k: (g ^ k, j, c)) if k else piece)
    spread = jnp.stack(spread)
    early, half = 2, points // 2
    sibling = move(raw_columns, swap)
    early_parts = [move(collocation[:, :half], across(early))]
    spread, sibling, early_parts, own_rows, first, metric_late = lax.optimization_barrier(
        (spread, sibling, early_parts, metric_factor.astype(BF16), collocation, metric_factor)
    )
    early_parts.append(move(first[:, half:], across(early)))
    left_own = move(own_rows, lambda g, j, c: (g + 1, j, c) if j == g + 1 else None)
    own_parts = []
    for k in range(gen_count):
        piece = lax.dynamic_index_in_dim(spread, gen_index ^ chip ^ k, 0, keepdims=False)
        own_parts.append(move(piece, across(k)) if k else piece)
    own_raw = raw_columns.transpose(1, 0, 2)
    sib_raw = sibling.transpose(1, 0, 2)
    pivot_rows = pivot_pairs // NORB - gen_index * orb_block
    own_cols = pivot_pairs % NORB - fit_index * pair_block
    sib_cols = pivot_pairs % NORB - (fit_index ^ 1) * pair_block
    entries = pivot_entries(own_raw, sib_raw, pivot_rows, own_cols, sib_cols)

    own_inverse = invert_block(jnp.stack([core, diagonal.astype(jnp.int32)]), metric_late)
    own_parts, first, early_parts, left_own, own_inverse, entries = lax.optimization_barrier(
        (own_parts, collocation, early_parts, left_own, own_inverse, entries)
    )
    upper = move(own_inverse, swap)
    first_side = {0: [collocation], early: early_parts}
    for k in others:
        if k != early:
            first_side[k] = [move(first, across(k))]
    all_parts = [jnp.stack(own_parts)]
    for k in others:
        all_parts.append(move(all_parts[0], lambda g, j, c, k=k: (g ^ k, j, c)))

    def second_side(k):
        if part % 128 == 0:
            return all_parts
        whole = jnp.zeros(halves.shape, BF16)
        for n, x in enumerate(all_parts):
            whole = lax.dynamic_update_slice_in_dim(whole, x[k], (gen_index ^ n) * part, 2)
        return [whole[None]]

    corner = jnp.dot(metric_factor[:, :points], upper, precision=HIGHEST)
    corner = -jnp.dot(own_inverse, corner, precision=HIGHEST)
    inverse_rows = split_hi_lo(
        jnp.concatenate(
            [
                jnp.where(core == 0, own_inverse, corner),
                jnp.where(core == 0, jnp.zeros_like(own_inverse), own_inverse),
            ],
            axis=1,
        )
    )

    own_raw = own_raw.reshape(orb_block * vec_total, pair_block)
    sib_raw = sib_raw.reshape(orb_block * vec_total, pair_block)
    where = jnp.stack([core] + [gen_index ^ k for k in range(gen_count)])
    def shares_of(group):
        return project(
            where,
            own_raw,
            sib_raw,
            entries,
            [first_side[k] for k in group],
            [second_side(k) for k in group],
            [k if part % 128 == 0 else 0 for k in group],
        )

    all_parts, entries, inverse_rows = lax.optimization_barrier((all_parts, entries, inverse_rows))
    shares = []
    for i in range(0, gen_count - 1, 3):
        shares += shares_of(list(range(i, min(i + 3, gen_count - 1))))
    shares, first_side, left_own, left_rows = lax.optimization_barrier(
        (shares, first_side, left_own, own_rows)
    )
    left_own, left_sib = {1: left_own}, {1: move(left_own, swap)}
    for d in range(2, gen_count - 1):
        left_own[d] = move(left_rows, lambda g, j, c: (j, j, c) if g >= 1 and j == g + d else None)
    shares += shares_of([gen_count - 1])
    shares, left_sib[1] = lax.optimization_barrier((shares, left_sib[1]))
    total = shares[0]
    for k in others:
        total += move(shares[k], across(k))
    total = sum([move(total, lambda g, j, c, k=k: (g ^ k, j, c)) for k in others], total)

    at_core = core[None]
    inverse_factor = factor_inverse(total)
    rest, sib_rest = total, move(total, swap)
    solved = apply_weights(at_core, inverse_rows, rest, sib_rest)
    turns = [solved]
    for t in range(1, gen_count):
        near = move(solved, lambda g, j, c: (t, t, c) if g == j == t - 1 else None)
        near_sib = move(solved, lambda g, j, c: (t, t, 1 - c) if g == j == t - 1 else None)
        if t == 1 and gen_count > 2:
            far = [
                move(solved, lambda g, j, c: (0, z, c) if g == j == 0 else None)
                for z in range(2, gen_count)
            ]
            near, near_sib, far = lax.optimization_barrier((near, near_sib, far))
        if t == 2:
            far = sum(far[1:], far[0])
            acted = apply_weights(at_core, [own_rows], far, move(far, swap))
            brought = {
                z: move(acted, lambda g, j, c: (j, j, c) if g == 0 and j == z else None)
                for z in range(2, gen_count)
            }
        if t >= 2:
            if t == 2:
                near, near_sib, brought[t] = lax.optimization_barrier((near, near_sib, brought[t]))
            else:
                brought[t], _ = lax.optimization_barrier((brought[t], solved))
            rest = rest[:, :points] - brought[t]
            sib_rest = move(rest, swap)
        if t == gen_count - 1:
            near, inverse_factor = lax.optimization_barrier((near, inverse_factor))
        lefts = []
        for g in range(min(1, t - 1), t):
            lefts += [left_own[t - g], left_sib[t - g]]
        solved = turn(at_core, lefts, inverse_rows, near, near_sib, rest, sib_rest, t > 1)
        turns.append(solved)
        if t == 1:
            for d in range(2, gen_count - 1):
                _, left_own[d] = lax.optimization_barrier((solved, left_own[d]))
                left_sib[d] = move(left_own[d], swap)

    which = jnp.stack([jnp.where(diagonal, gen_index, -1)] + [gen_index ^ k for k in range(gen_count)])
    shares = combine(which, inverse_factor, turns, vec_dev)
    result = shares[0]
    for k in others:
        result += move(shares[k], lambda g, j, c, k=k: (g ^ k, j, c) if g == j else None)
    return result


def solution(mesh):
    in_specs = (P(None, "gen", "fit"), P(), P("gen", "fit"), P("fit", "gen"))
    out_specs = P("gen", "fit")
    return jax.shard_map(
        on_device, mesh=mesh, in_specs=in_specs, out_specs=out_specs, check_vma=False
    )
```
